32 devices in a mesh: groups: 2 (over y), img: 4 (over z), ref: 2 (over x), rep: 2 (over core).
Axes of the slice: x: 2, y: 2, z: 4, core: 2. Of those that a mesh axis runs over, the one named last changes fastest.
Arguments:
- images: float32 [768, 4096], P(('groups', 'img')), parts along dimension 0, may hold values from -24 to 24
- references: float32 [4096, 2048], P('img', ('groups', 'ref', 'rep')), parts along dimension 1, may hold values from -1.2 to 1.2
- rotations: int32 [2048], P(('groups', 'ref', 'rep')), parts along dimension 0, may hold values from 0 to 7
- image_group: int32 [768], P(('groups', 'img')), parts along dimension 0, may hold values from 0 to 15
- noise_var: float32 [16], replicated, may hold values from 0.5 to 2
Outputs:
- class_means: float32 [4096, 2048], P('img', ('groups', 'ref', 'rep')), parts along dimension 1
- class_weights: float32 [2048], P(('groups', 'ref', 'rep')), parts along dimension 0
- log_evidence: float32 [768], P(('groups', 'img')), parts along dimension 0
The draws below stay inside these ranges and needn't reach their ends.
There are 2 independent parts, one for each index of `groups`. The reference program is written for one: setup_inputs(seed, part) draws one part's arguments, and reference() takes and returns one part's arrays. A program takes and returns all parts, laid end to end along the dimension named above; an argument that names none is the same for every part. Nothing has to cross between parts.
All inputs are finite; a program needn't handle non-finite values.
Results may differ from the reference program's by a relative error of at most 0.0003.
Values sent between devices are 32-bit elements; how exact they have to be, the bound alone decides.
A program may use at most 64 MiB of HBM per device.

```python
import math
import jax
import jax.numpy as jnp
from jax import lax

IMAGE_SIDE = 64
PIXELS = 4096
CLASSES = 1024
IMAGES = 384
NOISE_GROUPS = 16


def shared_classes(key):
    values = jax.random.normal(jax.random.fold_in(key, 101), (PIXELS, CLASSES), jnp.float32)
    scales = jnp.full((CLASSES,), 0.05, jnp.float32)
    values = jnp.clip(values, -6.0, 6.0) * scales[None, :]
    turns = jax.random.randint(jax.random.fold_in(key, 103), (CLASSES,), 0, 8).astype(jnp.int32)
    return (values, turns)


def draw_references(key, part):
    return shared_classes(key)[0]


def draw_rotations(key, part):
    return shared_classes(key)[1]


def draw_images(key, part):
    base = jnp.clip(jax.random.normal(jax.random.fold_in(key, 301), (IMAGES, PIXELS), jnp.float32), -6.0, 6.0)
    return jnp.clip(base, -24.0, 24.0)


def touch_ends(values, own_key, low, top_value):
    index_at = [jax.random.randint(jax.random.fold_in(own_key, axis), (), 0, length) for axis, length in enumerate(values.shape)]
    widest = values.shape.index(max(values.shape))
    beside = index_at[:widest] + [(index_at[widest] + 1) % values.shape[widest]] + index_at[widest + 1:]
    return values.at[tuple(index_at)].set(low).at[tuple(beside)].set(top_value)


def setup_inputs(seed: int = 0, part: int = 0) -> dict:
    seeds = jax.random.split(jax.random.key(seed), 6)
    part_splits = jax.random.split(jax.random.fold_in(seeds[5], part), 6)
    return {
        "images": draw_images(jax.random.fold_in(jax.random.fold_in(seeds[5], part), 71), part),
        "references": draw_references(jax.random.fold_in(jax.random.fold_in(seeds[5], part), 71), part),
        "rotations": draw_rotations(jax.random.fold_in(jax.random.fold_in(seeds[5], part), 71), part),
        "image_group": touch_ends(jax.random.randint(part_splits[3], (IMAGES,), 0, NOISE_GROUPS), jax.random.fold_in(part_splits[3], 1), 0, NOISE_GROUPS - 1).astype(jnp.int32),
        "noise_var": jnp.clip(jnp.exp(jax.random.uniform(seeds[4], (NOISE_GROUPS,), jnp.float32, math.log(0.5), math.log(2.0))), 0.5, 2.0),
    }


def turn_forward(field, which):
    quarter = which % 4
    base = field if which < 4 else jnp.swapaxes(field, 0, 1)
    return jnp.rot90(base, quarter, axes=(0, 1))


def turn_inverse(field, which):
    quarter = which % 4
    base = jnp.rot90(field, -quarter, axes=(0, 1))
    return base if which < 4 else jnp.swapaxes(base, 0, 1)


def select_turn(field, rotations, turner):
    result = jnp.zeros_like(field)
    for which in range(8):
        result = jnp.where(rotations[None, None, :] == which, turner(field, which), result)
    return result


def reference(images, references, rotations, image_group, noise_var):
    rotated = select_turn(references.reshape(IMAGE_SIDE, IMAGE_SIDE, -1), rotations, turn_inverse).reshape(PIXELS, -1)
    norms = jnp.sum(references * references, axis=0)
    sigma = noise_var[image_group]
    scores = (jnp.dot(images, rotated, precision=lax.Precision.HIGHEST, preferred_element_type=jnp.float32) - 0.5 * norms[None, :]) / sigma[:, None]
    top = jnp.max(scores, axis=1)
    log_evidence = top + jnp.log(jnp.sum(jnp.exp(scores - top[:, None]), axis=1))
    posterior = jnp.exp(scores - log_evidence[:, None])
    weight_sum = jnp.sum(posterior, axis=0)
    numer_image = jnp.dot(images.T, posterior, precision=lax.Precision.HIGHEST, preferred_element_type=jnp.float32)
    numerator = select_turn(numer_image.reshape(IMAGE_SIDE, IMAGE_SIDE, -1), rotations, turn_forward).reshape(PIXELS, -1)
    class_means = numerator / (weight_sum + 1.0)[None, :]
    class_weights = weight_sum * (CLASSES / IMAGES)
    return class_means, class_weights, log_evidence
```

```python
import functools

import jax
import jax.numpy as jnp
from jax import lax
from jax.experimental import pallas as pl
from jax.experimental.pallas import tpu as pltpu
from jax.sharding import PartitionSpec as P

IMAGE_SIDE = 64
PIXELS = 4096
MESH = pl.DeviceIdType.MESH
F32 = jnp.float32
BF16 = jnp.bfloat16
LANES = 128
VMEM_BYTES = 62 * 1024 * 1024


def joined(part, axis, combine):
    gathered = jax.tree.map(lambda a: lax.all_gather(a, axis), part)

    def take(source):
        return jax.tree.map(lambda a: lax.dynamic_index_in_dim(a, source, 0, False), gathered)

    return lax.fori_loop(
        1, lax.axis_size(axis), lambda source, state: combine(state, take(source)), take(0)
    )


def turn_forward(field, which):
    quarter = which % 4
    base = field if which < 4 else jnp.swapaxes(field, 0, 1)
    return jnp.rot90(base, quarter, axes=(0, 1))


def turn_inverse(field, which):
    quarter = which % 4
    base = jnp.rot90(field, -quarter, axes=(0, 1))
    return base if which < 4 else jnp.swapaxes(base, 0, 1)


def select_turn(field, rotations, turner):
    result = jnp.zeros_like(field)
    for which in range(8):
        result = jnp.where(rotations[None, None, :] == which, turner(field, which), result)
    return result


def combine_stats(first, second):
    top = jnp.maximum(first[0], second[0])
    total = first[1] * jnp.exp(first[0] - top) + second[1] * jnp.exp(second[0] - top)
    return (top, total)


def body(images, references, rotations, image_group, noise_var):
    gathered = lax.all_gather(references, "img", axis=0, tiled=True)
    rotated = select_turn(
        gathered.reshape(IMAGE_SIDE, IMAGE_SIDE, -1), rotations, turn_inverse
    ).reshape(PIXELS, -1)
    norms = jnp.sum(gathered * gathered, axis=0)
    group_hot = image_group[:, None] == jnp.arange(noise_var.shape[0])[None, :]
    sigma = jnp.sum(jnp.where(group_hot, noise_var[None, :], 0.0), axis=1)
    scores = (
        jnp.dot(
            images, rotated, precision=lax.Precision.HIGHEST, preferred_element_type=jnp.float32
        )
        - 0.5 * norms[None, :]
    ) / sigma[:, None]
    local_top = jnp.max(scores, axis=1)
    local_total = jnp.sum(jnp.exp(scores - local_top[:, None]), axis=1)
    top, total = joined((local_top, local_total), ("ref", "rep"), combine_stats)
    log_evidence = top + jnp.log(total)
    posterior = jnp.exp(scores - log_evidence[:, None])
    weight_sum = lax.psum(jnp.sum(posterior, axis=0), "img")
    numer_image = lax.dot_general(
        images,
        posterior,
        (((0,), (0,)), ((), ())),
        precision=lax.Precision.HIGHEST,
        preferred_element_type=jnp.float32,
    )
    numerator = select_turn(
        numer_image.reshape(IMAGE_SIDE, IMAGE_SIDE, -1), rotations, turn_forward
    ).reshape(PIXELS, -1)
    owned = lax.psum_scatter(numerator, "img", scatter_dimension=0, tiled=True)
    class_means = owned / (weight_sum + 1.0)[None, :]
    class_total = weight_sum.shape[0] * lax.axis_size("ref") * lax.axis_size("rep")
    image_total = images.shape[0] * lax.axis_size("img")
    class_weights = weight_sum * (class_total / image_total)
    return (class_means, class_weights, log_evidence)


def halves(x):
    high = x.astype(BF16)
    return high, (x - high.astype(F32)).astype(BF16)


def reverse_rows(x):
    place = lax.broadcasted_iota(jnp.int32, (8, x.shape[1]), 0)
    odd = place % 2 == 1
    second = (place // 2) % 2 == 1
    pieces = []
    for g in reversed(range(x.shape[0] // 8)):
        p = x[8 * g : 8 * g + 8]
        p = jnp.where(odd, pltpu.roll(p, 1, 0), pltpu.roll(p, 7, 0))
        p = jnp.where(second, pltpu.roll(p, 2, 0), pltpu.roll(p, 6, 0))
        pieces.append(pltpu.roll(p, 4, 0))
    return jnp.concatenate(pieces, axis=0)


def kernel(
    zs, weight_scale,
    images_ref, source_ref, rot_ref, group_ref, noise_ref,
    means_ref, weights_ref, evidence_ref,
    raw, full, wide, scores, parts, stats, posts, num, refs_ref, factors, tall_high, tall_low, post_high, post_low,
    load_sem, refs_sem, z_recv, x_recv, cx_recv,
    in_send, out_send, far_send, x_send, cx_send,
    s_send, s_recv, t_send, t_recv, p_send, p_recv, f_send, f_recv,
):
    z = lax.axis_index("img")
    x = lax.axis_index("ref")
    c = lax.axis_index("rep")
    rows = images_ref.shape[0]
    classes = refs_ref.shape[1]
    quarter = rows // 4
    side = IMAGE_SIDE
    band = side // zs
    section = PIXELS // 4
    others = [{"ref": 1 - x}, {"rep": 1 - c}, {"ref": 1 - x, "rep": 1 - c}]
    upper = jnp.where(z >= 2, 1, 0)
    middle = jnp.where((z == 1) | (z == 2), 1, 0)
    inward = 1 - 2 * upper

    def quarter_at(xi, ci):
        return pl.ds(pl.multiple_of((ci * 2 + xi) * quarter, 8), quarter)

    load_quarters = []
    for q, (xi, ci) in enumerate([(x, c), (1 - x, c), (x, 1 - c), (1 - x, 1 - c)]):
        at = quarter_at(xi, ci)
        load_quarters.append((pltpu.make_async_copy(images_ref.at[at, :], raw.at[at, :], load_sem.at[q]), at))
    for load, _ in load_quarters:
        load.start()
    load_refs = pltpu.make_async_copy(source_ref, refs_ref, refs_sem)
    load_refs.start()
    barrier = pltpu.get_barrier_semaphore()
    for d in range(1, zs):
        pl.semaphore_signal(barrier, inc=1, device_id={"img": lax.rem(z + d, zs)}, device_id_type=MESH)
    for where in others:
        pl.semaphore_signal(barrier, inc=1, device_id=where, device_id_type=MESH)

    def repack(at):
        place = lax.broadcasted_iota(jnp.int32, (quarter, LANES), 1) // band
        low = place % 4
        for g in range(4):
            for v in range(4):
                first = raw[at, g * section + v * LANES : g * section + (v + 1) * LANES]
                start = g * section + section // 2 + v * LANES
                second = raw[at, start : start + LANES]
                first_a, first_b = pltpu.roll(first, band, 1), pltpu.roll(first, 5 * band, 1)
                second_a, second_b = pltpu.roll(second, 3 * band, 1), pltpu.roll(second, 7 * band, 1)
                outer = jnp.where(low < 2, jnp.where(low == 0, first_b, first_a), jnp.where(low == 2, second_b, second_a))
                inner = jnp.where(low < 2, second_b, first_a)
                which = 0 if g in (0, 3) else 2
                start = (section // 2 if g >= 2 else 0) + v * LANES
                full[z, which, at, start : start + LANES] = outer
                full[z, which + 1, at, start : start + LANES] = inner

    load_quarters[0][0].wait()
    repack(load_quarters[0][1])
    pl.semaphore_wait(barrier, zs + 2)

    def send(src, dst, ssem, rsem, where):
        return pltpu.make_async_remote_copy(
            src_ref=src, dst_ref=dst, send_sem=ssem, recv_sem=rsem,
            device_id=where, device_id_type=MESH,
        )

    def piece(src, sec):
        return full.at[src, sec, quarter_at(x, c), :]

    def go_in(src, sec):
        return send(piece(src, sec), piece(src, sec), in_send.at[src, sec], z_recv.at[src, sec], {"img": z + inward})

    def go_out(src, sec):
        return send(piece(src, sec), piece(src, sec), out_send.at[src, sec], z_recv.at[src, sec], {"img": z - inward})

    def go_far():
        target = jnp.where(upper == 1, 0, zs - 1)
        return send(piece(z, 0), piece(z, 0), far_send, z_recv.at[z, 0], {"img": target})

    def go_x(src, sec):
        return send(piece(src, sec), piece(src, sec), x_send.at[src, sec], x_recv.at[src, sec], {"ref": 1 - x})

    def go_cx(src, sec):
        pair = full.at[src, sec, pl.ds(pl.multiple_of(c * 2 * quarter, 8), 2 * quarter), :]
        return send(pair, pair, cx_send.at[src, sec], cx_recv.at[src, sec], {"rep": 1 - c})

    def partial(src):
        return send(scores.at[src], parts.at[z], s_send.at[src], s_recv.at[z], {"img": src})

    is_end = middle == 0
    is_middle = middle == 1

    @pl.when(is_end)
    def _():
        for sec in (1, 2, 3):
            go_in(z, sec).start()
        go_far().start()

    @pl.when(is_middle)
    def _():
        for sec_in, sec_out in ((1, 1), (2, 2), (3, 0)):
            go_in(z, sec_in).start()
            go_out(z, sec_out).start()
        go_far().start()

    rot = rot_ref[...]
    is_row = (rot == 0) | (rot == 7)
    is_row_up = (rot == 5) | (rot == 2)
    is_col = (rot == 4) | (rot == 3)
    is_col_up = (rot == 1) | (rot == 6)
    flipped = (rot == 7) | (rot == 2) | (rot == 3) | (rot == 6)

    def lane(h):
        return slice(h * LANES, (h + 1) * LANES)

    def line(i):
        return pl.ds(pl.multiple_of(i * side, side), side)

    def row_at(b, i, which):
        base = jnp.where(b >= 2, section // 2, 0) + side * lax.rem(i, 8)
        if which in (0, 3):
            place = base + section * middle + 2 * band * (i // 8) + (band if which == 0 else 0)
        else:
            place = base + section * (middle + 1) + 2 * band * (1 - i // 8) + (band if which == 2 else 0)
        return pl.ds(pl.multiple_of(place, band), band)

    def column_at(b, i, g, half):
        base = (0 if g in (0, 3) else 2 * section) + (section // 2 if g >= 2 else 0)
        swapped = half + middle * (1 - 2 * half)
        place = base + 2 * band * swapped + band * (1 - lax.rem(b, 2)) + i
        return pl.ds(place, 8, stride=side)

    def turned(i):
        field = refs_ref[line(i), :]
        return jnp.where(flipped, reverse_rows(field), field)

    def put_rows(i, norm):
        raw_field = refs_ref[line(i), :]
        field = turned(i)
        up = jnp.where(is_row, field, 0.0)
        down = jnp.where(is_row_up, field, 0.0)
        for h in range(classes // LANES):
            for which in range(4):
                part = slice(which * band, (which + 1) * band)
                wide[h, row_at(z, i, which), :] = up[part, lane(h)]
                wide[h, row_at(zs - 1 - z, band - 1 - i, which), :] = down[part, lane(h)]
        return norm + jnp.sum(raw_field * raw_field, axis=0, keepdims=True)

    def put_columns(i, _):
        field = turned(i)
        across = jnp.where(is_col, field, 0.0)
        back = jnp.where(is_col_up, field, 0.0)

        def put(added):
            for h in range(classes // LANES):
                for g in range(4):
                    for half in range(2):
                        part = slice(g * band + half * 8, g * band + half * 8 + 8)
                        for at, value in (
                            (column_at(z, i, g, half), across[part, lane(h)]),
                            (column_at(zs - 1 - z, band - 1 - i, g, half), back[part, lane(h)]),
                        ):
                            if g in added:
                                wide[h, at, :] = wide[h, at, :] + value
                            else:
                                wide[h, at, :] = value

        @pl.when(is_end)
        def _():
            put((0, 3))

        @pl.when(is_middle)
        def _():
            put((1, 2))

        return 0

    def section_at(sec):
        return pl.ds(pl.multiple_of((sec - middle) * section, section), section)

    def multiply(src, sec):
        at = section_at(sec)
        weight = jnp.concatenate([wide[h, at, :] for h in range(classes // LANES)], axis=1)
        return jnp.dot(full[src, sec], weight, precision=lax.Precision.HIGHEST, preferred_element_type=F32)

    def keep(src, sec):
        block = full[src, sec]
        if rows < LANES:
            block = jnp.concatenate([block, jnp.zeros((LANES - rows, section), F32)], axis=0)
        high, low = halves(block.T)
        at = pl.ds(pl.multiple_of(src * LANES, LANES), LANES)
        tall_high[section_at(sec), at] = high
        tall_low[section_at(sec), at] = low

    for src in range(zs):
        post_high[src * LANES + rows : (src + 1) * LANES, :] = jnp.zeros((LANES - rows, classes), BF16)
        post_low[src * LANES + rows : (src + 1) * LANES, :] = jnp.zeros((LANES - rows, classes), BF16)

    for load, at in load_quarters[1:]:
        load.wait()
        repack(at)
    load_refs.wait()
    norm = lax.fori_loop(0, band, put_rows, jnp.zeros((1, classes), F32))
    start = jnp.broadcast_to(-0.5 * norm, (rows, classes))
    for src in range(zs):
        scores[src] = start

    units = 3 * (zs - 1)

    def chunk(n):
        end_src, end_sec = z + inward * (n // 3 + 1), lax.rem(n + 1, 3)
        early = n < units - 3
        near = z + inward * jnp.where(early, 1 - 2 * lax.rem(n, 2), 2)
        near_sec = 1 + jnp.where(early, n // 2, n - (units - 3))
        return jnp.where(is_end, end_src, near), jnp.where(is_end, end_sec, near_sec)

    def take_z(n):
        src, sec = chunk(n)
        go_in(src, sec).wait_recv()
        from_out = is_middle & (src == z - inward)
        from_in = is_middle & (src != z - inward) & (sec < 3)

        @pl.when(from_out)
        def _():
            go_in(src, sec).start()

        @pl.when(from_in)
        def _():
            go_out(src, sec).start()

        go_x(src, sec).start()

    def take_x(n):
        src, sec = chunk(n)
        go_x(src, sec).wait_recv()
        go_cx(src, sec).start()

    def take_item(item):
        other_src, other_sec = chunk(jnp.maximum(item - 3, 0))
        own = item < 3
        src = jnp.where(own, z, other_src)
        sec = jnp.where(own, middle + item, other_sec)

        @pl.when(item >= 3)
        def _():
            go_cx(src, sec).wait_recv()

        scores[src] = scores[src] + multiply(src, sec)
        keep(src, sec)
        n = item - 3
        last = (is_end & (lax.rem(n, 3) == 2)) | (is_middle & ((n == 4) | (n == 5) | (n == 8)))

        @pl.when((item >= 3) & last)
        def _():
            partial(src).start()

    @pl.when(is_middle)
    def _():
        take_z(0)

    def unit(n, _):
        @pl.when(n + middle < units)
        def _():
            take_z(n + middle)

        @pl.when((n >= 1) & (n <= units))
        def _():
            take_x(n - 1)

        @pl.when(n < 2)
        def _():
            lax.fori_loop(n * band // 2, (n + 1) * band // 2, put_columns, 0)

        @pl.when(n >= 2)
        def _():
            first = jnp.where(n < 5, 2 * (n - 2), n + 1)

            def run(item, _):
                take_item(item)
                return 0

            lax.fori_loop(first, first + jnp.where(n < 5, 2, 1), run, 0)

        return 0

    lax.fori_loop(0, units + 2, unit, 0)

    total_score = scores[z]
    for d in range(1, zs):
        src = lax.rem(z + d, zs)
        send(scores.at[src], parts.at[src], s_send.at[src], s_recv.at[src], {"img": src}).wait_recv()
        total_score = total_score + parts[src]
    groups = group_ref[...]
    sigma_row = jnp.zeros(groups.shape, F32)
    for g in range(noise_ref.shape[1]):
        sigma_row = jnp.where(groups == g, noise_ref[0:1, g : g + 1], sigma_row)

    def upright(row):
        return jnp.broadcast_to(row, (LANES, row.shape[1])).T[:, 0:1]

    total_score = total_score / upright(sigma_row)
    top = jnp.max(total_score, axis=1, keepdims=True)
    shifted = jnp.exp(total_score - top)
    posts[z] = shifted

    def give(src):
        return send(posts.at[z], posts.at[z], p_send.at[src], p_recv.at[z], {"img": src})

    def give_factor(src):
        return send(factors.at[z], factors.at[z], f_send.at[src], f_recv.at[z], {"img": src})

    for d in range(1, zs):
        give(lax.rem(z + d, zs)).start()
    total = jnp.sum(shifted, axis=1, keepdims=True)
    place = lax.broadcasted_iota(jnp.int32, (rows, LANES), 1)
    pair = jnp.where(place < LANES // 2, top, total)
    if rows < LANES:
        pair = jnp.concatenate([pair, jnp.ones((LANES - rows, LANES), F32)], axis=0)
    pair = pair.T
    tops, totals = pair[0:8], pair[LANES // 2 : LANES // 2 + 8]
    stats[3, 0:8, :] = tops
    stats[3, 8:16, :] = totals
    shares = [send(stats.at[3], stats.at[m], t_send.at[m], t_recv.at[m], where) for m, where in enumerate(others)]
    for share in shares:
        share.start()
    for share in shares:
        share.wait()
    best = tops
    for m in range(3):
        best = jnp.maximum(best, stats[m, 0:8, :])
    summed = totals * jnp.exp(tops - best)
    for m in range(3):
        summed = summed + stats[m, 8:16, :] * jnp.exp(stats[m, 0:8, :] - best)
    evidence = best + jnp.log(summed)
    evidence_ref[...] = evidence[0:1, :rows]
    factors[z] = jnp.exp(tops - evidence)
    for d in range(1, zs):
        give_factor(lax.rem(z + d, zs)).start()

    def settle_posts(src, weight_sum):
        factor = upright(factors[src, 0:1, :])[:rows]
        post = posts[src] * factor
        high, low = halves(post)
        at = pl.ds(pl.multiple_of(src * LANES, LANES), rows)
        post_high[at, :] = high
        post_low[at, :] = low
        return weight_sum + jnp.sum(post, axis=0, keepdims=True)

    weight_sum = settle_posts(z, jnp.zeros((1, classes), F32))
    for d in range(1, zs):
        src = lax.rem(z + d, zs)
        send(posts.at[src], posts.at[src], p_send.at[src], p_recv.at[src], {"img": src}).wait_recv()
        send(factors.at[src], factors.at[src], f_send.at[src], f_recv.at[src], {"img": src}).wait_recv()
        weight_sum = settle_posts(src, weight_sum)
    weights_ref[...] = weight_sum * weight_scale
    width = section

    def weigh(n, _):
        at = pl.ds(pl.multiple_of(n * width, width), width)
        ah, al, bh, bl = tall_high[at, :], tall_low[at, :], post_high[...], post_low[...]
        one = lambda p, q: jnp.dot(p, q, preferred_element_type=F32)
        result = one(ah, bh) + (one(ah, bl) + one(al, bh))
        for h in range(classes // LANES):
            num[h, at, :] = result[:, lane(h)]
        return 0

    lax.fori_loop(0, 3, weigh, 0)

    scale = 1.0 / (weight_sum + 1.0)

    def finish(i, _):
        fields = []
        for h in range(classes // LANES):
            pull_row = lambda b, j: jnp.concatenate([num[h, row_at(b, j, which), :] for which in range(4)], axis=0)
            pull_column = lambda b, j: jnp.concatenate(
                [num[h, column_at(b, j, g, half), :] for g in range(4) for half in range(2)], axis=0
            )
            up = pull_row(z, i)
            down = pull_row(zs - 1 - z, band - 1 - i)
            across = pull_column(z, i)
            back = pull_column(zs - 1 - z, band - 1 - i)
            k = lane(h)
            fields.append(jnp.where(is_row[:, k], up, jnp.where(is_row_up[:, k], down, jnp.where(is_col[:, k], across, back))))
        field = jnp.concatenate(fields, axis=1)
        means_ref[line(i), :] = jnp.where(flipped, reverse_rows(field), field) * scale
        return 0

    lax.fori_loop(0, band, finish, 0, unroll=2)

    @pl.when(is_end)
    def _():
        for sec in (1, 2, 3):
            go_in(z, sec).wait_send()
        go_far().wait_send()

    @pl.when(is_middle)
    def _():
        for sec_in, sec_out in ((1, 1), (2, 2), (3, 0)):
            go_in(z, sec_in).wait_send()
            go_out(z, sec_out).wait_send()
        go_far().wait_send()

    def settle(n, _):
        src, sec = chunk(n)

        @pl.when(is_middle & (src == z - inward))
        def _():
            go_in(src, sec).wait_send()

        @pl.when(is_middle & (src != z - inward) & (sec < 3))
        def _():
            go_out(src, sec).wait_send()

        go_x(src, sec).wait_send()
        go_cx(src, sec).wait_send()
        return 0

    lax.fori_loop(0, units, settle, 0)
    for d in range(1, zs):
        src = lax.rem(z + d, zs)
        partial(src).wait_send()
        give(src).wait_send()
        give_factor(src).wait_send()


def turned_images_body(zs, images, references, rotations, image_group, noise_var):
    rows = images.shape[0]
    pixels, classes = references.shape
    class_total = classes * lax.axis_size("ref") * lax.axis_size("rep")
    image_total = rows * zs
    dma = pltpu.SemaphoreType.DMA
    vmem = pl.BlockSpec(memory_space=pltpu.VMEM)
    many = dma((zs, 4))
    section = PIXELS // 4
    means, weight_sum, evidence = pl.pallas_call(
        functools.partial(kernel, zs, class_total / image_total),
        name="class_step",
        out_shape=(
            jax.ShapeDtypeStruct((pixels, classes), F32),
            jax.ShapeDtypeStruct((1, classes), F32),
            jax.ShapeDtypeStruct((1, rows), F32),
        ),
        in_specs=[pl.BlockSpec(memory_space=pl.ANY), pl.BlockSpec(memory_space=pl.ANY), vmem, vmem, vmem],
        out_specs=(vmem, vmem, vmem),
        scratch_shapes=[
            pltpu.VMEM((rows, PIXELS), F32),
            pltpu.VMEM((zs, 4, rows, section), F32),
            pltpu.VMEM((classes // LANES, 3 * section, LANES), F32),
            pltpu.VMEM((zs, rows, classes), F32),
            pltpu.VMEM((zs, rows, classes), F32),
            pltpu.VMEM((4, 16, LANES), F32),
            pltpu.VMEM((zs, rows, classes), F32),
            pltpu.VMEM((classes // LANES, 3 * section, LANES), F32),
            pltpu.VMEM((pixels, classes), F32),
            pltpu.VMEM((zs, 8, LANES), F32),
            pltpu.VMEM((3 * section, zs * LANES), BF16),
            pltpu.VMEM((3 * section, zs * LANES), BF16),
            pltpu.VMEM((zs * LANES, classes), BF16),
            pltpu.VMEM((zs * LANES, classes), BF16),
            dma((4,)), dma, many, many, many, many, many, dma, many, many,
            dma((zs,)), dma((zs,)), dma((3,)), dma((3,)), dma((zs,)), dma((zs,)), dma((zs,)), dma((zs,)),
        ],
        compiler_params=pltpu.CompilerParams(
            collective_id=0, has_side_effects=True, vmem_limit_bytes=VMEM_BYTES
        ),
    )(images, references, rotations[None, :], image_group[None, :], noise_var[None, :])
    return (means, weight_sum[0], evidence[0])


def solution(mesh):
    sizes = dict(mesh.shape)
    placed = (
        P(("groups", "img"), None),
        P("img", ("groups", "ref", "rep")),
        P(("groups", "ref", "rep")),
        P(("groups", "img")),
        P(),
    )

    def choose(images, references, rotations, image_group, noise_var):
        zs = sizes["img"]
        rows = images.shape[0]
        fits = (
            sizes["ref"] == 2
            and sizes["rep"] == 2
            and rows % 32 == 0
            and rows <= LANES
            and zs == 4
            and IMAGE_SIDE == 64
            and references.shape[1] % LANES == 0
            and zs * rows * PIXELS * 4 <= 12 * 1024 * 1024
        )
        if fits:
            return turned_images_body(zs, images, references, rotations, image_group, noise_var)
        return body(images, references, rotations, image_group, noise_var)

    return jax.shard_map(
        choose,
        mesh=mesh,
        in_specs=placed,
        out_specs=(
            P("img", ("groups", "ref", "rep")),
            P(("groups", "ref", "rep")),
            P(("groups", "img")),
        ),
        check_vma=False,
    )
```

```python
import functools

import jax
import jax.numpy as jnp
from jax import lax
from jax.experimental import pallas as pl
from jax.experimental.pallas import tpu as pltpu
from jax.sharding import PartitionSpec as P

IMAGE_SIDE = 64
PIXELS = 4096
MESH = pl.DeviceIdType.MESH
F32 = jnp.float32
BF16 = jnp.bfloat16
LANES = 128
VMEM_BYTES = 62 * 1024 * 1024


def joined(part, axis, combine):
    gathered = jax.tree.map(lambda a: lax.all_gather(a, axis), part)

    def take(source):
        return jax.tree.map(lambda a: lax.dynamic_index_in_dim(a, source, 0, False), gathered)

    return lax.fori_loop(
        1, lax.axis_size(axis), lambda source, state: combine(state, take(source)), take(0)
    )


def turn_forward(field, which):
    quarter = which % 4
    base = field if which < 4 else jnp.swapaxes(field, 0, 1)
    return jnp.rot90(base, quarter, axes=(0, 1))


def turn_inverse(field, which):
    quarter = which % 4
    base = jnp.rot90(field, -quarter, axes=(0, 1))
    return base if which < 4 else jnp.swapaxes(base, 0, 1)


def select_turn(field, rotations, turner):
    result = jnp.zeros_like(field)
    for which in range(8):
        result = jnp.where(rotations[None, None, :] == which, turner(field, which), result)
    return result


def combine_stats(first, second):
    top = jnp.maximum(first[0], second[0])
    total = first[1] * jnp.exp(first[0] - top) + second[1] * jnp.exp(second[0] - top)
    return (top, total)


def body(images, references, rotations, image_group, noise_var):
    gathered = lax.all_gather(references, "img", axis=0, tiled=True)
    rotated = select_turn(
        gathered.reshape(IMAGE_SIDE, IMAGE_SIDE, -1), rotations, turn_inverse
    ).reshape(PIXELS, -1)
    norms = jnp.sum(gathered * gathered, axis=0)
    group_hot = image_group[:, None] == jnp.arange(noise_var.shape[0])[None, :]
    sigma = jnp.sum(jnp.where(group_hot, noise_var[None, :], 0.0), axis=1)
    scores = (
        jnp.dot(
            images, rotated, precision=lax.Precision.HIGHEST, preferred_element_type=jnp.float32
        )
        - 0.5 * norms[None, :]
    ) / sigma[:, None]
    local_top = jnp.max(scores, axis=1)
    local_total = jnp.sum(jnp.exp(scores - local_top[:, None]), axis=1)
    top, total = joined((local_top, local_total), ("ref", "rep"), combine_stats)
    log_evidence = top + jnp.log(total)
    posterior = jnp.exp(scores - log_evidence[:, None])
    weight_sum = lax.psum(jnp.sum(posterior, axis=0), "img")
    numer_image = lax.dot_general(
        images,
        posterior,
        (((0,), (0,)), ((), ())),
        precision=lax.Precision.HIGHEST,
        preferred_element_type=jnp.float32,
    )
    numerator = select_turn(
        numer_image.reshape(IMAGE_SIDE, IMAGE_SIDE, -1), rotations, turn_forward
    ).reshape(PIXELS, -1)
    owned = lax.psum_scatter(numerator, "img", scatter_dimension=0, tiled=True)
    class_means = owned / (weight_sum + 1.0)[None, :]
    class_total = weight_sum.shape[0] * lax.axis_size("ref") * lax.axis_size("rep")
    image_total = images.shape[0] * lax.axis_size("img")
    class_weights = weight_sum * (class_total / image_total)
    return (class_means, class_weights, log_evidence)


def halves(x):
    high = x.astype(BF16)
    return high, (x - high.astype(F32)).astype(BF16)


def reverse_rows(x):
    place = lax.broadcasted_iota(jnp.int32, (8, x.shape[1]), 0)
    odd = place % 2 == 1
    second = (place // 2) % 2 == 1
    pieces = []
    for g in reversed(range(x.shape[0] // 8)):
        p = x[8 * g : 8 * g + 8]
        p = jnp.where(odd, pltpu.roll(p, 1, 0), pltpu.roll(p, 7, 0))
        p = jnp.where(second, pltpu.roll(p, 2, 0), pltpu.roll(p, 6, 0))
        pieces.append(pltpu.roll(p, 4, 0))
    return jnp.concatenate(pieces, axis=0)


def kernel(
    zs, weight_scale,
    images_ref, source_ref, rot_ref, group_ref, noise_ref,
    means_ref, weights_ref, evidence_ref,
    raw, full, wide, scores, parts, stats, posts, num, refs_ref, facs, sigmas, tall_high, tall_low, post_high, post_low,
    load_sem, refs_sem, z_recv, pair_recv, x_recv, cx_recv,
    in_send, out_send, far_send, pair_send, x_send, cx_send, g_send, g_recv,
    s_send, s_recv, t_send, t_recv, p_send, p_recv, f_send, f_recv,
):
    z = lax.axis_index("img")
    x = lax.axis_index("ref")
    c = lax.axis_index("rep")
    rows = images_ref.shape[0]
    classes = refs_ref.shape[1]
    quarter = rows // 4
    side = IMAGE_SIDE
    band = side // zs
    section = PIXELS // 4
    others = [{"ref": 1 - x}, {"rep": 1 - c}, {"ref": 1 - x, "rep": 1 - c}]
    upper = jnp.where(z >= 2, 1, 0)
    middle = jnp.where((z == 1) | (z == 2), 1, 0)
    inward = 1 - 2 * upper

    def quarter_at(xi, ci):
        return pl.ds(pl.multiple_of((ci * 2 + xi) * quarter, 8), quarter)

    load_quarters = []
    for q, (xi, ci) in enumerate([(x, c), (1 - x, c), (x, 1 - c), (1 - x, 1 - c)]):
        at = quarter_at(xi, ci)
        load_quarters.append((pltpu.make_async_copy(images_ref.at[at, :], raw.at[at, :], load_sem.at[q]), at))
    for load, _ in load_quarters:
        load.start()
    load_refs = pltpu.make_async_copy(source_ref, refs_ref, refs_sem)
    load_refs.start()
    barrier = pltpu.get_barrier_semaphore()
    for d in range(1, zs):
        pl.semaphore_signal(barrier, inc=1, device_id={"img": lax.rem(z + d, zs)}, device_id_type=MESH)
    for where in others:
        pl.semaphore_signal(barrier, inc=1, device_id=where, device_id_type=MESH)

    def repack(at):
        place = lax.broadcasted_iota(jnp.int32, (quarter, LANES), 1) // band
        low = place % 4
        for g in range(4):
            for v in range(4):
                first = raw[at, g * section + v * LANES : g * section + (v + 1) * LANES]
                start = g * section + section // 2 + v * LANES
                second = raw[at, start : start + LANES]
                first_a, first_b = pltpu.roll(first, band, 1), pltpu.roll(first, 5 * band, 1)
                second_a, second_b = pltpu.roll(second, 3 * band, 1), pltpu.roll(second, 7 * band, 1)
                outer = jnp.where(low < 2, jnp.where(low == 0, first_b, first_a), jnp.where(low == 2, second_b, second_a))
                inner = jnp.where(low < 2, second_b, first_a)
                which = 0 if g in (0, 3) else 2
                start = (section // 2 if g >= 2 else 0) + v * LANES
                full[z, which, at, start : start + LANES] = outer
                full[z, which + 1, at, start : start + LANES] = inner

    load_quarters[0][0].wait()
    repack(load_quarters[0][1])
    pl.semaphore_wait(barrier, zs + 2)

    def send(src, dst, ssem, rsem, where):
        return pltpu.make_async_remote_copy(
            src_ref=src, dst_ref=dst, send_sem=ssem, recv_sem=rsem,
            device_id=where, device_id_type=MESH,
        )

    def piece(src, sec):
        return full.at[src, sec, quarter_at(x, c), :]

    def go_in(src, sec):
        return send(piece(src, sec), piece(src, sec), in_send.at[src, sec], z_recv.at[src, sec], {"img": z + inward})

    def go_out(src, sec):
        return send(piece(src, sec), piece(src, sec), out_send.at[src, sec], z_recv.at[src, sec], {"img": z - inward})

    def go_far():
        target = jnp.where(upper == 1, 0, zs - 1)
        return send(piece(z, 0), piece(z, 0), far_send, z_recv.at[z, 0], {"img": target})

    def go_x(src, sec):
        return send(piece(src, sec), piece(src, sec), x_send.at[src, sec], x_recv.at[src, sec], {"ref": 1 - x})

    def go_cx(src, sec):
        pair = full.at[src, sec, pl.ds(pl.multiple_of(c * 2 * quarter, 8), 2 * quarter), :]
        return send(pair, pair, cx_send.at[src, sec], cx_recv.at[src, sec], {"rep": 1 - c})

    def go_pair(src, sec):
        rest = full.at[src, sec, quarter_at(1 - x, c), :]
        return send(rest, rest, pair_send.at[sec], pair_recv.at[sec], {"img": z + inward})

    def partial_in(src, number, slot):
        return send(scores.at[src], parts.at[slot], s_send.at[number], s_recv.at[slot], {"img": z + inward})

    def partial_out(src, number):
        return send(scores.at[src], parts.at[0], s_send.at[number], s_recv.at[0], {"img": z - inward})

    give_sigma = send(sigmas.at[0], sigmas.at[1], g_send, g_recv, {"img": zs - 1 - z})

    is_end = middle == 0
    is_middle = middle == 1
    near, across_z, far = z - inward, z + inward, z + 2 * inward

    @pl.when(is_end)
    def _():
        for sec in (1, 2, 3):
            go_in(z, sec).start()
        go_far().start()

    @pl.when(is_middle)
    def _():
        for sec_in, sec_out in ((1, 1), (2, 2), (3, 0)):
            go_in(z, sec_in).start()
            go_out(z, sec_out).start()
        go_far().start()

    rot = rot_ref[...]
    is_row = (rot == 0) | (rot == 7)
    is_row_up = (rot == 5) | (rot == 2)
    is_col = (rot == 4) | (rot == 3)
    is_col_up = (rot == 1) | (rot == 6)
    flipped = (rot == 7) | (rot == 2) | (rot == 3) | (rot == 6)

    def lane(h):
        return slice(h * LANES, (h + 1) * LANES)

    def line(i):
        return pl.ds(pl.multiple_of(i * side, side), side)

    def row_at(b, i, which):
        base = jnp.where(b >= 2, section // 2, 0) + side * lax.rem(i, 8)
        if which in (0, 3):
            place = base + section * middle + 2 * band * (i // 8) + (band if which == 0 else 0)
        else:
            place = base + section * (middle + 1) + 2 * band * (1 - i // 8) + (band if which == 2 else 0)
        return pl.ds(pl.multiple_of(place, band), band)

    def column_at(b, i, g, half):
        base = (0 if g in (0, 3) else 2 * section) + (section // 2 if g >= 2 else 0)
        swapped = half + middle * (1 - 2 * half)
        place = base + 2 * band * swapped + band * (1 - lax.rem(b, 2)) + i
        return pl.ds(place, 8, stride=side)

    def turned(i):
        field = refs_ref[line(i), :]
        return jnp.where(flipped, reverse_rows(field), field)

    def put_rows(i, norm):
        raw_field = refs_ref[line(i), :]
        field = turned(i)
        up = jnp.where(is_row, field, 0.0)
        down = jnp.where(is_row_up, field, 0.0)
        for h in range(classes // LANES):
            for which in range(4):
                part = slice(which * band, (which + 1) * band)
                wide[h, row_at(z, i, which), :] = up[part, lane(h)]
                wide[h, row_at(zs - 1 - z, band - 1 - i, which), :] = down[part, lane(h)]
        return norm + jnp.sum(raw_field * raw_field, axis=0, keepdims=True)

    def put_columns(i, _):
        field = turned(i)
        across = jnp.where(is_col, field, 0.0)
        back = jnp.where(is_col_up, field, 0.0)

        def put(added):
            for h in range(classes // LANES):
                for g in range(4):
                    for half in range(2):
                        part = slice(g * band + half * 8, g * band + half * 8 + 8)
                        for at, value in (
                            (column_at(z, i, g, half), across[part, lane(h)]),
                            (column_at(zs - 1 - z, band - 1 - i, g, half), back[part, lane(h)]),
                        ):
                            if g in added:
                                wide[h, at, :] = wide[h, at, :] + value
                            else:
                                wide[h, at, :] = value

        @pl.when(is_end)
        def _():
            put((0, 3))

        @pl.when(is_middle)
        def _():
            put((1, 2))

        return 0

    def section_at(sec):
        return pl.ds(pl.multiple_of((sec - middle) * section, section), section)

    def multiply(src, sec):
        at = section_at(sec)
        weight = jnp.concatenate([wide[h, at, :] for h in range(classes // LANES)], axis=1)
        return jnp.dot(full[src, sec], weight, precision=lax.Precision.HIGHEST, preferred_element_type=F32)

    def keep(src, sec):
        block = full[src, sec]
        if rows < LANES:
            block = jnp.concatenate([block, jnp.zeros((LANES - rows, section), F32)], axis=0)
        high, low = halves(block.T)
        slot = jnp.where(src == 0, 2, jnp.where(src == zs - 1, zs - 1, src - 1))
        at = pl.ds(pl.multiple_of(slot * LANES, LANES), LANES)
        tall_high[section_at(sec), at] = high
        tall_low[section_at(sec), at] = low

    for src in range(zs):
        post_high[src * LANES + rows : (src + 1) * LANES, :] = jnp.zeros((LANES - rows, classes), BF16)
        post_low[src * LANES + rows : (src + 1) * LANES, :] = jnp.zeros((LANES - rows, classes), BF16)

    groups = group_ref[...]
    sigma_row = jnp.ones(groups.shape, F32)
    for g in range(noise_ref.shape[1]):
        sigma_row = jnp.where(groups == g, noise_ref[0:1, g : g + 1], sigma_row)
    if rows < LANES:
        sigma_row = jnp.concatenate([sigma_row, jnp.ones((1, LANES - rows), F32)], axis=1)
    sigmas[0] = jnp.broadcast_to(sigma_row, (8, LANES))
    give_sigma.start()

    load_quarters[1][0].wait()
    repack(load_quarters[1][1])

    @pl.when(is_end)
    def _():
        for sec in (1, 2, 3):
            go_pair(z, sec).start()

    for load, at in load_quarters[2:]:
        load.wait()
        repack(at)
    load_refs.wait()
    norm = lax.fori_loop(0, band, put_rows, jnp.zeros((1, classes), F32))
    start = jnp.broadcast_to(-0.5 * norm, (rows, classes))
    for src in range(zs):
        scores[src] = start

    units = 3 * (zs - 1)

    def chunk(n):
        return z + inward * (n // 3 + 1), lax.rem(n + 1, 3)

    def end_unit(n):
        @pl.when(n < units)
        def _():
            src, sec = chunk(n)
            go_in(src, sec).wait_recv()
            go_x(src, sec).start()

        @pl.when((n >= 1) & (n <= units))
        def _():
            src, sec = chunk(n - 1)
            go_x(src, sec).wait_recv()
            go_cx(src, sec).start()

    def pass_out(src, sec):
        go_in(src, sec).wait_recv()

        @pl.when(sec < 3)
        def _():
            go_out(src, sec).start()

        go_x(src, sec).start()

    def take_x(src, sec):
        go_x(src, sec).wait_recv()
        go_cx(src, sec).start()

    def middle_unit(n):
        @pl.when(n < 3)
        def _():
            pass_out(across_z, n + 1)
            go_in(near, n + 1).wait_recv()
            go_in(near, n + 1).start()

        @pl.when((n >= 4) & (n < 7))
        def _():
            pass_out(far, n - 3)
            go_pair(near, n - 3).wait_recv()
            go_cx(near, n - 3).start()

        @pl.when((n >= 1) & (n < 4))
        def _():
            take_x(across_z, n)

        @pl.when((n >= 5) & (n < 8))
        def _():
            take_x(far, n - 4)

    def take_item(item):
        other = jnp.maximum(item - 3, 0)
        end_src, end_sec = chunk(other)
        middle_src = jnp.where(other < 3, across_z, jnp.where(other < 6, near, far))
        own = item < 3
        src = jnp.where(own, z, jnp.where(is_end, end_src, middle_src))
        sec = jnp.where(own, middle + item, jnp.where(is_end, end_sec, 1 + lax.rem(other, 3)))

        @pl.when(item >= 3)
        def _():
            go_cx(src, sec).wait_recv()

        scores[src] = scores[src] + multiply(src, sec)
        keep(src, sec)

    def arrived(slot):
        partial_in(z, 0, slot).wait_recv()
        return parts[slot]

    def end_sums(n):
        for when, src, number in ((3, z, 0), (4, z + inward, 1), (7, z + 2 * inward, 2)):
            @pl.when(n == when)
            def _():
                partial_in(src, number, number).start()

    def middle_sums(n):
        @pl.when(n == 7)
        def _():
            scores[near] = scores[near] + arrived(0)
            partial_in(near, 0, 4).start()
            scores[z] = scores[z] + arrived(1)
            partial_in(z, 1, 3).start()

        @pl.when(n == 9)
        def _():
            scores[far] = scores[far] + arrived(4)
            partial_out(far, 2).start()

    def unit(n, _):
        @pl.when(is_end)
        def _():
            end_unit(n)

        @pl.when(is_middle)
        def _():
            middle_unit(n)

        @pl.when(n < 2)
        def _():
            lax.fori_loop(n * band // 2, (n + 1) * band // 2, put_columns, 0)

        @pl.when(n >= 2)
        def _():
            single = jnp.where(n < 5, 2 * (n - 2), n + 1)
            first = jnp.where(is_middle & (n >= 8), 2 * n - 6, single)
            paired = (n < 5) | (is_middle & (n >= 7))
            count = jnp.where(is_middle & (n >= 9), 0, jnp.where(paired, 2, 1))

            def run(item, _):
                take_item(item)
                return 0

            lax.fori_loop(first, first + count, run, 0)

        @pl.when(is_end)
        def _():
            end_sums(n)

        @pl.when(is_middle)
        def _():
            middle_sums(n)

        return 0

    lax.fori_loop(0, units + 2, unit, 0)

    owned = zs - 1 - z

    @pl.when(is_end)
    def _():
        scores[owned] = scores[owned] + arrived(0)

    @pl.when(is_middle)
    def _():
        scores[owned] = scores[owned] + arrived(2) + arrived(3)

    def upright(row):
        return jnp.broadcast_to(row, (LANES, row.shape[1])).T[:rows, 0:1]

    give_sigma.wait_recv()
    total_score = scores[owned] / upright(sigmas[1, 0:1, :])
    top = jnp.max(total_score, axis=1, keepdims=True)
    shifted = jnp.exp(total_score - top)
    posts[owned] = shifted
    givers = [lax.rem(z + d, zs) for d in range(1, zs)]

    def give(d):
        where = {"img": lax.rem(z + d, zs)}
        return send(posts.at[owned], posts.at[owned], p_send.at[d], p_recv.at[owned], where)

    def give_factor(d):
        where = {"img": lax.rem(z + d, zs)}
        return send(facs.at[owned], facs.at[owned], f_send.at[d], f_recv.at[owned], where)

    def take_posts(src):
        send(posts.at[src], posts.at[src], p_send.at[0], p_recv.at[src], {"img": givers[0]}).wait_recv()
        send(facs.at[src], facs.at[src], f_send.at[0], f_recv.at[src], {"img": givers[0]}).wait_recv()

    for d in (3, 2, 1):
        give(d).start()
    total = jnp.sum(shifted, axis=1, keepdims=True)
    place = lax.broadcasted_iota(jnp.int32, (rows, LANES), 1)
    pair = jnp.where(place < LANES // 2, top, total)
    if rows < LANES:
        pair = jnp.concatenate([pair, jnp.ones((LANES - rows, LANES), F32)], axis=0)
    pair = pair.T
    tops, totals = pair[0:8], pair[LANES // 2 : LANES // 2 + 8]
    stats[3, 0:8, :] = tops
    stats[3, 8:16, :] = totals
    shares = [send(stats.at[3], stats.at[m], t_send.at[m], t_recv.at[m], where) for m, where in enumerate(others)]
    for share in shares:
        share.start()
    for share in shares:
        share.wait()
    best = tops
    for m in range(3):
        best = jnp.maximum(best, stats[m, 0:8, :])
    summed = totals * jnp.exp(tops - best)
    for m in range(3):
        summed = summed + stats[m, 8:16, :] * jnp.exp(stats[m, 0:8, :] - best)
    evidence = best + jnp.log(summed)
    facs[owned, 0:8, :] = jnp.exp(tops - evidence)
    facs[owned, 8:16, :] = evidence
    for d in (3, 2, 1):
        give_factor(d).start()

    def settle_posts(src, slot, weight_sum):
        @pl.when(z != zs - 1 - src)
        def _():
            take_posts(src)

        factor = upright(facs[src, 0:1, :])
        post = posts[src] * factor
        high, low = halves(post)
        post_high[slot * LANES : slot * LANES + rows, :] = high
        post_low[slot * LANES : slot * LANES + rows, :] = low
        return weight_sum + jnp.sum(post, axis=0, keepdims=True)

    def weigh(half, add):
        part = slice(half * 2 * LANES, (half + 1) * 2 * LANES)

        def step(n, _):
            at = pl.ds(pl.multiple_of(n * section, section), section)
            ah, al, bh, bl = tall_high[at, part], tall_low[at, part], post_high[part, :], post_low[part, :]
            one = lambda p, q: jnp.dot(p, q, preferred_element_type=F32)
            result = one(ah, bh) + (one(ah, bl) + one(al, bh))
            for h in range(classes // LANES):
                num[h, at, :] = num[h, at, :] + result[:, lane(h)] if add else result[:, lane(h)]
            return 0

        lax.fori_loop(0, 3, step, 0)

    weight_sum = settle_posts(1, 0, jnp.zeros((1, classes), F32))
    weight_sum = settle_posts(2, 1, weight_sum)
    weigh(0, False)
    weight_sum = settle_posts(0, 2, weight_sum)
    weight_sum = settle_posts(3, 3, weight_sum)
    weigh(1, True)
    weights_ref[...] = weight_sum * weight_scale
    evidence_ref[...] = facs[z, 8:9, :rows]
    scale = 1.0 / (weight_sum + 1.0)

    def finish(i, _):
        fields = []
        for h in range(classes // LANES):
            pull_row = lambda b, j: jnp.concatenate([num[h, row_at(b, j, which), :] for which in range(4)], axis=0)
            pull_column = lambda b, j: jnp.concatenate(
                [num[h, column_at(b, j, g, half), :] for g in range(4) for half in range(2)], axis=0
            )
            up = pull_row(z, i)
            down = pull_row(zs - 1 - z, band - 1 - i)
            across = pull_column(z, i)
            back = pull_column(zs - 1 - z, band - 1 - i)
            k = lane(h)
            fields.append(jnp.where(is_row[:, k], up, jnp.where(is_row_up[:, k], down, jnp.where(is_col[:, k], across, back))))
        field = jnp.concatenate(fields, axis=1)
        means_ref[line(i), :] = jnp.where(flipped, reverse_rows(field), field) * scale
        return 0

    lax.fori_loop(0, band, finish, 0, unroll=2)

    @pl.when(is_end)
    def _():
        for sec in (1, 2, 3):
            go_in(z, sec).wait_send()
            go_pair(z, sec).wait_send()

        def settle(n, _):
            src, sec = chunk(n)
            go_x(src, sec).wait_send()
            go_cx(src, sec).wait_send()
            return 0

        lax.fori_loop(0, units, settle, 0)

    @pl.when(is_middle)
    def _():
        for sec in (1, 2, 3):
            go_in(z, sec).wait_send()
            go_out(z, sec - 1).wait_send()
            go_in(near, sec).wait_send()
            go_cx(near, sec).wait_send()
            for src in (across_z, far):
                if sec < 3:
                    go_out(src, sec).wait_send()
                go_x(src, sec).wait_send()
                go_cx(src, sec).wait_send()

    go_far().wait_send()
    give_sigma.wait_send()
    for number in range(3):
        partial_in(z, number, 0).wait_send()
    for d in (1, 2, 3):
        give(d).wait_send()
        give_factor(d).wait_send()


def turned_images_body(zs, images, references, rotations, image_group, noise_var):
    rows = images.shape[0]
    pixels, classes = references.shape
    class_total = classes * lax.axis_size("ref") * lax.axis_size("rep")
    image_total = rows * zs
    dma = pltpu.SemaphoreType.DMA
    vmem = pl.BlockSpec(memory_space=pltpu.VMEM)
    many = dma((zs, 4))
    section = PIXELS // 4
    means, weight_sum, evidence = pl.pallas_call(
        functools.partial(kernel, zs, class_total / image_total),
        name="class_step",
        out_shape=(
            jax.ShapeDtypeStruct((pixels, classes), F32),
            jax.ShapeDtypeStruct((1, classes), F32),
            jax.ShapeDtypeStruct((1, rows), F32),
        ),
        in_specs=[pl.BlockSpec(memory_space=pl.ANY), pl.BlockSpec(memory_space=pl.ANY), vmem, vmem, vmem],
        out_specs=(vmem, vmem, vmem),
        scratch_shapes=[
            pltpu.VMEM((rows, PIXELS), F32),
            pltpu.VMEM((zs, 4, rows, section), F32),
            pltpu.VMEM((classes // LANES, 3 * section, LANES), F32),
            pltpu.VMEM((zs, rows, classes), F32),
            pltpu.VMEM((5, rows, classes), F32),
            pltpu.VMEM((4, 16, LANES), F32),
            pltpu.VMEM((zs, rows, classes), F32),
            pltpu.VMEM((classes // LANES, 3 * section, LANES), F32),
            pltpu.VMEM((pixels, classes), F32),
            pltpu.VMEM((zs, 16, LANES), F32),
            pltpu.VMEM((2, 8, LANES), F32),
            pltpu.VMEM((3 * section, zs * LANES), BF16),
            pltpu.VMEM((3 * section, zs * LANES), BF16),
            pltpu.VMEM((zs * LANES, classes), BF16),
            pltpu.VMEM((zs * LANES, classes), BF16),
            dma((4,)), dma, many, dma((4,)), many, many, many, many, dma, dma((4,)), many, many, dma, dma,
            dma((3,)), dma((5,)), dma((3,)), dma((3,)), dma((zs,)), dma((zs,)), dma((zs,)), dma((zs,)),
        ],
        compiler_params=pltpu.CompilerParams(
            collective_id=0, has_side_effects=True, vmem_limit_bytes=VMEM_BYTES
        ),
    )(images, references, rotations[None, :], image_group[None, :], noise_var[None, :])
    return (means, weight_sum[0], evidence[0])


def solution(mesh):
    sizes = dict(mesh.shape)
    placed = (
        P(("groups", "img"), None),
        P("img", ("groups", "ref", "rep")),
        P(("groups", "ref", "rep")),
        P(("groups", "img")),
        P(),
    )

    def choose(images, references, rotations, image_group, noise_var):
        zs = sizes["img"]
        rows = images.shape[0]
        fits = (
            sizes["ref"] == 2
            and sizes["rep"] == 2
            and rows % 32 == 0
            and rows <= LANES
            and zs == 4
            and IMAGE_SIDE == 64
            and references.shape[1] % LANES == 0
            and zs * rows * PIXELS * 4 <= 12 * 1024 * 1024
        )
        if fits:
            return turned_images_body(zs, images, references, rotations, image_group, noise_var)
        return body(images, references, rotations, image_group, noise_var)

    return jax.shard_map(
        choose,
        mesh=mesh,
        in_specs=placed,
        out_specs=(
            P("img", ("groups", "ref", "rep")),
            P(("groups", "ref", "rep")),
            P(("groups", "img")),
        ),
        check_vma=False,
    )
```

```python
import functools

import jax
import jax.numpy as jnp
from jax import lax
from jax.experimental import pallas as pl
from jax.experimental.pallas import tpu as pltpu
from jax.sharding import PartitionSpec as P

IMAGE_SIDE = 64
PIXELS = 4096
MESH = pl.DeviceIdType.MESH
F32 = jnp.float32
BF16 = jnp.bfloat16
LANES = 128
LAG = 3
AHEAD = 3
VMEM_BYTES = 62 * 1024 * 1024


def joined(part, axis, combine):
    gathered = jax.tree.map(lambda a: lax.all_gather(a, axis), part)

    def take(source):
        return jax.tree.map(lambda a: lax.dynamic_index_in_dim(a, source, 0, False), gathered)

    return lax.fori_loop(
        1, lax.axis_size(axis), lambda source, state: combine(state, take(source)), take(0)
    )


def turn_forward(field, which):
    quarter = which % 4
    base = field if which < 4 else jnp.swapaxes(field, 0, 1)
    return jnp.rot90(base, quarter, axes=(0, 1))


def turn_inverse(field, which):
    quarter = which % 4
    base = jnp.rot90(field, -quarter, axes=(0, 1))
    return base if which < 4 else jnp.swapaxes(base, 0, 1)


def select_turn(field, rotations, turner):
    result = jnp.zeros_like(field)
    for which in range(8):
        result = jnp.where(rotations[None, None, :] == which, turner(field, which), result)
    return result


def combine_stats(first, second):
    top = jnp.maximum(first[0], second[0])
    total = first[1] * jnp.exp(first[0] - top) + second[1] * jnp.exp(second[0] - top)
    return (top, total)


def body(images, references, rotations, image_group, noise_var):
    gathered = lax.all_gather(references, "img", axis=0, tiled=True)
    rotated = select_turn(
        gathered.reshape(IMAGE_SIDE, IMAGE_SIDE, -1), rotations, turn_inverse
    ).reshape(PIXELS, -1)
    norms = jnp.sum(gathered * gathered, axis=0)
    group_hot = image_group[:, None] == jnp.arange(noise_var.shape[0])[None, :]
    sigma = jnp.sum(jnp.where(group_hot, noise_var[None, :], 0.0), axis=1)
    scores = (
        jnp.dot(
            images, rotated, precision=lax.Precision.HIGHEST, preferred_element_type=jnp.float32
        )
        - 0.5 * norms[None, :]
    ) / sigma[:, None]
    local_top = jnp.max(scores, axis=1)
    local_total = jnp.sum(jnp.exp(scores - local_top[:, None]), axis=1)
    top, total = joined((local_top, local_total), ("ref", "rep"), combine_stats)
    log_evidence = top + jnp.log(total)
    posterior = jnp.exp(scores - log_evidence[:, None])
    weight_sum = lax.psum(jnp.sum(posterior, axis=0), "img")
    numer_image = lax.dot_general(
        images,
        posterior,
        (((0,), (0,)), ((), ())),
        precision=lax.Precision.HIGHEST,
        preferred_element_type=jnp.float32,
    )
    numerator = select_turn(
        numer_image.reshape(IMAGE_SIDE, IMAGE_SIDE, -1), rotations, turn_forward
    ).reshape(PIXELS, -1)
    owned = lax.psum_scatter(numerator, "img", scatter_dimension=0, tiled=True)
    class_means = owned / (weight_sum + 1.0)[None, :]
    class_total = weight_sum.shape[0] * lax.axis_size("ref") * lax.axis_size("rep")
    image_total = images.shape[0] * lax.axis_size("img")
    class_weights = weight_sum * (class_total / image_total)
    return (class_means, class_weights, log_evidence)


def halves(x):
    high = x.astype(BF16)
    return high, (x - high.astype(F32)).astype(BF16)


def reverse_rows(x):
    place = lax.broadcasted_iota(jnp.int32, (8, x.shape[1]), 0)
    odd = place % 2 == 1
    second = (place // 2) % 2 == 1
    pieces = []
    for g in reversed(range(x.shape[0] // 8)):
        p = x[8 * g : 8 * g + 8]
        p = jnp.where(odd, pltpu.roll(p, 1, 0), pltpu.roll(p, 7, 0))
        p = jnp.where(second, pltpu.roll(p, 2, 0), pltpu.roll(p, 6, 0))
        pieces.append(pltpu.roll(p, 4, 0))
    return jnp.concatenate(pieces, axis=0)


def kernel(
    zs, weight_scale,
    images_ref, source_ref, rot_ref, group_ref, noise_ref,
    means_ref, weights_ref, evidence_ref,
    raw, full, wide, scores, parts, stats, posts, num, refs_ref, facs, sigmas, tall_high, tall_low, post_high, post_low,
    load_sem, refs_sem, z_recv, pair_recv, x_recv, cx_recv,
    in_send, out_send, far_send, pair_send, x_send, cx_send, g_send, g_recv,
    s_send, s_recv, t_send, t_recv, p_send, p_recv, f_send, f_recv,
):
    z = lax.axis_index("img")
    x = lax.axis_index("ref")
    c = lax.axis_index("rep")
    rows = images_ref.shape[0]
    classes = refs_ref.shape[1]
    quarter = rows // 4
    side = IMAGE_SIDE
    band = side // zs
    section = PIXELS // 8
    others = [{"ref": 1 - x}, {"rep": 1 - c}, {"ref": 1 - x, "rep": 1 - c}]
    upper = jnp.where(z >= 2, 1, 0)
    middle = jnp.where((z == 1) | (z == 2), 1, 0)
    inward = 1 - 2 * upper

    def quarter_at(xi, ci):
        return pl.ds(pl.multiple_of((ci * 2 + xi) * quarter, 8), quarter)

    load_quarters = []
    for q, (xi, ci) in enumerate([(x, c), (1 - x, c), (x, 1 - c), (1 - x, 1 - c)]):
        at = quarter_at(xi, ci)
        load_quarters.append((pltpu.make_async_copy(images_ref.at[at, :], raw.at[at, :], load_sem.at[q]), at))
    for load, _ in load_quarters:
        load.start()
    load_refs = pltpu.make_async_copy(source_ref, refs_ref, refs_sem)
    load_refs.start()
    barrier = pltpu.get_barrier_semaphore()
    for d in range(1, zs):
        pl.semaphore_signal(barrier, inc=1, device_id={"img": lax.rem(z + d, zs)}, device_id_type=MESH)
    for where in others:
        pl.semaphore_signal(barrier, inc=1, device_id=where, device_id_type=MESH)

    def repack(at):
        place = lax.broadcasted_iota(jnp.int32, (quarter, LANES), 1) // band
        low = place % 4
        for g in range(4):
            for v in range(4):
                start = 2 * g * section + v * LANES
                first = raw[at, start : start + LANES]
                start = (2 * g + 1) * section + v * LANES
                second = raw[at, start : start + LANES]
                first_a, first_b = pltpu.roll(first, band, 1), pltpu.roll(first, 5 * band, 1)
                second_a, second_b = pltpu.roll(second, 3 * band, 1), pltpu.roll(second, 7 * band, 1)
                outer = jnp.where(low < 2, jnp.where(low == 0, first_b, first_a), jnp.where(low == 2, second_b, second_a))
                inner = jnp.where(low < 2, second_b, first_a)
                which = (0 if g in (0, 3) else 4) + g // 2
                full[z, which, at, v * LANES : (v + 1) * LANES] = outer
                full[z, which + 2, at, v * LANES : (v + 1) * LANES] = inner

    load_quarters[0][0].wait()
    repack(load_quarters[0][1])
    pl.semaphore_wait(barrier, zs + 2)

    def send(src, dst, ssem, rsem, where):
        return pltpu.make_async_remote_copy(
            src_ref=src, dst_ref=dst, send_sem=ssem, recv_sem=rsem,
            device_id=where, device_id_type=MESH,
        )

    def piece(src, sec):
        return full.at[src, sec, quarter_at(x, c), :]

    def go_in(src, sec):
        return send(piece(src, sec), piece(src, sec), in_send.at[src, sec], z_recv.at[src, sec], {"img": z + inward})

    def go_out(src, sec):
        return send(piece(src, sec), piece(src, sec), out_send.at[src, sec], z_recv.at[src, sec], {"img": z - inward})

    def go_far(sec):
        target = jnp.where(upper == 1, 0, zs - 1)
        return send(piece(z, sec), piece(z, sec), far_send.at[sec], z_recv.at[z, sec], {"img": target})

    def go_x(src, sec):
        return send(piece(src, sec), piece(src, sec), x_send.at[src, sec], x_recv.at[src, sec], {"ref": 1 - x})

    def go_cx(src, sec):
        pair = full.at[src, sec, pl.ds(pl.multiple_of(c * 2 * quarter, 8), 2 * quarter), :]
        return send(pair, pair, cx_send.at[src, sec], cx_recv.at[src, sec], {"rep": 1 - c})

    def go_pair(src, sec):
        rest = full.at[src, sec, quarter_at(1 - x, c), :]
        return send(rest, rest, pair_send.at[sec], pair_recv.at[sec], {"img": z + inward})

    def partial_in(src, number, slot):
        return send(scores.at[src], parts.at[slot], s_send.at[number], s_recv.at[slot], {"img": z + inward})

    def partial_out(src, number):
        return send(scores.at[src], parts.at[0], s_send.at[number], s_recv.at[0], {"img": z - inward})

    give_sigma = send(sigmas.at[0], sigmas.at[1], g_send, g_recv, {"img": zs - 1 - z})

    is_end = middle == 0
    is_middle = middle == 1
    near, across_z, far = z - inward, z + inward, z + 2 * inward

    def end_send(i):
        @pl.when(i < 6)
        def _():
            go_in(z, i + 2).start()

        @pl.when((i >= 6) & (i < 12))
        def _():
            go_pair(z, i - 4).start()

        @pl.when((i >= 12) & (i < 14))
        def _():
            go_far(i - 12).start()

    def middle_send(i):
        @pl.when(i < 6)
        def _():
            go_in(z, i + 2).start()
            go_out(z, lax.rem(i + 2, 6)).start()

        @pl.when((i >= 6) & (i < 10))
        def _():
            go_in(near, i - 4).start()
            go_out(across_z, i - 4).start()

        @pl.when((i >= 10) & (i < 12))
        def _():
            go_far(i - 10).start()

        @pl.when((i >= 12) & (i < 14))
        def _():
            go_in(near, i - 6).start()

    @pl.when(is_end)
    def _():
        for i in range(AHEAD):
            end_send(i)

    @pl.when(is_middle)
    def _():
        for i in range(AHEAD):
            middle_send(i)

    rot = rot_ref[...]
    is_row = (rot == 0) | (rot == 7)
    is_row_up = (rot == 5) | (rot == 2)
    is_col = (rot == 4) | (rot == 3)
    is_col_up = (rot == 1) | (rot == 6)
    flipped = (rot == 7) | (rot == 2) | (rot == 3) | (rot == 6)

    def lane(h):
        return slice(h * LANES, (h + 1) * LANES)

    def line(i):
        return pl.ds(pl.multiple_of(i * side, side), side)

    def row_at(b, i, which):
        base = jnp.where(b >= 2, section, 0) + side * lax.rem(i, 8)
        if which in (0, 3):
            place = base + 2 * section * middle + 2 * band * (i // 8) + (band if which == 0 else 0)
        else:
            place = base + 2 * section * (middle + 1) + 2 * band * (1 - i // 8) + (band if which == 2 else 0)
        return pl.ds(pl.multiple_of(place, band), band)

    def column_at(b, i, g, half):
        base = (0 if g in (0, 3) else 4 * section) + (section if g >= 2 else 0)
        swapped = half + middle * (1 - 2 * half)
        place = base + 2 * band * swapped + band * (1 - lax.rem(b, 2)) + i
        return pl.ds(place, 8, stride=side)

    def turned(i):
        field = refs_ref[line(i), :]
        return jnp.where(flipped, reverse_rows(field), field)

    def put_rows(i, norm):
        raw_field = refs_ref[line(i), :]
        field = turned(i)
        up = jnp.where(is_row, field, 0.0)
        down = jnp.where(is_row_up, field, 0.0)
        for h in range(classes // LANES):
            for which in range(4):
                part = slice(which * band, (which + 1) * band)
                wide[h, row_at(z, i, which), :] = up[part, lane(h)]
                wide[h, row_at(zs - 1 - z, band - 1 - i, which), :] = down[part, lane(h)]
        return norm + jnp.sum(raw_field * raw_field, axis=0, keepdims=True)

    def put_columns(i, _):
        field = turned(i)
        across = jnp.where(is_col, field, 0.0)
        back = jnp.where(is_col_up, field, 0.0)

        def put(added):
            for h in range(classes // LANES):
                for g in range(4):
                    for half in range(2):
                        part = slice(g * band + half * 8, g * band + half * 8 + 8)
                        for at, value in (
                            (column_at(z, i, g, half), across[part, lane(h)]),
                            (column_at(zs - 1 - z, band - 1 - i, g, half), back[part, lane(h)]),
                        ):
                            if g in added:
                                wide[h, at, :] = wide[h, at, :] + value
                            else:
                                wide[h, at, :] = value

        @pl.when(is_end)
        def _():
            put((0, 3))

        @pl.when(is_middle)
        def _():
            put((1, 2))

        return 0

    def section_at(sec):
        return pl.ds(pl.multiple_of((sec - 2 * middle) * section, section), section)

    def multiply(src, sec):
        at = section_at(sec)
        weight = jnp.concatenate([wide[h, at, :] for h in range(classes // LANES)], axis=1)
        return jnp.dot(full[src, sec], weight, precision=lax.Precision.HIGHEST, preferred_element_type=F32)

    def keep(src, sec):
        block = full[src, sec]
        if rows < LANES:
            block = jnp.concatenate([block, jnp.zeros((LANES - rows, section), F32)], axis=0)
        high, low = halves(block.T)
        slot = jnp.where(src == 0, 2, jnp.where(src == zs - 1, zs - 1, src - 1))
        at = pl.ds(pl.multiple_of(slot * LANES, LANES), LANES)
        tall_high[section_at(sec), at] = high
        tall_low[section_at(sec), at] = low

    for src in range(zs):
        post_high[src * LANES + rows : (src + 1) * LANES, :] = jnp.zeros((LANES - rows, classes), BF16)
        post_low[src * LANES + rows : (src + 1) * LANES, :] = jnp.zeros((LANES - rows, classes), BF16)

    groups = group_ref[...]
    sigma_row = jnp.ones(groups.shape, F32)
    for g in range(noise_ref.shape[1]):
        sigma_row = jnp.where(groups == g, noise_ref[0:1, g : g + 1], sigma_row)
    if rows < LANES:
        sigma_row = jnp.concatenate([sigma_row, jnp.ones((1, LANES - rows), F32)], axis=1)
    sigmas[0] = jnp.broadcast_to(sigma_row, (8, LANES))
    give_sigma.start()

    load_quarters[1][0].wait()
    repack(load_quarters[1][1])

    for load, at in load_quarters[2:]:
        load.wait()
        repack(at)
    load_refs.wait()
    norm = lax.fori_loop(0, band, put_rows, jnp.zeros((1, classes), F32))
    start = jnp.broadcast_to(-0.5 * norm, (rows, classes))
    for src in range(zs):
        scores[src] = start

    units = 6 * (zs - 1)

    def chunk(n):
        return z + inward * (n // 6 + 1), lax.rem(n + 2, 6)

    def end_unit(n):
        @pl.when(n < units)
        def _():
            src, sec = chunk(n)
            go_in(src, sec).wait_recv()
            go_x(src, sec).start()
            end_send(n + AHEAD)

        @pl.when((n >= LAG) & (n < units + LAG))
        def _():
            src, sec = chunk(n - LAG)
            go_x(src, sec).wait_recv()
            go_cx(src, sec).start()

    def pass_x(src, sec):
        go_in(src, sec).wait_recv()
        go_x(src, sec).start()

    def take_x(src, sec):
        go_x(src, sec).wait_recv()
        go_cx(src, sec).start()

    def middle_unit(n):
        @pl.when(n < 6)
        def _():
            pass_x(across_z, n + 2)
            go_in(near, n + 2).wait_recv()

        middle_send(n + AHEAD)

        @pl.when((n >= 6) & (n < 10))
        def _():
            pass_x(far, n - 4)
            go_out(far, n - 4).start()

        @pl.when((n >= 12) & (n < 14))
        def _():
            pass_x(far, n - 6)

        @pl.when((n >= 6) & (n < 12))
        def _():
            go_pair(near, n - 4).wait_recv()
            go_cx(near, n - 4).start()

        @pl.when((n >= LAG) & (n < LAG + 6))
        def _():
            take_x(across_z, n - LAG + 2)

        @pl.when((n >= LAG + 6) & (n < LAG + 10))
        def _():
            take_x(far, n - LAG - 4)

        @pl.when((n >= LAG + 12) & (n < LAG + 14))
        def _():
            take_x(far, n - LAG - 6)

    def take_item(item):
        other = jnp.maximum(item - 6, 0)
        end_src, end_sec = chunk(other)
        middle_src = jnp.where(other < 6, across_z, jnp.where(other < 12, near, far))
        own = item < 6
        src = jnp.where(own, z, jnp.where(is_end, end_src, middle_src))
        sec = jnp.where(own, 2 * middle + item, jnp.where(is_end, end_sec, 2 + lax.rem(other, 6)))

        @pl.when(item >= 6)
        def _():
            go_cx(src, sec).wait_recv()

        scores[src] = scores[src] + multiply(src, sec)
        keep(src, sec)

    def arrived(slot):
        partial_in(z, 0, slot).wait_recv()
        return parts[slot]

    def end_sums(n):
        for when, src, number in ((6, z, 0), (9, z + inward, 1), (15, z + 2 * inward, 2)):
            @pl.when(n == when)
            def _():
                partial_in(src, number, number).start()

    def middle_sums(n):
        @pl.when(n == 12)
        def _():
            scores[near] = scores[near] + arrived(0)
            partial_in(near, 0, 4).start()
            scores[z] = scores[z] + arrived(1)
            partial_in(z, 1, 3).start()

        @pl.when(n == 17)
        def _():
            scores[far] = scores[far] + arrived(4)
            partial_out(far, 2).start()

    def unit(n, _):
        @pl.when(is_end)
        def _():
            end_unit(n)

        @pl.when(is_middle)
        def _():
            middle_unit(n)

        @pl.when(n < 4)
        def _():
            lax.fori_loop(n * band // 4, (n + 1) * band // 4, put_columns, 0)

        @pl.when(n >= 4)
        def _():
            end_first = jnp.where(n < 10, 2 * (n - 4), n + 2)
            end_count = jnp.where(n < 10, 2, 1)
            middle_first = jnp.where(n < 15, 2 * (n - 4), 22)
            middle_count = jnp.where((n < 15) | (n == 17), 2, 0)
            first = jnp.where(is_end, end_first, middle_first)
            count = jnp.where(is_end, end_count, middle_count)

            def run(item, _):
                take_item(item)
                return 0

            lax.fori_loop(first, first + count, run, 0)

        @pl.when(is_end)
        def _():
            end_sums(n)

        @pl.when(is_middle)
        def _():
            middle_sums(n)

        return 0

    lax.fori_loop(0, units + LAG + 1, unit, 0)

    owned = zs - 1 - z

    @pl.when(is_end)
    def _():
        scores[owned] = scores[owned] + arrived(0)

    @pl.when(is_middle)
    def _():
        scores[owned] = scores[owned] + arrived(2) + arrived(3)

    def upright(row):
        return jnp.broadcast_to(row, (LANES, row.shape[1])).T[:rows, 0:1]

    give_sigma.wait_recv()
    total_score = scores[owned] / upright(sigmas[1, 0:1, :])
    top = jnp.max(total_score, axis=1, keepdims=True)
    shifted = jnp.exp(total_score - top)
    posts[owned] = shifted
    givers = [lax.rem(z + d, zs) for d in range(1, zs)]

    def give(d):
        where = {"img": lax.rem(z + d, zs)}
        return send(posts.at[owned], posts.at[owned], p_send.at[d], p_recv.at[owned], where)

    def give_factor(d):
        where = {"img": lax.rem(z + d, zs)}
        return send(facs.at[owned], facs.at[owned], f_send.at[d], f_recv.at[owned], where)

    def take_posts(src):
        send(posts.at[src], posts.at[src], p_send.at[0], p_recv.at[src], {"img": givers[0]}).wait_recv()
        send(facs.at[src], facs.at[src], f_send.at[0], f_recv.at[src], {"img": givers[0]}).wait_recv()

    for d in (3, 2, 1):
        give(d).start()
    total = jnp.sum(shifted, axis=1, keepdims=True)
    place = lax.broadcasted_iota(jnp.int32, (rows, LANES), 1)
    pair = jnp.where(place < LANES // 2, top, total)
    if rows < LANES:
        pair = jnp.concatenate([pair, jnp.ones((LANES - rows, LANES), F32)], axis=0)
    pair = pair.T
    tops, totals = pair[0:8], pair[LANES // 2 : LANES // 2 + 8]
    stats[3, 0:8, :] = tops
    stats[3, 8:16, :] = totals
    shares = [send(stats.at[3], stats.at[m], t_send.at[m], t_recv.at[m], where) for m, where in enumerate(others)]
    for share in shares:
        share.start()
    for share in shares:
        share.wait()
    best = tops
    for m in range(3):
        best = jnp.maximum(best, stats[m, 0:8, :])
    summed = totals * jnp.exp(tops - best)
    for m in range(3):
        summed = summed + stats[m, 8:16, :] * jnp.exp(stats[m, 0:8, :] - best)
    evidence = best + jnp.log(summed)
    facs[owned, 0:8, :] = jnp.exp(tops - evidence)
    facs[owned, 8:16, :] = evidence
    for d in (3, 2, 1):
        give_factor(d).start()

    def settle_posts(src, slot, weight_sum):
        @pl.when(z != zs - 1 - src)
        def _():
            take_posts(src)

        factor = upright(facs[src, 0:1, :])
        post = posts[src] * factor
        high, low = halves(post)
        post_high[slot * LANES : slot * LANES + rows, :] = high
        post_low[slot * LANES : slot * LANES + rows, :] = low
        return weight_sum + jnp.sum(post, axis=0, keepdims=True)

    def weigh(half, add):
        part = slice(half * 2 * LANES, (half + 1) * 2 * LANES)

        def step(n, _):
            at = pl.ds(pl.multiple_of(2 * n * section, 2 * section), 2 * section)
            ah, al, bh, bl = tall_high[at, part], tall_low[at, part], post_high[part, :], post_low[part, :]
            one = lambda p, q: jnp.dot(p, q, preferred_element_type=F32)
            result = one(ah, bh) + (one(ah, bl) + one(al, bh))
            for h in range(classes // LANES):
                num[h, at, :] = num[h, at, :] + result[:, lane(h)] if add else result[:, lane(h)]
            return 0

        lax.fori_loop(0, 3, step, 0)

    weight_sum = settle_posts(1, 0, jnp.zeros((1, classes), F32))
    weight_sum = settle_posts(2, 1, weight_sum)
    weigh(0, False)
    weight_sum = settle_posts(0, 2, weight_sum)
    weight_sum = settle_posts(3, 3, weight_sum)
    weigh(1, True)
    weights_ref[...] = weight_sum * weight_scale
    evidence_ref[...] = facs[z, 8:9, :rows]
    scale = 1.0 / (weight_sum + 1.0)

    def finish(i, _):
        fields = []
        for h in range(classes // LANES):
            pull_row = lambda b, j: jnp.concatenate([num[h, row_at(b, j, which), :] for which in range(4)], axis=0)
            pull_column = lambda b, j: jnp.concatenate(
                [num[h, column_at(b, j, g, half), :] for g in range(4) for half in range(2)], axis=0
            )
            up = pull_row(z, i)
            down = pull_row(zs - 1 - z, band - 1 - i)
            across = pull_column(z, i)
            back = pull_column(zs - 1 - z, band - 1 - i)
            k = lane(h)
            fields.append(jnp.where(is_row[:, k], up, jnp.where(is_row_up[:, k], down, jnp.where(is_col[:, k], across, back))))
        field = jnp.concatenate(fields, axis=1)
        means_ref[line(i), :] = jnp.where(flipped, reverse_rows(field), field) * scale
        return 0

    lax.fori_loop(0, band, finish, 0, unroll=2)

    @pl.when(is_end)
    def _():
        def settle(n, _):
            src, sec = chunk(n)
            go_x(src, sec).wait_send()
            go_cx(src, sec).wait_send()

            @pl.when(n < 6)
            def _():
                go_in(z, n + 2).wait_send()
                go_pair(z, n + 2).wait_send()

            return 0

        lax.fori_loop(0, units, settle, 0)

    @pl.when(is_middle)
    def _():
        def settle(n, _):
            go_in(z, n + 2).wait_send()
            go_out(z, n).wait_send()
            go_in(near, n + 2).wait_send()
            go_cx(near, n + 2).wait_send()
            for src in (across_z, far):
                @pl.when(n < 4)
                def _():
                    go_out(src, n + 2).wait_send()

                go_x(src, n + 2).wait_send()
                go_cx(src, n + 2).wait_send()

            return 0

        lax.fori_loop(0, 6, settle, 0)

    go_far(0).wait_send()
    go_far(1).wait_send()
    give_sigma.wait_send()
    for number in range(3):
        partial_in(z, number, 0).wait_send()
    for d in (1, 2, 3):
        give(d).wait_send()
        give_factor(d).wait_send()


def turned_images_body(zs, images, references, rotations, image_group, noise_var):
    rows = images.shape[0]
    pixels, classes = references.shape
    class_total = classes * lax.axis_size("ref") * lax.axis_size("rep")
    image_total = rows * zs
    dma = pltpu.SemaphoreType.DMA
    vmem = pl.BlockSpec(memory_space=pltpu.VMEM)
    many = dma((zs, 8))
    section = PIXELS // 8
    means, weight_sum, evidence = pl.pallas_call(
        functools.partial(kernel, zs, class_total / image_total),
        name="class_step",
        out_shape=(
            jax.ShapeDtypeStruct((pixels, classes), F32),
            jax.ShapeDtypeStruct((1, classes), F32),
            jax.ShapeDtypeStruct((1, rows), F32),
        ),
        in_specs=[pl.BlockSpec(memory_space=pl.ANY), pl.BlockSpec(memory_space=pl.ANY), vmem, vmem, vmem],
        out_specs=(vmem, vmem, vmem),
        scratch_shapes=[
            pltpu.VMEM((rows, PIXELS), F32),
            pltpu.VMEM((zs, 8, rows, section), F32),
            pltpu.VMEM((classes // LANES, 6 * section, LANES), F32),
            pltpu.VMEM((zs, rows, classes), F32),
            pltpu.VMEM((5, rows, classes), F32),
            pltpu.VMEM((4, 16, LANES), F32),
            pltpu.VMEM((zs, rows, classes), F32),
            pltpu.VMEM((classes // LANES, 6 * section, LANES), F32),
            pltpu.VMEM((pixels, classes), F32),
            pltpu.VMEM((zs, 16, LANES), F32),
            pltpu.VMEM((2, 8, LANES), F32),
            pltpu.VMEM((6 * section, zs * LANES), BF16),
            pltpu.VMEM((6 * section, zs * LANES), BF16),
            pltpu.VMEM((zs * LANES, classes), BF16),
            pltpu.VMEM((zs * LANES, classes), BF16),
            dma((4,)), dma, many, dma((8,)), many, many, many, many, dma((2,)), dma((8,)), many, many, dma, dma,
            dma((3,)), dma((5,)), dma((3,)), dma((3,)), dma((zs,)), dma((zs,)), dma((zs,)), dma((zs,)),
        ],
        compiler_params=pltpu.CompilerParams(
            collective_id=0, has_side_effects=True, vmem_limit_bytes=VMEM_BYTES
        ),
    )(images, references, rotations[None, :], image_group[None, :], noise_var[None, :])
    return (means, weight_sum[0], evidence[0])


def solution(mesh):
    sizes = dict(mesh.shape)
    placed = (
        P(("groups", "img"), None),
        P("img", ("groups", "ref", "rep")),
        P(("groups", "ref", "rep")),
        P(("groups", "img")),
        P(),
    )

    def choose(images, references, rotations, image_group, noise_var):
        zs = sizes["img"]
        rows = images.shape[0]
        fits = (
            sizes["ref"] == 2
            and sizes["rep"] == 2
            and rows % 32 == 0
            and rows <= LANES
            and zs == 4
            and IMAGE_SIDE == 64
            and references.shape[1] % LANES == 0
            and zs * rows * PIXELS * 4 <= 12 * 1024 * 1024
        )
        if fits:
            return turned_images_body(zs, images, references, rotations, image_group, noise_var)
        return body(images, references, rotations, image_group, noise_var)

    return jax.shard_map(
        choose,
        mesh=mesh,
        in_specs=placed,
        out_specs=(
            P("img", ("groups", "ref", "rep")),
            P(("groups", "ref", "rep")),
            P(("groups", "img")),
        ),
        check_vma=False,
    )
```

```python
import functools

import jax
import jax.numpy as jnp
from jax import lax
from jax.experimental import pallas as pl
from jax.experimental.pallas import tpu as pltpu
from jax.sharding import PartitionSpec as P

IMAGE_SIDE = 64
PIXELS = 4096
MESH = pl.DeviceIdType.MESH
F32 = jnp.float32
BF16 = jnp.bfloat16
LANES = 128
LAG = 3
GAP = 8
AHEAD = 3
VMEM_BYTES = 62 * 1024 * 1024


def joined(part, axis, combine):
    gathered = jax.tree.map(lambda a: lax.all_gather(a, axis), part)

    def take(source):
        return jax.tree.map(lambda a: lax.dynamic_index_in_dim(a, source, 0, False), gathered)

    return lax.fori_loop(
        1, lax.axis_size(axis), lambda source, state: combine(state, take(source)), take(0)
    )


def turn_forward(field, which):
    quarter = which % 4
    base = field if which < 4 else jnp.swapaxes(field, 0, 1)
    return jnp.rot90(base, quarter, axes=(0, 1))


def turn_inverse(field, which):
    quarter = which % 4
    base = jnp.rot90(field, -quarter, axes=(0, 1))
    return base if which < 4 else jnp.swapaxes(base, 0, 1)


def select_turn(field, rotations, turner):
    result = jnp.zeros_like(field)
    for which in range(8):
        result = jnp.where(rotations[None, None, :] == which, turner(field, which), result)
    return result


def combine_stats(first, second):
    top = jnp.maximum(first[0], second[0])
    total = first[1] * jnp.exp(first[0] - top) + second[1] * jnp.exp(second[0] - top)
    return (top, total)


def body(images, references, rotations, image_group, noise_var):
    gathered = lax.all_gather(references, "img", axis=0, tiled=True)
    rotated = select_turn(
        gathered.reshape(IMAGE_SIDE, IMAGE_SIDE, -1), rotations, turn_inverse
    ).reshape(PIXELS, -1)
    norms = jnp.sum(gathered * gathered, axis=0)
    group_hot = image_group[:, None] == jnp.arange(noise_var.shape[0])[None, :]
    sigma = jnp.sum(jnp.where(group_hot, noise_var[None, :], 0.0), axis=1)
    scores = (
        jnp.dot(
            images, rotated, precision=lax.Precision.HIGHEST, preferred_element_type=jnp.float32
        )
        - 0.5 * norms[None, :]
    ) / sigma[:, None]
    local_top = jnp.max(scores, axis=1)
    local_total = jnp.sum(jnp.exp(scores - local_top[:, None]), axis=1)
    top, total = joined((local_top, local_total), ("ref", "rep"), combine_stats)
    log_evidence = top + jnp.log(total)
    posterior = jnp.exp(scores - log_evidence[:, None])
    weight_sum = lax.psum(jnp.sum(posterior, axis=0), "img")
    numer_image = lax.dot_general(
        images,
        posterior,
        (((0,), (0,)), ((), ())),
        precision=lax.Precision.HIGHEST,
        preferred_element_type=jnp.float32,
    )
    numerator = select_turn(
        numer_image.reshape(IMAGE_SIDE, IMAGE_SIDE, -1), rotations, turn_forward
    ).reshape(PIXELS, -1)
    owned = lax.psum_scatter(numerator, "img", scatter_dimension=0, tiled=True)
    class_means = owned / (weight_sum + 1.0)[None, :]
    class_total = weight_sum.shape[0] * lax.axis_size("ref") * lax.axis_size("rep")
    image_total = images.shape[0] * lax.axis_size("img")
    class_weights = weight_sum * (class_total / image_total)
    return (class_means, class_weights, log_evidence)


def halves(x):
    high = x.astype(BF16)
    return high, (x - high.astype(F32)).astype(BF16)


def reverse_rows(x):
    place = lax.broadcasted_iota(jnp.int32, (8, x.shape[1]), 0)
    odd = place % 2 == 1
    second = (place // 2) % 2 == 1
    pieces = []
    for g in reversed(range(x.shape[0] // 8)):
        p = x[8 * g : 8 * g + 8]
        p = jnp.where(odd, pltpu.roll(p, 1, 0), pltpu.roll(p, 7, 0))
        p = jnp.where(second, pltpu.roll(p, 2, 0), pltpu.roll(p, 6, 0))
        pieces.append(pltpu.roll(p, 4, 0))
    return jnp.concatenate(pieces, axis=0)


def kernel(
    zs, weight_scale,
    images_ref, source_ref, rot_ref, group_ref, noise_ref,
    means_out, weights_ref, evidence_ref,
    means_ref, raw, full, wide, scores, parts, stats, posts, num, refs_ref, facs, sigmas, tall_high, tall_low, post_high, post_low,
    load_sem, refs_sem, z_recv, pair_recv, x_recv, cx_recv,
    in_send, out_send, far_send, pair_send, x_send, cx_send, g_send, g_recv,
    s_send, s_recv, t_send, t_recv, p_send, p_recv, f_send, f_recv, out_sem,
):
    z = lax.axis_index("img")
    x = lax.axis_index("ref")
    c = lax.axis_index("rep")
    rows = images_ref.shape[0]
    classes = refs_ref.shape[1]
    quarter = rows // 4
    side = IMAGE_SIDE
    band = side // zs
    apart = side + GAP
    section = PIXELS // 8
    others = [{"ref": 1 - x}, {"rep": 1 - c}, {"ref": 1 - x, "rep": 1 - c}]
    upper = jnp.where(z >= 2, 1, 0)
    middle = jnp.where((z == 1) | (z == 2), 1, 0)
    inward = 1 - 2 * upper

    def quarter_at(xi, ci):
        return pl.ds(pl.multiple_of((ci * 2 + xi) * quarter, 8), quarter)

    load_quarters = []
    for q, (xi, ci) in enumerate([(x, c), (1 - x, c), (x, 1 - c), (1 - x, 1 - c)]):
        at = quarter_at(xi, ci)
        load_quarters.append((pltpu.make_async_copy(images_ref.at[at, :], raw.at[at, :], load_sem.at[q]), at))
    for load, _ in load_quarters:
        load.start()
    load_refs = pltpu.make_async_copy(source_ref, refs_ref, refs_sem)
    load_refs.start()
    barrier = pltpu.get_barrier_semaphore()
    for d in range(1, zs):
        pl.semaphore_signal(barrier, inc=1, device_id={"img": lax.rem(z + d, zs)}, device_id_type=MESH)
    for where in others:
        pl.semaphore_signal(barrier, inc=1, device_id=where, device_id_type=MESH)

    def repack(at):
        place = lax.broadcasted_iota(jnp.int32, (quarter, LANES), 1) // band
        low = place % 4
        for g in range(4):
            for v in range(4):
                start = 2 * g * section + v * LANES
                first = raw[at, start : start + LANES]
                start = (2 * g + 1) * section + v * LANES
                second = raw[at, start : start + LANES]
                first_a, first_b = pltpu.roll(first, band, 1), pltpu.roll(first, 5 * band, 1)
                second_a, second_b = pltpu.roll(second, 3 * band, 1), pltpu.roll(second, 7 * band, 1)
                outer = jnp.where(low < 2, jnp.where(low == 0, first_b, first_a), jnp.where(low == 2, second_b, second_a))
                inner = jnp.where(low < 2, second_b, first_a)
                which = (0 if g in (0, 3) else 4) + g // 2
                full[z, which, at, v * LANES : (v + 1) * LANES] = outer
                full[z, which + 2, at, v * LANES : (v + 1) * LANES] = inner

    load_quarters[0][0].wait()
    repack(load_quarters[0][1])
    pl.semaphore_wait(barrier, zs + 2)

    def send(src, dst, ssem, rsem, where):
        return pltpu.make_async_remote_copy(
            src_ref=src, dst_ref=dst, send_sem=ssem, recv_sem=rsem,
            device_id=where, device_id_type=MESH,
        )

    def piece(src, sec):
        return full.at[src, sec, quarter_at(x, c), :]

    def go_in(src, sec):
        return send(piece(src, sec), piece(src, sec), in_send.at[src, sec], z_recv.at[src, sec], {"img": z + inward})

    def go_out(src, sec):
        return send(piece(src, sec), piece(src, sec), out_send.at[src, sec], z_recv.at[src, sec], {"img": z - inward})

    def go_far(sec):
        target = jnp.where(upper == 1, 0, zs - 1)
        return send(piece(z, sec), piece(z, sec), far_send.at[sec], z_recv.at[z, sec], {"img": target})

    def go_x(src, sec):
        return send(piece(src, sec), piece(src, sec), x_send.at[src, sec], x_recv.at[src, sec], {"ref": 1 - x})

    def go_cx(src, sec):
        pair = full.at[src, sec, pl.ds(pl.multiple_of(c * 2 * quarter, 8), 2 * quarter), :]
        return send(pair, pair, cx_send.at[src, sec], cx_recv.at[src, sec], {"rep": 1 - c})

    def go_pair(src, sec):
        rest = full.at[src, sec, quarter_at(1 - x, c), :]
        return send(rest, rest, pair_send.at[sec], pair_recv.at[sec], {"img": z + inward})

    def partial_in(src, number, slot):
        return send(scores.at[src], parts.at[slot], s_send.at[number], s_recv.at[slot], {"img": z + inward})

    def partial_out(src, number):
        return send(scores.at[src], parts.at[0], s_send.at[number], s_recv.at[0], {"img": z - inward})

    give_sigma = send(sigmas.at[0], sigmas.at[1], g_send, g_recv, {"img": zs - 1 - z})

    is_end = middle == 0
    is_middle = middle == 1
    near, across_z, far = z - inward, z + inward, z + 2 * inward

    def end_send(i):
        @pl.when(i < 6)
        def _():
            go_in(z, i + 2).start()

        @pl.when((i >= 6) & (i < 12))
        def _():
            go_pair(z, i - 4).start()

        @pl.when((i >= 12) & (i < 14))
        def _():
            go_far(i - 12).start()

    def middle_send(i):
        @pl.when(i < 6)
        def _():
            go_in(z, i + 2).start()
            go_out(z, lax.rem(i + 2, 6)).start()

        @pl.when((i >= 6) & (i < 10))
        def _():
            go_in(near, i - 4).start()
            go_out(across_z, i - 4).start()

        @pl.when((i >= 10) & (i < 12))
        def _():
            go_far(i - 10).start()

        @pl.when((i >= 12) & (i < 14))
        def _():
            go_in(near, i - 6).start()

    @pl.when(is_end)
    def _():
        for i in range(AHEAD):
            end_send(i)

    @pl.when(is_middle)
    def _():
        for i in range(AHEAD):
            middle_send(i)

    rot = rot_ref[...]
    is_row = (rot == 0) | (rot == 7)
    is_row_up = (rot == 5) | (rot == 2)
    is_col = (rot == 4) | (rot == 3)
    is_col_up = (rot == 1) | (rot == 6)
    flipped = (rot == 7) | (rot == 2) | (rot == 3) | (rot == 6)

    def lane(h):
        return slice(h * LANES, (h + 1) * LANES)

    def line(i):
        return pl.ds(pl.multiple_of(i * side, side), side)

    def row_at(b, i, which, stride):
        block = 8 * stride
        base = jnp.where(b >= 2, block, 0) + stride * lax.rem(i, 8)
        if which in (0, 3):
            place = base + 2 * block * middle + 2 * band * (i // 8) + (band if which == 0 else 0)
        else:
            place = base + 2 * block * (middle + 1) + 2 * band * (1 - i // 8) + (band if which == 2 else 0)
        return pl.ds(pl.multiple_of(place, 8), band)

    def column_at(b, i, g, half, stride):
        block = 8 * stride
        base = (0 if g in (0, 3) else 4 * block) + (block if g >= 2 else 0)
        swapped = half + middle * (1 - 2 * half)
        place = base + 2 * band * swapped + band * (1 - lax.rem(b, 2)) + i
        return pl.ds(place, 8, stride=stride)

    def turned(i):
        field = refs_ref[line(i), :]
        return jnp.where(flipped, reverse_rows(field), field)

    def put_rows(i, norm):
        raw_field = refs_ref[line(i), :]
        field = turned(i)
        up = jnp.where(is_row, field, 0.0)
        down = jnp.where(is_row_up, field, 0.0)
        for h in range(classes // LANES):
            for which in range(4):
                part = slice(which * band, (which + 1) * band)
                wide[h, row_at(z, i, which, apart), :] = up[part, lane(h)]
                wide[h, row_at(zs - 1 - z, band - 1 - i, which, apart), :] = down[part, lane(h)]
        return norm + jnp.sum(raw_field * raw_field, axis=0, keepdims=True)

    def put_columns(i, _):
        field = turned(i)
        across = jnp.where(is_col, field, 0.0)
        back = jnp.where(is_col_up, field, 0.0)

        def put(added):
            for h in range(classes // LANES):
                for g in range(4):
                    for half in range(2):
                        part = slice(g * band + half * 8, g * band + half * 8 + 8)
                        for at, value in (
                            (column_at(z, i, g, half, apart), across[part, lane(h)]),
                            (column_at(zs - 1 - z, band - 1 - i, g, half, apart), back[part, lane(h)]),
                        ):
                            if g in added:
                                wide[h, at, :] = wide[h, at, :] + value
                            else:
                                wide[h, at, :] = value

        @pl.when(is_end)
        def _():
            put((0, 3))

        @pl.when(is_middle)
        def _():
            put((1, 2))

        return 0

    def section_at(sec):
        return pl.ds(pl.multiple_of((sec - 2 * middle) * section, section), section)

    def multiply(src, sec):
        first = (sec - 2 * middle) * 8 * apart
        pieces = [pl.ds(pl.multiple_of(first + k * apart, 8), side) for k in range(section // side)]
        weight = jnp.concatenate(
            [jnp.concatenate([wide[h, at, :] for at in pieces], axis=0) for h in range(classes // LANES)], axis=1
        )
        return jnp.dot(full[src, sec], weight, precision=lax.Precision.HIGHEST, preferred_element_type=F32)

    def keep(src, sec):
        block = full[src, sec]
        if rows < LANES:
            block = jnp.concatenate([block, jnp.zeros((LANES - rows, section), F32)], axis=0)
        high, low = halves(block.T)
        slot = jnp.where(src == 0, 2, jnp.where(src == zs - 1, zs - 1, src - 1))
        at = pl.ds(pl.multiple_of(slot * LANES, LANES), LANES)
        tall_high[section_at(sec), at] = high
        tall_low[section_at(sec), at] = low

    for src in range(zs):
        post_high[src * LANES + rows : (src + 1) * LANES, :] = jnp.zeros((LANES - rows, classes), BF16)
        post_low[src * LANES + rows : (src + 1) * LANES, :] = jnp.zeros((LANES - rows, classes), BF16)

    groups = group_ref[...]
    sigma_row = jnp.ones(groups.shape, F32)
    for g in range(noise_ref.shape[1]):
        sigma_row = jnp.where(groups == g, noise_ref[0:1, g : g + 1], sigma_row)
    if rows < LANES:
        sigma_row = jnp.concatenate([sigma_row, jnp.ones((1, LANES - rows), F32)], axis=1)
    sigmas[0] = jnp.broadcast_to(sigma_row, (8, LANES))
    give_sigma.start()

    load_quarters[1][0].wait()
    repack(load_quarters[1][1])

    for load, at in load_quarters[2:]:
        load.wait()
        repack(at)
    load_refs.wait()
    norm = lax.fori_loop(0, band, put_rows, jnp.zeros((1, classes), F32))
    start = jnp.broadcast_to(-0.5 * norm, (rows, classes))
    for src in range(zs):
        scores[src] = start

    units = 6 * (zs - 1)

    def chunk(n):
        return z + inward * (n // 6 + 1), lax.rem(n + 2, 6)

    def end_unit(n):
        @pl.when(n < units)
        def _():
            src, sec = chunk(n)
            go_in(src, sec).wait_recv()
            go_x(src, sec).start()
            end_send(n + AHEAD)

        @pl.when((n >= LAG) & (n < units + LAG))
        def _():
            src, sec = chunk(n - LAG)
            go_x(src, sec).wait_recv()
            go_cx(src, sec).start()

    def pass_x(src, sec):
        go_in(src, sec).wait_recv()
        go_x(src, sec).start()

    def take_x(src, sec):
        go_x(src, sec).wait_recv()
        go_cx(src, sec).start()

    def middle_unit(n):
        @pl.when(n < 6)
        def _():
            pass_x(across_z, n + 2)
            go_in(near, n + 2).wait_recv()

        middle_send(n + AHEAD)

        @pl.when((n >= 6) & (n < 10))
        def _():
            pass_x(far, n - 4)
            go_out(far, n - 4).start()

        @pl.when((n >= 12) & (n < 14))
        def _():
            pass_x(far, n - 6)

        @pl.when((n >= 6) & (n < 12))
        def _():
            go_pair(near, n - 4).wait_recv()
            go_cx(near, n - 4).start()

        @pl.when((n >= LAG) & (n < LAG + 6))
        def _():
            take_x(across_z, n - LAG + 2)

        @pl.when((n >= LAG + 6) & (n < LAG + 10))
        def _():
            take_x(far, n - LAG - 4)

        @pl.when((n >= LAG + 12) & (n < LAG + 14))
        def _():
            take_x(far, n - LAG - 6)

    def take_item(item):
        other = jnp.maximum(item - 6, 0)
        end_src, end_sec = chunk(other)
        middle_src = jnp.where(other < 6, across_z, jnp.where(other < 12, near, far))
        own = item < 6
        src = jnp.where(own, z, jnp.where(is_end, end_src, middle_src))
        sec = jnp.where(own, 2 * middle + item, jnp.where(is_end, end_sec, 2 + lax.rem(other, 6)))

        @pl.when(item >= 6)
        def _():
            go_cx(src, sec).wait_recv()

        scores[src] = scores[src] + multiply(src, sec)
        keep(src, sec)

    def arrived(slot):
        partial_in(z, 0, slot).wait_recv()
        return parts[slot]

    def end_sums(n):
        for when, src, number in ((6, z, 0), (9, z + inward, 1), (15, z + 2 * inward, 2)):
            @pl.when(n == when)
            def _():
                partial_in(src, number, number).start()

    def middle_sums(n):
        @pl.when(n == 12)
        def _():
            scores[near] = scores[near] + arrived(0)
            partial_in(near, 0, 4).start()
            scores[z] = scores[z] + arrived(1)
            partial_in(z, 1, 3).start()

        @pl.when(n == 17)
        def _():
            scores[far] = scores[far] + arrived(4)
            partial_out(far, 2).start()

    def unit(n, _):
        @pl.when(is_end)
        def _():
            end_unit(n)

        @pl.when(is_middle)
        def _():
            middle_unit(n)

        @pl.when(n < 4)
        def _():
            lax.fori_loop(n * band // 4, (n + 1) * band // 4, put_columns, 0)

        @pl.when(n >= 4)
        def _():
            end_first = jnp.where(n < 10, 2 * (n - 4), n + 2)
            end_count = jnp.where(n < 10, 2, 1)
            middle_first = jnp.where(n < 15, 2 * (n - 4), 22)
            middle_count = jnp.where((n < 15) | (n == 17), 2, 0)
            first = jnp.where(is_end, end_first, middle_first)
            count = jnp.where(is_end, end_count, middle_count)

            def run(item, _):
                take_item(item)
                return 0

            lax.fori_loop(first, first + count, run, 0)

        @pl.when(is_end)
        def _():
            end_sums(n)

        @pl.when(is_middle)
        def _():
            middle_sums(n)

        return 0

    lax.fori_loop(0, units + LAG + 1, unit, 0)

    owned = zs - 1 - z

    @pl.when(is_end)
    def _():
        scores[owned] = scores[owned] + arrived(0)

    @pl.when(is_middle)
    def _():
        scores[owned] = scores[owned] + arrived(2) + arrived(3)

    def upright(row):
        return jnp.broadcast_to(row, (LANES, row.shape[1])).T[:rows, 0:1]

    give_sigma.wait_recv()
    total_score = scores[owned] / upright(sigmas[1, 0:1, :])
    top = jnp.max(total_score, axis=1, keepdims=True)
    shifted = jnp.exp(total_score - top)
    posts[owned] = shifted
    half_rows = rows // 2

    def give(src, half, where, ssem):
        part = posts.at[src, half * half_rows : (half + 1) * half_rows, :]
        return send(part, part, ssem, p_recv.at[src, half], {"img": where})

    def give_in(half):
        return give(owned, half, z + inward, p_send.at[0, half])

    def give_far(half):
        return give(owned, half, jnp.where(is_end, owned, z + 2 * inward), p_send.at[1, half])

    def give_out(half):
        return give(owned, half, z - inward, p_send.at[2, half])

    def pass_on(half):
        return give(far, half, z + inward, p_send.at[3, half])

    def give_factor(d):
        where = {"img": lax.rem(z + d, zs)}
        return send(facs.at[owned], facs.at[owned], f_send.at[d], f_recv.at[owned], where)

    def take_posts(src):
        @pl.when(is_end | (src != far))
        def _():
            for half in range(2):
                give(src, half, 0, p_send.at[0, half]).wait_recv()

        send(facs.at[src], facs.at[src], f_send.at[0], f_recv.at[src], {"img": owned}).wait_recv()

    for half in range(2):
        give_in(half).start()

    @pl.when(is_middle)
    def _():
        for half in range(2):
            give_out(half).start()

    total = jnp.sum(shifted, axis=1, keepdims=True)
    place = lax.broadcasted_iota(jnp.int32, (rows, LANES), 1)
    pair = jnp.where(place < LANES // 2, top, total)
    if rows < LANES:
        pair = jnp.concatenate([pair, jnp.ones((LANES - rows, LANES), F32)], axis=0)
    pair = pair.T
    tops, totals = pair[0:8], pair[LANES // 2 : LANES // 2 + 8]
    stats[3, 0:8, :] = tops
    stats[3, 8:16, :] = totals
    shares = [send(stats.at[3], stats.at[m], t_send.at[m], t_recv.at[m], where) for m, where in enumerate(others)]
    for share in shares:
        share.start()
    for half in range(2):
        give_far(half).start()
    for share in shares:
        share.wait()
    best = tops
    for m in range(3):
        best = jnp.maximum(best, stats[m, 0:8, :])
    summed = totals * jnp.exp(tops - best)
    for m in range(3):
        summed = summed + stats[m, 8:16, :] * jnp.exp(stats[m, 0:8, :] - best)
    evidence = best + jnp.log(summed)
    facs[owned, 0:8, :] = jnp.exp(tops - evidence)
    facs[owned, 8:16, :] = evidence
    for d in (3, 2, 1):
        give_factor(d).start()

    def settle_posts(src, slot, weight_sum):
        @pl.when(z != zs - 1 - src)
        def _():
            take_posts(src)

        factor = upright(facs[src, 0:1, :])
        post = posts[src] * factor
        high, low = halves(post)
        post_high[slot * LANES : slot * LANES + rows, :] = high
        post_low[slot * LANES : slot * LANES + rows, :] = low
        return weight_sum + jnp.sum(post, axis=0, keepdims=True)

    def weigh(half, add):
        part = slice(half * 2 * LANES, (half + 1) * 2 * LANES)

        def step(n, _):
            at = pl.ds(pl.multiple_of(2 * n * section, 2 * section), 2 * section)
            ah, al, bh, bl = tall_high[at, part], tall_low[at, part], post_high[part, :], post_low[part, :]
            one = lambda p, q: jnp.dot(p, q, preferred_element_type=F32)
            result = one(ah, bh) + (one(ah, bl) + one(al, bh))
            for k in range(2 * section // side):
                at = pl.ds(pl.multiple_of(2 * n * 8 * apart + k * apart, 8), side)
                for h in range(classes // LANES):
                    value = result[k * side : (k + 1) * side, lane(h)]
                    num[h, at, :] = num[h, at, :] + value if add else value
            return 0

        lax.fori_loop(0, 3, step, 0)

    weight_sum = settle_posts(1, 0, jnp.zeros((1, classes), F32))
    weight_sum = settle_posts(2, 1, weight_sum)
    weigh(0, False)

    @pl.when(is_middle)
    def _():
        for half in range(2):
            give(far, half, 0, p_send.at[0, half]).wait_recv()
            pass_on(half).start()

    weight_sum = settle_posts(0, 2, weight_sum)
    weight_sum = settle_posts(3, 3, weight_sum)
    weigh(1, True)
    weights_ref[...] = weight_sum * weight_scale
    evidence_ref[...] = facs[z, 8:9, :rows]
    scale = 1.0 / (weight_sum + 1.0)

    def finish(i, _):
        fields = []
        for h in range(classes // LANES):
            pull_row = lambda b, j: jnp.concatenate([num[h, row_at(b, j, which, apart), :] for which in range(4)], axis=0)
            pull_column = lambda b, j: jnp.concatenate(
                [num[h, column_at(b, j, g, half, apart), :] for g in range(4) for half in range(2)], axis=0
            )
            up = pull_row(z, i)
            down = pull_row(zs - 1 - z, band - 1 - i)
            across = pull_column(z, i)
            back = pull_column(zs - 1 - z, band - 1 - i)
            k = lane(h)
            fields.append(jnp.where(is_row[:, k], up, jnp.where(is_row_up[:, k], down, jnp.where(is_col[:, k], across, back))))
        field = jnp.concatenate(fields, axis=1)
        means_ref[line(i), :] = jnp.where(flipped, reverse_rows(field), field) * scale
        return 0

    step = band // 4

    def store(k):
        at = pl.ds(pl.multiple_of(k * step * side, step * side), step * side)
        return pltpu.make_async_copy(means_ref.at[at, :], means_out.at[at, :], out_sem.at[k])

    for k in range(4):
        lax.fori_loop(k * step, (k + 1) * step, finish, 0, unroll=2)
        store(k).start()

    @pl.when(is_end)
    def _():
        def settle(n, _):
            src, sec = chunk(n)
            go_x(src, sec).wait_send()
            go_cx(src, sec).wait_send()

            @pl.when(n < 6)
            def _():
                go_in(z, n + 2).wait_send()
                go_pair(z, n + 2).wait_send()

            return 0

        lax.fori_loop(0, units, settle, 0)

    @pl.when(is_middle)
    def _():
        def settle(n, _):
            go_in(z, n + 2).wait_send()
            go_out(z, n).wait_send()
            go_in(near, n + 2).wait_send()
            go_cx(near, n + 2).wait_send()
            for src in (across_z, far):
                @pl.when(n < 4)
                def _():
                    go_out(src, n + 2).wait_send()

                go_x(src, n + 2).wait_send()
                go_cx(src, n + 2).wait_send()

            return 0

        lax.fori_loop(0, 6, settle, 0)

    go_far(0).wait_send()
    go_far(1).wait_send()
    for k in range(4):
        store(k).wait()
    give_sigma.wait_send()
    for number in range(3):
        partial_in(z, number, 0).wait_send()
    for d in (1, 2, 3):
        give_factor(d).wait_send()
    for half in range(2):
        give_in(half).wait_send()
        give_far(half).wait_send()

        @pl.when(is_middle)
        def _():
            give_out(half).wait_send()
            pass_on(half).wait_send()


def deliver(means, weights, evidence, means_out, weights_out, evidence_out, held, held_weights, held_evidence, in_sem, out_sem):
    parts = in_sem.shape[0] - 2
    step = means.shape[0] // parts
    pieces = [(means.at[pl.ds(k * step, step)], held.at[pl.ds(k * step, step)], means_out.at[pl.ds(k * step, step)]) for k in range(parts)]
    pieces += [(weights, held_weights, weights_out), (evidence, held_evidence, evidence_out)]
    loads = [pltpu.make_async_copy(a, b, in_sem.at[k]) for k, (a, b, _) in enumerate(pieces)]
    stores = [pltpu.make_async_copy(b, d, out_sem.at[k]) for k, (_, b, d) in enumerate(pieces)]
    for load in loads:
        load.start()
    for load, store in zip(loads, stores):
        load.wait()
        store.start()
    for store in stores:
        store.wait()


def turned_images_body(zs, images, references, rotations, image_group, noise_var):
    rows = images.shape[0]
    pixels, classes = references.shape
    class_total = classes * lax.axis_size("ref") * lax.axis_size("rep")
    image_total = rows * zs
    dma = pltpu.SemaphoreType.DMA
    vmem = pl.BlockSpec(memory_space=pltpu.VMEM)
    many = dma((zs, 8))
    section = PIXELS // 8
    means, weight_sum, evidence = pl.pallas_call(
        functools.partial(kernel, zs, class_total / image_total),
        name="class_step",
        out_shape=(
            jax.ShapeDtypeStruct((pixels, classes), F32),
            jax.ShapeDtypeStruct((1, classes), F32),
            jax.ShapeDtypeStruct((1, rows), F32),
        ),
        in_specs=[pl.BlockSpec(memory_space=pl.ANY), pl.BlockSpec(memory_space=pl.ANY), vmem, vmem, vmem],
        out_specs=(pl.BlockSpec(memory_space=pl.ANY), vmem, vmem),
        scratch_shapes=[
            pltpu.VMEM((pixels, classes), F32),
            pltpu.VMEM((rows, PIXELS), F32),
            pltpu.VMEM((zs, 8, rows, section), F32),
            pltpu.VMEM((classes // LANES, 6 * 8 * (IMAGE_SIDE + GAP), LANES), F32),
            pltpu.VMEM((zs, rows, classes), F32),
            pltpu.VMEM((5, rows, classes), F32),
            pltpu.VMEM((4, 16, LANES), F32),
            pltpu.VMEM((zs, rows, classes), F32),
            pltpu.VMEM((classes // LANES, 6 * 8 * (IMAGE_SIDE + GAP), LANES), F32),
            pltpu.VMEM((pixels, classes), F32),
            pltpu.VMEM((zs, 16, LANES), F32),
            pltpu.VMEM((2, 8, LANES), F32),
            pltpu.VMEM((6 * section, zs * LANES), BF16),
            pltpu.VMEM((6 * section, zs * LANES), BF16),
            pltpu.VMEM((zs * LANES, classes), BF16),
            pltpu.VMEM((zs * LANES, classes), BF16),
            dma((4,)), dma, many, dma((8,)), many, many, many, many, dma((2,)), dma((8,)), many, many, dma, dma,
            dma((3,)), dma((5,)), dma((3,)), dma((3,)), dma((4, 2)), dma((zs, 2)), dma((zs,)), dma((zs,)), dma((4,)),
        ],
        compiler_params=pltpu.CompilerParams(
            collective_id=0, has_side_effects=True, vmem_limit_bytes=VMEM_BYTES
        ),
    )(images, references, rotations[None, :], image_group[None, :], noise_var[None, :])
    anywhere = pl.BlockSpec(memory_space=pl.ANY)
    results = (means, weight_sum, evidence)
    means, weight_sum, evidence = pl.pallas_call(
        deliver,
        name="deliver",
        out_shape=tuple(jax.ShapeDtypeStruct(a.shape, a.dtype) for a in results),
        in_specs=[anywhere] * 3,
        out_specs=(anywhere,) * 3,
        scratch_shapes=[pltpu.VMEM(a.shape, a.dtype) for a in results] + [dma((6,)), dma((6,))],
    )(*results)
    return (means, weight_sum[0], evidence[0])


def solution(mesh):
    sizes = dict(mesh.shape)
    placed = (
        P(("groups", "img"), None),
        P("img", ("groups", "ref", "rep")),
        P(("groups", "ref", "rep")),
        P(("groups", "img")),
        P(),
    )

    def choose(images, references, rotations, image_group, noise_var):
        zs = sizes["img"]
        rows = images.shape[0]
        fits = (
            sizes["ref"] == 2
            and sizes["rep"] == 2
            and rows % 32 == 0
            and rows <= LANES
            and zs == 4
            and IMAGE_SIDE == 64
            and references.shape[1] % LANES == 0
            and zs * rows * PIXELS * 4 <= 12 * 1024 * 1024
        )
        if fits:
            return turned_images_body(zs, images, references, rotations, image_group, noise_var)
        return body(images, references, rotations, image_group, noise_var)

    return jax.shard_map(
        choose,
        mesh=mesh,
        in_specs=placed,
        out_specs=(
            P("img", ("groups", "ref", "rep")),
            P(("groups", "ref", "rep")),
            P(("groups", "img")),
        ),
        check_vma=False,
    )
```

```python
import functools

import jax
import jax.numpy as jnp
from jax import lax
from jax.experimental import pallas as pl
from jax.experimental.pallas import tpu as pltpu
from jax.sharding import PartitionSpec as P

IMAGE_SIDE = 64
PIXELS = 4096
MESH = pl.DeviceIdType.MESH
F32 = jnp.float32
BF16 = jnp.bfloat16
LANES = 128
LAG = 3
GAP = 8
AHEAD = 3
VMEM_BYTES = 62 * 1024 * 1024


def joined(part, axis, combine):
    gathered = jax.tree.map(lambda a: lax.all_gather(a, axis), part)

    def take(source):
        return jax.tree.map(lambda a: lax.dynamic_index_in_dim(a, source, 0, False), gathered)

    return lax.fori_loop(
        1, lax.axis_size(axis), lambda source, state: combine(state, take(source)), take(0)
    )


def turn_forward(field, which):
    quarter = which % 4
    base = field if which < 4 else jnp.swapaxes(field, 0, 1)
    return jnp.rot90(base, quarter, axes=(0, 1))


def turn_inverse(field, which):
    quarter = which % 4
    base = jnp.rot90(field, -quarter, axes=(0, 1))
    return base if which < 4 else jnp.swapaxes(base, 0, 1)


def select_turn(field, rotations, turner):
    result = jnp.zeros_like(field)
    for which in range(8):
        result = jnp.where(rotations[None, None, :] == which, turner(field, which), result)
    return result


def combine_stats(first, second):
    top = jnp.maximum(first[0], second[0])
    total = first[1] * jnp.exp(first[0] - top) + second[1] * jnp.exp(second[0] - top)
    return (top, total)


def body(images, references, rotations, image_group, noise_var):
    gathered = lax.all_gather(references, "img", axis=0, tiled=True)
    rotated = select_turn(
        gathered.reshape(IMAGE_SIDE, IMAGE_SIDE, -1), rotations, turn_inverse
    ).reshape(PIXELS, -1)
    norms = jnp.sum(gathered * gathered, axis=0)
    group_hot = image_group[:, None] == jnp.arange(noise_var.shape[0])[None, :]
    sigma = jnp.sum(jnp.where(group_hot, noise_var[None, :], 0.0), axis=1)
    scores = (
        jnp.dot(
            images, rotated, precision=lax.Precision.HIGHEST, preferred_element_type=jnp.float32
        )
        - 0.5 * norms[None, :]
    ) / sigma[:, None]
    local_top = jnp.max(scores, axis=1)
    local_total = jnp.sum(jnp.exp(scores - local_top[:, None]), axis=1)
    top, total = joined((local_top, local_total), ("ref", "rep"), combine_stats)
    log_evidence = top + jnp.log(total)
    posterior = jnp.exp(scores - log_evidence[:, None])
    weight_sum = lax.psum(jnp.sum(posterior, axis=0), "img")
    numer_image = lax.dot_general(
        images,
        posterior,
        (((0,), (0,)), ((), ())),
        precision=lax.Precision.HIGHEST,
        preferred_element_type=jnp.float32,
    )
    numerator = select_turn(
        numer_image.reshape(IMAGE_SIDE, IMAGE_SIDE, -1), rotations, turn_forward
    ).reshape(PIXELS, -1)
    owned = lax.psum_scatter(numerator, "img", scatter_dimension=0, tiled=True)
    class_means = owned / (weight_sum + 1.0)[None, :]
    class_total = weight_sum.shape[0] * lax.axis_size("ref") * lax.axis_size("rep")
    image_total = images.shape[0] * lax.axis_size("img")
    class_weights = weight_sum * (class_total / image_total)
    return (class_means, class_weights, log_evidence)


def halves(x):
    high = x.astype(BF16)
    return high, (x - high.astype(F32)).astype(BF16)


def reverse_rows(x):
    place = lax.broadcasted_iota(jnp.int32, (8, x.shape[1]), 0)
    odd = place % 2 == 1
    second = (place // 2) % 2 == 1
    pieces = []
    for g in reversed(range(x.shape[0] // 8)):
        p = x[8 * g : 8 * g + 8]
        p = jnp.where(odd, pltpu.roll(p, 1, 0), pltpu.roll(p, 7, 0))
        p = jnp.where(second, pltpu.roll(p, 2, 0), pltpu.roll(p, 6, 0))
        pieces.append(pltpu.roll(p, 4, 0))
    return jnp.concatenate(pieces, axis=0)


def kernel(
    zs, weight_scale,
    images_ref, source_ref, rot_ref, group_ref, noise_ref,
    means_out, weights_ref, evidence_ref,
    means_ref, raw, full, wide, scores, parts, stats, posts, num, refs_ref, facs, sigmas, tall_high, tall_low, post_high, post_low,
    load_sem, refs_sem, z_recv, pair_recv, x_recv, cx_recv,
    in_send, out_send, far_send, pair_send, x_send, cx_send, g_send, g_recv,
    s_send, s_recv, t_send, t_recv, p_send, p_recv, f_send, f_recv, out_sem,
):
    z = lax.axis_index("img")
    x = lax.axis_index("ref")
    c = lax.axis_index("rep")
    rows = images_ref.shape[0]
    classes = refs_ref.shape[1]
    quarter = rows // 4
    side = IMAGE_SIDE
    band = side // zs
    apart = side + GAP
    section = PIXELS // 8
    others = [{"ref": 1 - x}, {"rep": 1 - c}, {"ref": 1 - x, "rep": 1 - c}]
    upper = jnp.where(z >= 2, 1, 0)
    middle = jnp.where((z == 1) | (z == 2), 1, 0)
    inward = 1 - 2 * upper

    def quarter_at(xi, ci):
        return pl.ds(pl.multiple_of((ci * 2 + xi) * quarter, 8), quarter)

    load_quarters = []
    for q, (xi, ci) in enumerate([(x, c), (1 - x, c), (x, 1 - c), (1 - x, 1 - c)]):
        at = quarter_at(xi, ci)
        load_quarters.append((pltpu.make_async_copy(images_ref.at[at, :], raw.at[at, :], load_sem.at[q]), at))
    for load, _ in load_quarters:
        load.start()
    load_refs = pltpu.make_async_copy(source_ref, refs_ref, refs_sem)
    load_refs.start()
    barrier = pltpu.get_barrier_semaphore()
    pl.semaphore_signal(barrier, inc=1, device_id={"img": z + inward}, device_id_type=MESH)

    @pl.when(middle == 1)
    def _():
        pl.semaphore_signal(barrier, inc=1, device_id={"img": z - inward}, device_id_type=MESH)

    for where in others:
        pl.semaphore_signal(barrier, inc=1, device_id=where, device_id_type=MESH)

    def repack(at):
        place = lax.broadcasted_iota(jnp.int32, (quarter, LANES), 1) // band
        low = place % 4
        for g in range(4):
            for v in range(4):
                start = 2 * g * section + v * LANES
                first = raw[at, start : start + LANES]
                start = (2 * g + 1) * section + v * LANES
                second = raw[at, start : start + LANES]
                first_a, first_b = pltpu.roll(first, band, 1), pltpu.roll(first, 5 * band, 1)
                second_a, second_b = pltpu.roll(second, 3 * band, 1), pltpu.roll(second, 7 * band, 1)
                outer = jnp.where(low < 2, jnp.where(low == 0, first_b, first_a), jnp.where(low == 2, second_b, second_a))
                inner = jnp.where(low < 2, second_b, first_a)
                which = (0 if g in (0, 3) else 4) + g // 2
                full[z, which, at, v * LANES : (v + 1) * LANES] = outer
                full[z, which + 2, at, v * LANES : (v + 1) * LANES] = inner

    load_quarters[0][0].wait()
    repack(load_quarters[0][1])
    pl.semaphore_wait(barrier, 4 + middle)

    def send(src, dst, ssem, rsem, where):
        return pltpu.make_async_remote_copy(
            src_ref=src, dst_ref=dst, send_sem=ssem, recv_sem=rsem,
            device_id=where, device_id_type=MESH,
        )

    def piece(src, sec):
        return full.at[src, sec, quarter_at(x, c), :]

    def go_in(src, sec):
        return send(piece(src, sec), piece(src, sec), in_send.at[src, sec], z_recv.at[src, sec], {"img": z + inward})

    def go_out(src, sec):
        return send(piece(src, sec), piece(src, sec), out_send.at[src, sec], z_recv.at[src, sec], {"img": z - inward})

    def go_far(sec):
        target = jnp.where(upper == 1, 0, zs - 1)
        return send(piece(z, sec), piece(z, sec), far_send.at[sec], z_recv.at[z, sec], {"img": target})

    def go_x(src, sec):
        return send(piece(src, sec), piece(src, sec), x_send.at[src, sec], x_recv.at[src, sec], {"ref": 1 - x})

    def go_cx(src, sec):
        pair = full.at[src, sec, pl.ds(pl.multiple_of(c * 2 * quarter, 8), 2 * quarter), :]
        return send(pair, pair, cx_send.at[src, sec], cx_recv.at[src, sec], {"rep": 1 - c})

    def go_pair(src, sec):
        rest = full.at[src, sec, quarter_at(1 - x, c), :]
        return send(rest, rest, pair_send.at[sec], pair_recv.at[sec], {"img": z + inward})

    def partial_in(src, number, slot):
        return send(scores.at[src], parts.at[slot], s_send.at[number], s_recv.at[slot], {"img": z + inward})

    def partial_out(src, number):
        return send(scores.at[src], parts.at[0], s_send.at[number], s_recv.at[0], {"img": z - inward})

    give_sigma = send(sigmas.at[0], sigmas.at[1], g_send, g_recv, {"img": zs - 1 - z})

    is_end = middle == 0
    is_middle = middle == 1
    near, across_z, far = z - inward, z + inward, z + 2 * inward

    def end_send(i):
        @pl.when(i < 6)
        def _():
            go_in(z, i + 2).start()

        @pl.when((i >= 6) & (i < 12))
        def _():
            go_pair(z, i - 4).start()

        @pl.when((i >= 12) & (i < 14))
        def _():
            go_far(i - 12).start()

    def middle_send(i):
        @pl.when(i < 6)
        def _():
            go_in(z, i + 2).start()
            go_out(z, lax.rem(i + 2, 6)).start()

        @pl.when((i >= 6) & (i < 10))
        def _():
            go_in(near, i - 4).start()
            go_out(across_z, i - 4).start()

        @pl.when((i >= 10) & (i < 12))
        def _():
            go_far(i - 10).start()

        @pl.when((i >= 12) & (i < 14))
        def _():
            go_in(near, i - 6).start()

    @pl.when(is_end)
    def _():
        for i in range(AHEAD):
            end_send(i)

    @pl.when(is_middle)
    def _():
        for i in range(AHEAD):
            middle_send(i)

    rot = rot_ref[...]
    is_row = (rot == 0) | (rot == 7)
    is_row_up = (rot == 5) | (rot == 2)
    is_col = (rot == 4) | (rot == 3)
    is_col_up = (rot == 1) | (rot == 6)
    flipped = (rot == 7) | (rot == 2) | (rot == 3) | (rot == 6)

    def lane(h):
        return slice(h * LANES, (h + 1) * LANES)

    def line(i):
        return pl.ds(pl.multiple_of(i * side, side), side)

    def row_at(b, i, which, stride):
        block = 8 * stride
        base = jnp.where(b >= 2, block, 0) + stride * lax.rem(i, 8)
        if which in (0, 3):
            place = base + 2 * block * middle + 2 * band * (i // 8) + (band if which == 0 else 0)
        else:
            place = base + 2 * block * (middle + 1) + 2 * band * (1 - i // 8) + (band if which == 2 else 0)
        return pl.ds(pl.multiple_of(place, 8), band)

    def column_at(b, i, g, half, stride):
        block = 8 * stride
        base = (0 if g in (0, 3) else 4 * block) + (block if g >= 2 else 0)
        swapped = half + middle * (1 - 2 * half)
        place = base + 2 * band * swapped + band * (1 - lax.rem(b, 2)) + i
        return pl.ds(place, 8, stride=stride)

    def turned(i):
        field = refs_ref[line(i), :]
        return jnp.where(flipped, reverse_rows(field), field)

    def put_rows(i, norm):
        raw_field = refs_ref[line(i), :]
        field = turned(i)
        up = jnp.where(is_row, field, 0.0)
        down = jnp.where(is_row_up, field, 0.0)
        for h in range(classes // LANES):
            for which in range(4):
                part = slice(which * band, (which + 1) * band)
                wide[h, row_at(z, i, which, apart), :] = up[part, lane(h)]
                wide[h, row_at(zs - 1 - z, band - 1 - i, which, apart), :] = down[part, lane(h)]
        return norm + jnp.sum(raw_field * raw_field, axis=0, keepdims=True)

    def put_columns(i, _):
        field = turned(i)
        across = jnp.where(is_col, field, 0.0)
        back = jnp.where(is_col_up, field, 0.0)

        def put(added):
            for h in range(classes // LANES):
                for g in range(4):
                    for half in range(2):
                        part = slice(g * band + half * 8, g * band + half * 8 + 8)
                        for at, value in (
                            (column_at(z, i, g, half, apart), across[part, lane(h)]),
                            (column_at(zs - 1 - z, band - 1 - i, g, half, apart), back[part, lane(h)]),
                        ):
                            if g in added:
                                wide[h, at, :] = wide[h, at, :] + value
                            else:
                                wide[h, at, :] = value

        @pl.when(is_end)
        def _():
            put((0, 3))

        @pl.when(is_middle)
        def _():
            put((1, 2))

        return 0

    def section_at(sec):
        return pl.ds(pl.multiple_of((sec - 2 * middle) * section, section), section)

    def multiply(src, sec):
        first = (sec - 2 * middle) * 8 * apart
        pieces = [pl.ds(pl.multiple_of(first + k * apart, 8), side) for k in range(section // side)]
        weight = jnp.concatenate(
            [jnp.concatenate([wide[h, at, :] for at in pieces], axis=0) for h in range(classes // LANES)], axis=1
        )
        return jnp.dot(full[src, sec], weight, precision=lax.Precision.HIGHEST, preferred_element_type=F32)

    def keep(src, sec):
        block = full[src, sec]
        if rows < LANES:
            block = jnp.concatenate([block, jnp.zeros((LANES - rows, section), F32)], axis=0)
        high, low = halves(block.T)
        slot = jnp.where(src == 0, 2, jnp.where(src == zs - 1, zs - 1, src - 1))
        at = pl.ds(pl.multiple_of(slot * LANES, LANES), LANES)
        tall_high[section_at(sec), at] = high
        tall_low[section_at(sec), at] = low

    for src in range(zs):
        post_high[src * LANES + rows : (src + 1) * LANES, :] = jnp.zeros((LANES - rows, classes), BF16)
        post_low[src * LANES + rows : (src + 1) * LANES, :] = jnp.zeros((LANES - rows, classes), BF16)

    groups = group_ref[...]
    sigma_row = jnp.ones(groups.shape, F32)
    for g in range(noise_ref.shape[1]):
        sigma_row = jnp.where(groups == g, noise_ref[0:1, g : g + 1], sigma_row)
    if rows < LANES:
        sigma_row = jnp.concatenate([sigma_row, jnp.ones((1, LANES - rows), F32)], axis=1)
    sigmas[0] = jnp.broadcast_to(sigma_row, (8, LANES))

    load_quarters[1][0].wait()
    repack(load_quarters[1][1])

    for load, at in load_quarters[2:]:
        load.wait()
        repack(at)
    load_refs.wait()
    norm = lax.fori_loop(0, band, put_rows, jnp.zeros((1, classes), F32))
    start = jnp.broadcast_to(-0.5 * norm, (rows, classes))
    for src in range(zs):
        scores[src] = start

    units = 6 * (zs - 1)

    def chunk(n):
        return z + inward * (n // 6 + 1), lax.rem(n + 2, 6)

    def end_unit(n):
        @pl.when(n < units)
        def _():
            src, sec = chunk(n)
            go_in(src, sec).wait_recv()
            go_x(src, sec).start()
            end_send(n + AHEAD)

        @pl.when((n >= LAG) & (n < units + LAG))
        def _():
            src, sec = chunk(n - LAG)
            go_x(src, sec).wait_recv()
            go_cx(src, sec).start()

    def pass_x(src, sec):
        go_in(src, sec).wait_recv()
        go_x(src, sec).start()

    def take_x(src, sec):
        go_x(src, sec).wait_recv()
        go_cx(src, sec).start()

    def middle_unit(n):
        @pl.when(n < 6)
        def _():
            pass_x(across_z, n + 2)
            go_in(near, n + 2).wait_recv()

        middle_send(n + AHEAD)

        @pl.when((n >= 6) & (n < 10))
        def _():
            pass_x(far, n - 4)
            go_out(far, n - 4).start()

        @pl.when((n >= 12) & (n < 14))
        def _():
            pass_x(far, n - 6)

        @pl.when((n >= 6) & (n < 12))
        def _():
            go_pair(near, n - 4).wait_recv()
            go_cx(near, n - 4).start()

        @pl.when((n >= LAG) & (n < LAG + 6))
        def _():
            take_x(across_z, n - LAG + 2)

        @pl.when((n >= LAG + 6) & (n < LAG + 10))
        def _():
            take_x(far, n - LAG - 4)

        @pl.when((n >= LAG + 12) & (n < LAG + 14))
        def _():
            take_x(far, n - LAG - 6)

    def take_item(item):
        other = jnp.maximum(item - 6, 0)
        end_src, end_sec = chunk(other)
        middle_src = jnp.where(other < 6, across_z, jnp.where(other < 12, near, far))
        own = item < 6
        src = jnp.where(own, z, jnp.where(is_end, end_src, middle_src))
        sec = jnp.where(own, 2 * middle + item, jnp.where(is_end, end_sec, 2 + lax.rem(other, 6)))

        @pl.when(item >= 6)
        def _():
            go_cx(src, sec).wait_recv()

        scores[src] = scores[src] + multiply(src, sec)
        keep(src, sec)

    def arrived(slot):
        partial_in(z, 0, slot).wait_recv()
        return parts[slot]

    def end_sums(n):
        for when, src, number in ((6, z, 0), (9, z + inward, 1), (15, z + 2 * inward, 2)):
            @pl.when(n == when)
            def _():
                partial_in(src, number, number).start()

    def middle_sums(n):
        @pl.when(n == 12)
        def _():
            scores[near] = scores[near] + arrived(0)
            partial_in(near, 0, 4).start()
            scores[z] = scores[z] + arrived(1)
            partial_in(z, 1, 3).start()

        @pl.when(n == 17)
        def _():
            scores[far] = scores[far] + arrived(4)
            partial_out(far, 2).start()

    def unit(n, _):
        @pl.when(is_end)
        def _():
            end_unit(n)

        @pl.when(is_middle)
        def _():
            middle_unit(n)

        @pl.when(n < 4)
        def _():
            lax.fori_loop(n * band // 4, (n + 1) * band // 4, put_columns, 0)

        @pl.when(n >= 4)
        def _():
            end_first = jnp.where(n < 10, 2 * (n - 4), n + 2)
            end_count = jnp.where(n < 10, 2, 1)
            middle_first = jnp.where(n < 15, 2 * (n - 4), 22)
            middle_count = jnp.where((n < 15) | (n == 17), 2, 0)
            first = jnp.where(is_end, end_first, middle_first)
            count = jnp.where(is_end, end_count, middle_count)

            def run(item, _):
                take_item(item)
                return 0

            lax.fori_loop(first, first + count, run, 0)

        @pl.when(n == 8)
        def _():
            give_sigma.start()

        @pl.when(is_end)
        def _():
            end_sums(n)

        @pl.when(is_middle)
        def _():
            middle_sums(n)

        return 0

    lax.fori_loop(0, units + LAG + 1, unit, 0)

    owned = zs - 1 - z

    @pl.when(is_end)
    def _():
        scores[owned] = scores[owned] + arrived(0)

    @pl.when(is_middle)
    def _():
        scores[owned] = scores[owned] + arrived(2) + arrived(3)

    def upright(row):
        return jnp.broadcast_to(row, (LANES, row.shape[1])).T[:rows, 0:1]

    give_sigma.wait_recv()
    total_score = scores[owned] / upright(sigmas[1, 0:1, :])
    top = jnp.max(total_score, axis=1, keepdims=True)
    shifted = jnp.exp(total_score - top)
    posts[owned] = shifted
    half_rows = rows // 2

    def give(src, half, where, ssem):
        part = posts.at[src, half * half_rows : (half + 1) * half_rows, :]
        return send(part, part, ssem, p_recv.at[src, half], {"img": where})

    def give_in(half):
        return give(owned, half, z + inward, p_send.at[0, half])

    def give_far(half):
        return give(owned, half, jnp.where(is_end, owned, z + 2 * inward), p_send.at[1, half])

    def give_out(half):
        return give(owned, half, z - inward, p_send.at[2, half])

    def pass_on(half):
        return give(far, half, z + inward, p_send.at[3, half])

    def give_factor(d):
        where = {"img": lax.rem(z + d, zs)}
        return send(facs.at[owned], facs.at[owned], f_send.at[d], f_recv.at[owned], where)

    def take_posts(src):
        @pl.when(is_end | (src != far))
        def _():
            for half in range(2):
                give(src, half, 0, p_send.at[0, half]).wait_recv()

        send(facs.at[src], facs.at[src], f_send.at[0], f_recv.at[src], {"img": owned}).wait_recv()

    for half in range(2):
        give_in(half).start()

    @pl.when(is_middle)
    def _():
        for half in range(2):
            give_out(half).start()

    total = jnp.sum(shifted, axis=1, keepdims=True)
    place = lax.broadcasted_iota(jnp.int32, (rows, LANES), 1)
    pair = jnp.where(place < LANES // 2, top, total)
    if rows < LANES:
        pair = jnp.concatenate([pair, jnp.ones((LANES - rows, LANES), F32)], axis=0)
    pair = pair.T
    tops, totals = pair[0:8], pair[LANES // 2 : LANES // 2 + 8]
    stats[3, 0:8, :] = tops
    stats[3, 8:16, :] = totals
    shares = [send(stats.at[3], stats.at[m], t_send.at[m], t_recv.at[m], where) for m, where in enumerate(others)]
    for share in shares:
        share.start()
    for half in range(2):
        give_far(half).start()
    for share in shares:
        share.wait()
    best = tops
    for m in range(3):
        best = jnp.maximum(best, stats[m, 0:8, :])
    summed = totals * jnp.exp(tops - best)
    for m in range(3):
        summed = summed + stats[m, 8:16, :] * jnp.exp(stats[m, 0:8, :] - best)
    evidence = best + jnp.log(summed)
    facs[owned, 0:8, :] = jnp.exp(tops - evidence)
    facs[owned, 8:16, :] = evidence
    for d in (3, 2, 1):
        give_factor(d).start()

    def settle_posts(src, slot, weight_sum):
        @pl.when(z != zs - 1 - src)
        def _():
            take_posts(src)

        factor = upright(facs[src, 0:1, :])
        post = posts[src] * factor
        high, low = halves(post)
        post_high[slot * LANES : slot * LANES + rows, :] = high
        post_low[slot * LANES : slot * LANES + rows, :] = low
        return weight_sum + jnp.sum(post, axis=0, keepdims=True)

    def weigh(half, add):
        part = slice(half * 2 * LANES, (half + 1) * 2 * LANES)

        def step(n, _):
            at = pl.ds(pl.multiple_of(2 * n * section, 2 * section), 2 * section)
            ah, al, bh, bl = tall_high[at, part], tall_low[at, part], post_high[part, :], post_low[part, :]
            one = lambda p, q: jnp.dot(p, q, preferred_element_type=F32)
            result = one(ah, bh) + (one(ah, bl) + one(al, bh))
            for k in range(2 * section // side):
                at = pl.ds(pl.multiple_of(2 * n * 8 * apart + k * apart, 8), side)
                for h in range(classes // LANES):
                    value = result[k * side : (k + 1) * side, lane(h)]
                    num[h, at, :] = num[h, at, :] + value if add else value
            return 0

        lax.fori_loop(0, 3, step, 0)

    weight_sum = settle_posts(1, 0, jnp.zeros((1, classes), F32))
    weight_sum = settle_posts(2, 1, weight_sum)
    weigh(0, False)

    @pl.when(is_middle)
    def _():
        for half in range(2):
            give(far, half, 0, p_send.at[0, half]).wait_recv()
            pass_on(half).start()

    weight_sum = settle_posts(0, 2, weight_sum)
    weight_sum = settle_posts(3, 3, weight_sum)
    weigh(1, True)
    weights_ref[...] = weight_sum * weight_scale
    evidence_ref[...] = facs[z, 8:9, :rows]
    scale = 1.0 / (weight_sum + 1.0)

    def finish(i, _):
        fields = []
        for h in range(classes // LANES):
            pull_row = lambda b, j: jnp.concatenate([num[h, row_at(b, j, which, apart), :] for which in range(4)], axis=0)
            pull_column = lambda b, j: jnp.concatenate(
                [num[h, column_at(b, j, g, half, apart), :] for g in range(4) for half in range(2)], axis=0
            )
            up = pull_row(z, i)
            down = pull_row(zs - 1 - z, band - 1 - i)
            across = pull_column(z, i)
            back = pull_column(zs - 1 - z, band - 1 - i)
            k = lane(h)
            fields.append(jnp.where(is_row[:, k], up, jnp.where(is_row_up[:, k], down, jnp.where(is_col[:, k], across, back))))
        field = jnp.concatenate(fields, axis=1)
        means_ref[line(i), :] = jnp.where(flipped, reverse_rows(field), field) * scale
        return 0

    step = band // 4

    def store(k):
        at = pl.ds(pl.multiple_of(k * step * side, step * side), step * side)
        return pltpu.make_async_copy(means_ref.at[at, :], means_out.at[at, :], out_sem.at[k])

    for k in range(4):
        lax.fori_loop(k * step, (k + 1) * step, finish, 0, unroll=2)
        store(k).start()

    @pl.when(is_end)
    def _():
        def settle(n, _):
            src, sec = chunk(n)
            go_x(src, sec).wait_send()
            go_cx(src, sec).wait_send()

            @pl.when(n < 6)
            def _():
                go_in(z, n + 2).wait_send()
                go_pair(z, n + 2).wait_send()

            return 0

        lax.fori_loop(0, units, settle, 0)

    @pl.when(is_middle)
    def _():
        def settle(n, _):
            go_in(z, n + 2).wait_send()
            go_out(z, n).wait_send()
            go_in(near, n + 2).wait_send()
            go_cx(near, n + 2).wait_send()
            for src in (across_z, far):
                @pl.when(n < 4)
                def _():
                    go_out(src, n + 2).wait_send()

                go_x(src, n + 2).wait_send()
                go_cx(src, n + 2).wait_send()

            return 0

        lax.fori_loop(0, 6, settle, 0)

    go_far(0).wait_send()
    go_far(1).wait_send()
    for k in range(4):
        store(k).wait()
    give_sigma.wait_send()
    for number in range(3):
        partial_in(z, number, 0).wait_send()
    for d in (1, 2, 3):
        give_factor(d).wait_send()
    for half in range(2):
        give_in(half).wait_send()
        give_far(half).wait_send()

        @pl.when(is_middle)
        def _():
            give_out(half).wait_send()
            pass_on(half).wait_send()


def deliver(means, weights, evidence, means_out, weights_out, evidence_out, held, held_weights, held_evidence, in_sem, out_sem):
    parts = in_sem.shape[0] - 2
    step = means.shape[0] // parts
    pieces = [(means.at[pl.ds(k * step, step)], held.at[pl.ds(k * step, step)], means_out.at[pl.ds(k * step, step)]) for k in range(parts)]
    pieces += [(weights, held_weights, weights_out), (evidence, held_evidence, evidence_out)]
    loads = [pltpu.make_async_copy(a, b, in_sem.at[k]) for k, (a, b, _) in enumerate(pieces)]
    stores = [pltpu.make_async_copy(b, d, out_sem.at[k]) for k, (_, b, d) in enumerate(pieces)]
    for load in loads:
        load.start()
    for load, store in zip(loads, stores):
        load.wait()
        store.start()
    for store in stores:
        store.wait()


def turned_images_body(zs, images, references, rotations, image_group, noise_var):
    rows = images.shape[0]
    pixels, classes = references.shape
    class_total = classes * lax.axis_size("ref") * lax.axis_size("rep")
    image_total = rows * zs
    dma = pltpu.SemaphoreType.DMA
    vmem = pl.BlockSpec(memory_space=pltpu.VMEM)
    many = dma((zs, 8))
    section = PIXELS // 8
    means, weight_sum, evidence = pl.pallas_call(
        functools.partial(kernel, zs, class_total / image_total),
        name="class_step",
        out_shape=(
            jax.ShapeDtypeStruct((pixels, classes), F32),
            jax.ShapeDtypeStruct((1, classes), F32),
            jax.ShapeDtypeStruct((1, rows), F32),
        ),
        in_specs=[pl.BlockSpec(memory_space=pl.ANY), pl.BlockSpec(memory_space=pl.ANY), vmem, vmem, vmem],
        out_specs=(pl.BlockSpec(memory_space=pl.ANY), vmem, vmem),
        scratch_shapes=[
            pltpu.VMEM((pixels, classes), F32),
            pltpu.VMEM((rows, PIXELS), F32),
            pltpu.VMEM((zs, 8, rows, section), F32),
            pltpu.VMEM((classes // LANES, 6 * 8 * (IMAGE_SIDE + GAP), LANES), F32),
            pltpu.VMEM((zs, rows, classes), F32),
            pltpu.VMEM((5, rows, classes), F32),
            pltpu.VMEM((4, 16, LANES), F32),
            pltpu.VMEM((zs, rows, classes), F32),
            pltpu.VMEM((classes // LANES, 6 * 8 * (IMAGE_SIDE + GAP), LANES), F32),
            pltpu.VMEM((pixels, classes), F32),
            pltpu.VMEM((zs, 16, LANES), F32),
            pltpu.VMEM((2, 8, LANES), F32),
            pltpu.VMEM((6 * section, zs * LANES), BF16),
            pltpu.VMEM((6 * section, zs * LANES), BF16),
            pltpu.VMEM((zs * LANES, classes), BF16),
            pltpu.VMEM((zs * LANES, classes), BF16),
            dma((4,)), dma, many, dma((8,)), many, many, many, many, dma((2,)), dma((8,)), many, many, dma, dma,
            dma((3,)), dma((5,)), dma((3,)), dma((3,)), dma((4, 2)), dma((zs, 2)), dma((zs,)), dma((zs,)), dma((4,)),
        ],
        compiler_params=pltpu.CompilerParams(
            collective_id=0, has_side_effects=True, vmem_limit_bytes=VMEM_BYTES
        ),
    )(images, references, rotations[None, :], image_group[None, :], noise_var[None, :])
    anywhere = pl.BlockSpec(memory_space=pl.ANY)
    results = (means, weight_sum, evidence)
    means, weight_sum, evidence = pl.pallas_call(
        deliver,
        name="deliver",
        out_shape=tuple(jax.ShapeDtypeStruct(a.shape, a.dtype) for a in results),
        in_specs=[anywhere] * 3,
        out_specs=(anywhere,) * 3,
        scratch_shapes=[pltpu.VMEM(a.shape, a.dtype) for a in results] + [dma((6,)), dma((6,))],
    )(*results)
    return (means, weight_sum[0], evidence[0])


def solution(mesh):
    sizes = dict(mesh.shape)
    placed = (
        P(("groups", "img"), None),
        P("img", ("groups", "ref", "rep")),
        P(("groups", "ref", "rep")),
        P(("groups", "img")),
        P(),
    )

    def choose(images, references, rotations, image_group, noise_var):
        zs = sizes["img"]
        rows = images.shape[0]
        fits = (
            sizes["ref"] == 2
            and sizes["rep"] == 2
            and rows % 32 == 0
            and rows <= LANES
            and zs == 4
            and IMAGE_SIDE == 64
            and references.shape[1] % LANES == 0
            and zs * rows * PIXELS * 4 <= 12 * 1024 * 1024
        )
        if fits:
            return turned_images_body(zs, images, references, rotations, image_group, noise_var)
        return body(images, references, rotations, image_group, noise_var)

    return jax.shard_map(
        choose,
        mesh=mesh,
        in_specs=placed,
        out_specs=(
            P("img", ("groups", "ref", "rep")),
            P(("groups", "ref", "rep")),
            P(("groups", "img")),
        ),
        check_vma=False,
    )
```

```python
import functools

import jax
import jax.numpy as jnp
from jax import lax
from jax.experimental import pallas as pl
from jax.experimental.pallas import tpu as pltpu
from jax.sharding import PartitionSpec as P

IMAGE_SIDE = 64
PIXELS = 4096
MESH = pl.DeviceIdType.MESH
F32 = jnp.float32
BF16 = jnp.bfloat16
LANES = 128
LAG = 3
GAP = 8
AHEAD = 3
VMEM_BYTES = 62 * 1024 * 1024


def joined(part, axis, combine):
    gathered = jax.tree.map(lambda a: lax.all_gather(a, axis), part)

    def take(source):
        return jax.tree.map(lambda a: lax.dynamic_index_in_dim(a, source, 0, False), gathered)

    return lax.fori_loop(
        1, lax.axis_size(axis), lambda source, state: combine(state, take(source)), take(0)
    )


def turn_forward(field, which):
    quarter = which % 4
    base = field if which < 4 else jnp.swapaxes(field, 0, 1)
    return jnp.rot90(base, quarter, axes=(0, 1))


def turn_inverse(field, which):
    quarter = which % 4
    base = jnp.rot90(field, -quarter, axes=(0, 1))
    return base if which < 4 else jnp.swapaxes(base, 0, 1)


def select_turn(field, rotations, turner):
    result = jnp.zeros_like(field)
    for which in range(8):
        result = jnp.where(rotations[None, None, :] == which, turner(field, which), result)
    return result


def combine_stats(first, second):
    top = jnp.maximum(first[0], second[0])
    total = first[1] * jnp.exp(first[0] - top) + second[1] * jnp.exp(second[0] - top)
    return (top, total)


def body(images, references, rotations, image_group, noise_var):
    gathered = lax.all_gather(references, "img", axis=0, tiled=True)
    rotated = select_turn(
        gathered.reshape(IMAGE_SIDE, IMAGE_SIDE, -1), rotations, turn_inverse
    ).reshape(PIXELS, -1)
    norms = jnp.sum(gathered * gathered, axis=0)
    group_hot = image_group[:, None] == jnp.arange(noise_var.shape[0])[None, :]
    sigma = jnp.sum(jnp.where(group_hot, noise_var[None, :], 0.0), axis=1)
    scores = (
        jnp.dot(
            images, rotated, precision=lax.Precision.HIGHEST, preferred_element_type=jnp.float32
        )
        - 0.5 * norms[None, :]
    ) / sigma[:, None]
    local_top = jnp.max(scores, axis=1)
    local_total = jnp.sum(jnp.exp(scores - local_top[:, None]), axis=1)
    top, total = joined((local_top, local_total), ("ref", "rep"), combine_stats)
    log_evidence = top + jnp.log(total)
    posterior = jnp.exp(scores - log_evidence[:, None])
    weight_sum = lax.psum(jnp.sum(posterior, axis=0), "img")
    numer_image = lax.dot_general(
        images,
        posterior,
        (((0,), (0,)), ((), ())),
        precision=lax.Precision.HIGHEST,
        preferred_element_type=jnp.float32,
    )
    numerator = select_turn(
        numer_image.reshape(IMAGE_SIDE, IMAGE_SIDE, -1), rotations, turn_forward
    ).reshape(PIXELS, -1)
    owned = lax.psum_scatter(numerator, "img", scatter_dimension=0, tiled=True)
    class_means = owned / (weight_sum + 1.0)[None, :]
    class_total = weight_sum.shape[0] * lax.axis_size("ref") * lax.axis_size("rep")
    image_total = images.shape[0] * lax.axis_size("img")
    class_weights = weight_sum * (class_total / image_total)
    return (class_means, class_weights, log_evidence)


def halves(x):
    high = x.astype(BF16)
    return high, (x - high.astype(F32)).astype(BF16)


def reverse_rows(x):
    place = lax.broadcasted_iota(jnp.int32, (8, x.shape[1]), 0)
    odd = place % 2 == 1
    second = (place // 2) % 2 == 1
    pieces = []
    for g in reversed(range(x.shape[0] // 8)):
        p = x[8 * g : 8 * g + 8]
        p = jnp.where(odd, pltpu.roll(p, 1, 0), pltpu.roll(p, 7, 0))
        p = jnp.where(second, pltpu.roll(p, 2, 0), pltpu.roll(p, 6, 0))
        pieces.append(pltpu.roll(p, 4, 0))
    return jnp.concatenate(pieces, axis=0)


def kernel(
    zs, weight_scale,
    images_ref, source_ref, rot_ref, group_ref, noise_ref,
    means_out, weights_ref, evidence_ref,
    means_ref, raw, full, wide, scores, parts, stats, posts, num, refs_ref, facs, sigmas, tall_high, tall_low, post_high, post_low,
    load_sem, refs_sem, z_recv, pair_recv, x_recv, cx_recv,
    in_send, out_send, far_send, pair_send, x_send, cx_send, g_send, g_recv,
    s_send, s_recv, t_send, t_recv, p_send, p_recv, f_send, f_recv, out_sem,
):
    z = lax.axis_index("img")
    x = lax.axis_index("ref")
    c = lax.axis_index("rep")
    rows = images_ref.shape[0]
    classes = refs_ref.shape[1]
    quarter = rows // 4
    side = IMAGE_SIDE
    band = side // zs
    apart = side + GAP
    section = PIXELS // 8
    others = [{"ref": 1 - x}, {"rep": 1 - c}, {"ref": 1 - x, "rep": 1 - c}]
    upper = jnp.where(z >= 2, 1, 0)
    middle = jnp.where((z == 1) | (z == 2), 1, 0)
    inward = 1 - 2 * upper

    def quarter_at(xi, ci):
        return pl.ds(pl.multiple_of((ci * 2 + xi) * quarter, 8), quarter)

    load_quarters = []
    for q, (xi, ci) in enumerate([(x, c), (1 - x, c), (x, 1 - c), (1 - x, 1 - c)]):
        at = quarter_at(xi, ci)
        load_quarters.append((pltpu.make_async_copy(images_ref.at[at, :], raw.at[at, :], load_sem.at[q]), at))
    for load, _ in load_quarters:
        load.start()
    load_refs = pltpu.make_async_copy(source_ref, refs_ref, refs_sem)
    load_refs.start()
    barrier = pltpu.get_barrier_semaphore()
    pl.semaphore_signal(barrier, inc=1, device_id={"img": z + inward}, device_id_type=MESH)

    @pl.when(middle == 1)
    def _():
        pl.semaphore_signal(barrier, inc=1, device_id={"img": z - inward}, device_id_type=MESH)

    for where in others:
        pl.semaphore_signal(barrier, inc=1, device_id=where, device_id_type=MESH)

    def repack(at):
        place = lax.broadcasted_iota(jnp.int32, (quarter, LANES), 1) // band
        low = place % 4
        for g in range(4):
            for v in range(4):
                start = 2 * g * section + v * LANES
                first = raw[at, start : start + LANES]
                start = (2 * g + 1) * section + v * LANES
                second = raw[at, start : start + LANES]
                first_a, first_b = pltpu.roll(first, band, 1), pltpu.roll(first, 5 * band, 1)
                second_a, second_b = pltpu.roll(second, 3 * band, 1), pltpu.roll(second, 7 * band, 1)
                outer = jnp.where(low < 2, jnp.where(low == 0, first_b, first_a), jnp.where(low == 2, second_b, second_a))
                inner = jnp.where(low < 2, second_b, first_a)
                which = (0 if g in (0, 3) else 4) + g // 2
                full[z, which, at, v * LANES : (v + 1) * LANES] = outer
                full[z, which + 2, at, v * LANES : (v + 1) * LANES] = inner

    load_quarters[0][0].wait()
    repack(load_quarters[0][1])
    pl.semaphore_wait(barrier, 4 + middle)

    def send(src, dst, ssem, rsem, where):
        return pltpu.make_async_remote_copy(
            src_ref=src, dst_ref=dst, send_sem=ssem, recv_sem=rsem,
            device_id=where, device_id_type=MESH,
        )

    def piece(src, sec):
        return full.at[src, sec, quarter_at(x, c), :]

    def go_in(src, sec):
        return send(piece(src, sec), piece(src, sec), in_send.at[src, sec], z_recv.at[src, sec], {"img": z + inward})

    def go_out(src, sec):
        return send(piece(src, sec), piece(src, sec), out_send.at[src, sec], z_recv.at[src, sec], {"img": z - inward})

    def go_far(sec):
        target = jnp.where(upper == 1, 0, zs - 1)
        return send(piece(z, sec), piece(z, sec), far_send.at[sec], z_recv.at[z, sec], {"img": target})

    def go_x(src, sec):
        return send(piece(src, sec), piece(src, sec), x_send.at[src, sec], x_recv.at[src, sec], {"ref": 1 - x})

    def go_cx(src, sec):
        pair = full.at[src, sec, pl.ds(pl.multiple_of(c * 2 * quarter, 8), 2 * quarter), :]
        return send(pair, pair, cx_send.at[src, sec], cx_recv.at[src, sec], {"rep": 1 - c})

    def go_pair(src, sec):
        rest = full.at[src, sec, quarter_at(1 - x, c), :]
        return send(rest, rest, pair_send.at[sec], pair_recv.at[sec], {"img": z + inward})

    def partial_in(src, number, slot):
        return send(scores.at[src], parts.at[slot], s_send.at[number], s_recv.at[slot], {"img": z + inward})

    def partial_out(src, number):
        return send(scores.at[src], parts.at[0], s_send.at[number], s_recv.at[0], {"img": z - inward})

    give_sigma = send(sigmas.at[0], sigmas.at[1], g_send, g_recv, {"img": zs - 1 - z})

    is_end = middle == 0
    is_middle = middle == 1
    near, across_z, far = z - inward, z + inward, z + 2 * inward

    def end_send(i):
        @pl.when(i < 6)
        def _():
            go_in(z, i + 2).start()

        @pl.when((i >= 6) & (i < 12))
        def _():
            go_pair(z, i - 4).start()

        @pl.when((i >= 12) & (i < 14))
        def _():
            go_far(i - 12).start()

    def middle_send(i):
        @pl.when(i < 6)
        def _():
            go_in(z, i + 2).start()
            go_out(z, lax.rem(i + 2, 6)).start()

        @pl.when((i >= 6) & (i < 10))
        def _():
            go_in(near, i - 4).start()
            go_out(across_z, i - 4).start()

        @pl.when((i >= 10) & (i < 12))
        def _():
            go_far(i - 10).start()

        @pl.when((i >= 12) & (i < 14))
        def _():
            go_in(near, i - 6).start()

    @pl.when(is_end)
    def _():
        for i in range(AHEAD):
            end_send(i)

    @pl.when(is_middle)
    def _():
        for i in range(AHEAD):
            middle_send(i)

    rot = rot_ref[...]
    is_row = (rot == 0) | (rot == 7)
    is_row_up = (rot == 5) | (rot == 2)
    is_col = (rot == 4) | (rot == 3)
    is_col_up = (rot == 1) | (rot == 6)
    flipped = (rot == 7) | (rot == 2) | (rot == 3) | (rot == 6)

    def lane(h):
        return slice(h * LANES, (h + 1) * LANES)

    def line(i):
        return pl.ds(pl.multiple_of(i * side, side), side)

    def row_at(b, i, which, stride):
        block = 8 * stride
        base = jnp.where(b >= 2, block, 0) + stride * lax.rem(i, 8)
        if which in (0, 3):
            place = base + 2 * block * middle + 2 * band * (i // 8) + (band if which == 0 else 0)
        else:
            place = base + 2 * block * (middle + 1) + 2 * band * (1 - i // 8) + (band if which == 2 else 0)
        return pl.ds(pl.multiple_of(place, 8), band)

    def column_at(b, i, g, half, stride):
        block = 8 * stride
        base = (0 if g in (0, 3) else 4 * block) + (block if g >= 2 else 0)
        swapped = half + middle * (1 - 2 * half)
        place = base + 2 * band * swapped + band * (1 - lax.rem(b, 2)) + i
        return pl.ds(place, 8, stride=stride)

    def turned(i):
        field = refs_ref[line(i), :]
        return jnp.where(flipped, reverse_rows(field), field)

    def put_rows(i, norm):
        raw_field = refs_ref[line(i), :]
        field = turned(i)
        up = jnp.where(is_row, field, 0.0)
        down = jnp.where(is_row_up, field, 0.0)
        for h in range(classes // LANES):
            for which in range(4):
                part = slice(which * band, (which + 1) * band)
                wide[h, row_at(z, i, which, apart), :] = up[part, lane(h)]
                wide[h, row_at(zs - 1 - z, band - 1 - i, which, apart), :] = down[part, lane(h)]
        return norm + jnp.sum(raw_field * raw_field, axis=0, keepdims=True)

    def put_columns(i, _):
        field = turned(i)
        across = jnp.where(is_col, field, 0.0)
        back = jnp.where(is_col_up, field, 0.0)

        def put(added):
            for h in range(classes // LANES):
                for g in range(4):
                    for half in range(2):
                        part = slice(g * band + half * 8, g * band + half * 8 + 8)
                        for at, value in (
                            (column_at(z, i, g, half, apart), across[part, lane(h)]),
                            (column_at(zs - 1 - z, band - 1 - i, g, half, apart), back[part, lane(h)]),
                        ):
                            if g in added:
                                wide[h, at, :] = wide[h, at, :] + value
                            else:
                                wide[h, at, :] = value

        @pl.when(is_end)
        def _():
            put((0, 3))

        @pl.when(is_middle)
        def _():
            put((1, 2))

        return 0

    def section_at(sec):
        return pl.ds(pl.multiple_of((sec - 2 * middle) * section, section), section)

    def multiply(src, sec):
        first = (sec - 2 * middle) * 8 * apart
        pieces = [pl.ds(pl.multiple_of(first + k * apart, 8), side) for k in range(section // side)]
        weight = jnp.concatenate(
            [jnp.concatenate([wide[h, at, :] for at in pieces], axis=0) for h in range(classes // LANES)], axis=1
        )
        return jnp.dot(full[src, sec], weight, precision=lax.Precision.HIGHEST, preferred_element_type=F32)

    def keep(src, sec):
        block = full[src, sec]
        if rows < LANES:
            block = jnp.concatenate([block, jnp.zeros((LANES - rows, section), F32)], axis=0)
        high, low = halves(block.T)
        slot = jnp.where(src == 0, 2, jnp.where(src == zs - 1, zs - 1, src - 1))
        at = pl.ds(pl.multiple_of(slot * LANES, LANES), LANES)
        tall_high[section_at(sec), at] = high
        tall_low[section_at(sec), at] = low

    for src in range(zs):
        post_high[src * LANES + rows : (src + 1) * LANES, :] = jnp.zeros((LANES - rows, classes), BF16)
        post_low[src * LANES + rows : (src + 1) * LANES, :] = jnp.zeros((LANES - rows, classes), BF16)

    groups = group_ref[...]
    sigma_row = jnp.ones(groups.shape, F32)
    for g in range(noise_ref.shape[1]):
        sigma_row = jnp.where(groups == g, noise_ref[0:1, g : g + 1], sigma_row)
    if rows < LANES:
        sigma_row = jnp.concatenate([sigma_row, jnp.ones((1, LANES - rows), F32)], axis=1)
    sigmas[0] = jnp.broadcast_to(sigma_row, (8, LANES))

    load_quarters[1][0].wait()
    repack(load_quarters[1][1])

    for load, at in load_quarters[2:]:
        load.wait()
        repack(at)
    load_refs.wait()
    norm = lax.fori_loop(0, band, put_rows, jnp.zeros((1, classes), F32))
    start = jnp.broadcast_to(-0.5 * norm, (rows, classes))
    for src in range(zs):
        scores[src] = start

    units = 6 * (zs - 1)

    def chunk(n):
        return z + inward * (n // 6 + 1), lax.rem(n + 2, 6)

    def end_unit(n):
        @pl.when(n < units)
        def _():
            src, sec = chunk(n)
            go_in(src, sec).wait_recv()
            go_x(src, sec).start()
            end_send(n + AHEAD)

        @pl.when((n >= LAG) & (n < units + LAG))
        def _():
            src, sec = chunk(n - LAG)
            go_x(src, sec).wait_recv()
            go_cx(src, sec).start()

    def pass_x(src, sec):
        go_in(src, sec).wait_recv()
        go_x(src, sec).start()

    def take_x(src, sec):
        go_x(src, sec).wait_recv()
        go_cx(src, sec).start()

    def middle_unit(n):
        @pl.when(n < 6)
        def _():
            pass_x(across_z, n + 2)
            go_in(near, n + 2).wait_recv()

        middle_send(n + AHEAD)

        @pl.when((n >= 6) & (n < 10))
        def _():
            pass_x(far, n - 4)
            go_out(far, n - 4).start()

        @pl.when((n >= 12) & (n < 14))
        def _():
            pass_x(far, n - 6)

        @pl.when((n >= 6) & (n < 12))
        def _():
            go_pair(near, n - 4).wait_recv()
            go_cx(near, n - 4).start()

        @pl.when((n >= LAG) & (n < LAG + 6))
        def _():
            take_x(across_z, n - LAG + 2)

        @pl.when((n >= LAG + 6) & (n < LAG + 10))
        def _():
            take_x(far, n - LAG - 4)

        @pl.when((n >= LAG + 12) & (n < LAG + 14))
        def _():
            take_x(far, n - LAG - 6)

    def take_item(item):
        other = jnp.maximum(item - 6, 0)
        end_src, end_sec = chunk(other)
        middle_src = jnp.where(other < 6, across_z, jnp.where(other < 12, near, far))
        own = item < 6
        src = jnp.where(own, z, jnp.where(is_end, end_src, middle_src))
        sec = jnp.where(own, 2 * middle + item, jnp.where(is_end, end_sec, 2 + lax.rem(other, 6)))

        @pl.when(item >= 6)
        def _():
            go_cx(src, sec).wait_recv()

        scores[src] = scores[src] + multiply(src, sec)
        keep(src, sec)

    def arrived(slot):
        partial_in(z, 0, slot).wait_recv()
        return parts[slot]

    def end_sums(n):
        for when, src, number in ((8, z, 0), (11, z + inward, 1), (15, z + 2 * inward, 2)):
            @pl.when(n == when)
            def _():
                partial_in(src, number, number).start()

    def middle_sums(n):
        @pl.when(n == 12)
        def _():
            scores[near] = scores[near] + arrived(0)
            partial_in(near, 0, 4).start()

        @pl.when(n == 15)
        def _():
            scores[z] = scores[z] + arrived(1)
            partial_in(z, 1, 3).start()

        @pl.when(n == 17)
        def _():
            scores[far] = scores[far] + arrived(4)
            partial_out(far, 2).start()

    def unit(n, _):
        @pl.when(is_end)
        def _():
            end_unit(n)

        @pl.when(is_middle)
        def _():
            middle_unit(n)

        @pl.when(n < 4)
        def _():
            lax.fori_loop(n * band // 4, (n + 1) * band // 4, put_columns, 0)

        @pl.when(n >= 4)
        def _():
            end_first = jnp.where(n < 10, 2 * (n - 4), n + 2)
            end_count = jnp.where(n < 10, 2, 1)
            middle_first = jnp.where(n < 15, 2 * (n - 4), 22)
            middle_count = jnp.where((n < 15) | (n == 17), 2, 0)
            first = jnp.where(is_end, end_first, middle_first)
            count = jnp.where(is_end, end_count, middle_count)

            def run(item, _):
                take_item(item)
                return 0

            lax.fori_loop(first, first + count, run, 0)

        @pl.when(n == 8)
        def _():
            give_sigma.start()

        @pl.when(is_end)
        def _():
            end_sums(n)

        @pl.when(is_middle)
        def _():
            middle_sums(n)

        return 0

    lax.fori_loop(0, units + LAG + 1, unit, 0)

    owned = zs - 1 - z

    @pl.when(is_end)
    def _():
        scores[owned] = scores[owned] + arrived(0)

    @pl.when(is_middle)
    def _():
        scores[owned] = scores[owned] + arrived(2) + arrived(3)

    def upright(row):
        return jnp.broadcast_to(row, (LANES, row.shape[1])).T[:rows, 0:1]

    give_sigma.wait_recv()
    total_score = scores[owned] / upright(sigmas[1, 0:1, :])
    top = jnp.max(total_score, axis=1, keepdims=True)
    shifted = jnp.exp(total_score - top)
    posts[owned] = shifted
    half_rows = rows // 2

    def give(src, half, where, ssem):
        part = posts.at[src, half * half_rows : (half + 1) * half_rows, :]
        return send(part, part, ssem, p_recv.at[src, half], {"img": where})

    def give_in(half):
        return give(owned, half, z + inward, p_send.at[0, half])

    def give_far(half):
        return give(owned, half, jnp.where(is_end, owned, z + 2 * inward), p_send.at[1, half])

    def give_out(half):
        return give(owned, half, z - inward, p_send.at[2, half])

    def pass_on(half):
        return give(far, half, z + inward, p_send.at[3, half])

    def give_factor(d):
        where = {"img": lax.rem(z + d, zs)}
        return send(facs.at[owned], facs.at[owned], f_send.at[d], f_recv.at[owned], where)

    def take_posts(src):
        @pl.when(is_end | (src != far))
        def _():
            for half in range(2):
                give(src, half, 0, p_send.at[0, half]).wait_recv()

        send(facs.at[src], facs.at[src], f_send.at[0], f_recv.at[src], {"img": owned}).wait_recv()

    for half in range(2):
        give_in(half).start()

    @pl.when(is_middle)
    def _():
        for half in range(2):
            give_out(half).start()

    total = jnp.sum(shifted, axis=1, keepdims=True)
    place = lax.broadcasted_iota(jnp.int32, (rows, LANES), 1)
    pair = jnp.where(place < LANES // 2, top, total)
    if rows < LANES:
        pair = jnp.concatenate([pair, jnp.ones((LANES - rows, LANES), F32)], axis=0)
    pair = pair.T
    tops, totals = pair[0:8], pair[LANES // 2 : LANES // 2 + 8]
    stats[3, 0:8, :] = tops
    stats[3, 8:16, :] = totals
    shares = [send(stats.at[3], stats.at[m], t_send.at[m], t_recv.at[m], where) for m, where in enumerate(others)]
    for share in shares:
        share.start()
    for half in range(2):
        give_far(half).start()
    for share in shares:
        share.wait()
    best = tops
    for m in range(3):
        best = jnp.maximum(best, stats[m, 0:8, :])
    summed = totals * jnp.exp(tops - best)
    for m in range(3):
        summed = summed + stats[m, 8:16, :] * jnp.exp(stats[m, 0:8, :] - best)
    evidence = best + jnp.log(summed)
    facs[owned, 0:8, :] = jnp.exp(tops - evidence)
    facs[owned, 8:16, :] = evidence
    for d in (3, 2, 1):
        give_factor(d).start()

    def settle_posts(src, slot, weight_sum):
        @pl.when(z != zs - 1 - src)
        def _():
            take_posts(src)

        factor = upright(facs[src, 0:1, :])
        post = posts[src] * factor
        high, low = halves(post)
        post_high[slot * LANES : slot * LANES + rows, :] = high
        post_low[slot * LANES : slot * LANES + rows, :] = low
        return weight_sum + jnp.sum(post, axis=0, keepdims=True)

    def weigh(half, add):
        part = slice(half * 2 * LANES, (half + 1) * 2 * LANES)

        def step(n, _):
            at = pl.ds(pl.multiple_of(2 * n * section, 2 * section), 2 * section)
            ah, al, bh, bl = tall_high[at, part], tall_low[at, part], post_high[part, :], post_low[part, :]
            one = lambda p, q: jnp.dot(p, q, preferred_element_type=F32)
            result = one(ah, bh) + (one(ah, bl) + one(al, bh))
            for k in range(2 * section // side):
                at = pl.ds(pl.multiple_of(2 * n * 8 * apart + k * apart, 8), side)
                for h in range(classes // LANES):
                    value = result[k * side : (k + 1) * side, lane(h)]
                    num[h, at, :] = num[h, at, :] + value if add else value
            return 0

        lax.fori_loop(0, 3, step, 0)


    @pl.when(is_middle)
    def _():
        for half in range(2):
            give(far, half, 0, p_send.at[0, half]).wait_recv()
            pass_on(half).start()

    weight_sum = settle_posts(1, 0, jnp.zeros((1, classes), F32))
    weight_sum = settle_posts(2, 1, weight_sum)
    weigh(0, False)
    weight_sum = settle_posts(0, 2, weight_sum)
    weight_sum = settle_posts(3, 3, weight_sum)
    weigh(1, True)
    weights_ref[...] = weight_sum * weight_scale
    evidence_ref[...] = facs[z, 8:9, :rows]
    scale = 1.0 / (weight_sum + 1.0)

    def finish(i, _):
        fields = []
        for h in range(classes // LANES):
            pull_row = lambda b, j: jnp.concatenate([num[h, row_at(b, j, which, apart), :] for which in range(4)], axis=0)
            pull_column = lambda b, j: jnp.concatenate(
                [num[h, column_at(b, j, g, half, apart), :] for g in range(4) for half in range(2)], axis=0
            )
            up = pull_row(z, i)
            down = pull_row(zs - 1 - z, band - 1 - i)
            across = pull_column(z, i)
            back = pull_column(zs - 1 - z, band - 1 - i)
            k = lane(h)
            fields.append(jnp.where(is_row[:, k], up, jnp.where(is_row_up[:, k], down, jnp.where(is_col[:, k], across, back))))
        field = jnp.concatenate(fields, axis=1)
        means_ref[line(i), :] = jnp.where(flipped, reverse_rows(field), field) * scale
        return 0

    step = band // 4

    def store(k):
        at = pl.ds(pl.multiple_of(k * step * side, step * side), step * side)
        return pltpu.make_async_copy(means_ref.at[at, :], means_out.at[at, :], out_sem.at[k])

    for k in range(4):
        lax.fori_loop(k * step, (k + 1) * step, finish, 0, unroll=4)
        store(k).start()

    @pl.when(is_end)
    def _():
        def settle(n, _):
            src, sec = chunk(n)
            go_x(src, sec).wait_send()
            go_cx(src, sec).wait_send()

            @pl.when(n < 6)
            def _():
                go_in(z, n + 2).wait_send()
                go_pair(z, n + 2).wait_send()

            return 0

        lax.fori_loop(0, units, settle, 0)

    @pl.when(is_middle)
    def _():
        def settle(n, _):
            go_in(z, n + 2).wait_send()
            go_out(z, n).wait_send()
            go_in(near, n + 2).wait_send()
            go_cx(near, n + 2).wait_send()
            for src in (across_z, far):
                @pl.when(n < 4)
                def _():
                    go_out(src, n + 2).wait_send()

                go_x(src, n + 2).wait_send()
                go_cx(src, n + 2).wait_send()

            return 0

        lax.fori_loop(0, 6, settle, 0)

    go_far(0).wait_send()
    go_far(1).wait_send()
    for k in range(4):
        store(k).wait()
    give_sigma.wait_send()
    for number in range(3):
        partial_in(z, number, 0).wait_send()
    for d in (1, 2, 3):
        give_factor(d).wait_send()
    for half in range(2):
        give_in(half).wait_send()
        give_far(half).wait_send()

        @pl.when(is_middle)
        def _():
            give_out(half).wait_send()
            pass_on(half).wait_send()


def deliver(means, weights, evidence, means_out, weights_out, evidence_out, held, held_weights, held_evidence, in_sem, out_sem):
    parts = in_sem.shape[0] - 2
    step = means.shape[0] // parts
    pieces = [(means.at[pl.ds(k * step, step)], held.at[pl.ds(k * step, step)], means_out.at[pl.ds(k * step, step)]) for k in range(parts)]
    pieces += [(weights, held_weights, weights_out), (evidence, held_evidence, evidence_out)]
    loads = [pltpu.make_async_copy(a, b, in_sem.at[k]) for k, (a, b, _) in enumerate(pieces)]
    stores = [pltpu.make_async_copy(b, d, out_sem.at[k]) for k, (_, b, d) in enumerate(pieces)]
    for load in loads:
        load.start()
    for load, store in zip(loads, stores):
        load.wait()
        store.start()
    for store in stores:
        store.wait()


def turned_images_body(zs, images, references, rotations, image_group, noise_var):
    rows = images.shape[0]
    pixels, classes = references.shape
    class_total = classes * lax.axis_size("ref") * lax.axis_size("rep")
    image_total = rows * zs
    dma = pltpu.SemaphoreType.DMA
    vmem = pl.BlockSpec(memory_space=pltpu.VMEM)
    many = dma((zs, 8))
    section = PIXELS // 8
    means, weight_sum, evidence = pl.pallas_call(
        functools.partial(kernel, zs, class_total / image_total),
        name="class_step",
        out_shape=(
            jax.ShapeDtypeStruct((pixels, classes), F32),
            jax.ShapeDtypeStruct((1, classes), F32),
            jax.ShapeDtypeStruct((1, rows), F32),
        ),
        in_specs=[pl.BlockSpec(memory_space=pl.ANY), pl.BlockSpec(memory_space=pl.ANY), vmem, vmem, vmem],
        out_specs=(pl.BlockSpec(memory_space=pl.ANY), vmem, vmem),
        scratch_shapes=[
            pltpu.VMEM((pixels, classes), F32),
            pltpu.VMEM((rows, PIXELS), F32),
            pltpu.VMEM((zs, 8, rows, section), F32),
            pltpu.VMEM((classes // LANES, 6 * 8 * (IMAGE_SIDE + GAP), LANES), F32),
            pltpu.VMEM((zs, rows, classes), F32),
            pltpu.VMEM((5, rows, classes), F32),
            pltpu.VMEM((4, 16, LANES), F32),
            pltpu.VMEM((zs, rows, classes), F32),
            pltpu.VMEM((classes // LANES, 6 * 8 * (IMAGE_SIDE + GAP), LANES), F32),
            pltpu.VMEM((pixels, classes), F32),
            pltpu.VMEM((zs, 16, LANES), F32),
            pltpu.VMEM((2, 8, LANES), F32),
            pltpu.VMEM((6 * section, zs * LANES), BF16),
            pltpu.VMEM((6 * section, zs * LANES), BF16),
            pltpu.VMEM((zs * LANES, classes), BF16),
            pltpu.VMEM((zs * LANES, classes), BF16),
            dma((4,)), dma, many, dma((8,)), many, many, many, many, dma((2,)), dma((8,)), many, many, dma, dma,
            dma((3,)), dma((5,)), dma((3,)), dma((3,)), dma((4, 2)), dma((zs, 2)), dma((zs,)), dma((zs,)), dma((4,)),
        ],
        compiler_params=pltpu.CompilerParams(
            collective_id=0, has_side_effects=True, vmem_limit_bytes=VMEM_BYTES
        ),
    )(images, references, rotations[None, :], image_group[None, :], noise_var[None, :])
    anywhere = pl.BlockSpec(memory_space=pl.ANY)
    results = (means, weight_sum, evidence)
    means, weight_sum, evidence = pl.pallas_call(
        deliver,
        name="deliver",
        out_shape=tuple(jax.ShapeDtypeStruct(a.shape, a.dtype) for a in results),
        in_specs=[anywhere] * 3,
        out_specs=(anywhere,) * 3,
        scratch_shapes=[pltpu.VMEM(a.shape, a.dtype) for a in results] + [dma((6,)), dma((6,))],
    )(*results)
    return (means, weight_sum[0], evidence[0])


def solution(mesh):
    sizes = dict(mesh.shape)
    placed = (
        P(("groups", "img"), None),
        P("img", ("groups", "ref", "rep")),
        P(("groups", "ref", "rep")),
        P(("groups", "img")),
        P(),
    )

    def choose(images, references, rotations, image_group, noise_var):
        zs = sizes["img"]
        rows = images.shape[0]
        fits = (
            sizes["ref"] == 2
            and sizes["rep"] == 2
            and rows % 32 == 0
            and rows <= LANES
            and zs == 4
            and IMAGE_SIDE == 64
            and references.shape[1] % LANES == 0
            and zs * rows * PIXELS * 4 <= 12 * 1024 * 1024
        )
        if fits:
            return turned_images_body(zs, images, references, rotations, image_group, noise_var)
        return body(images, references, rotations, image_group, noise_var)

    return jax.shard_map(
        choose,
        mesh=mesh,
        in_specs=placed,
        out_specs=(
            P("img", ("groups", "ref", "rep")),
            P(("groups", "ref", "rep")),
            P(("groups", "img")),
        ),
        check_vma=False,
    )
```

```python
import functools

import jax
import jax.numpy as jnp
from jax import lax
from jax.experimental import pallas as pl
from jax.experimental.pallas import tpu as pltpu
from jax.sharding import PartitionSpec as P

IMAGE_SIDE = 64
PIXELS = 4096
MESH = pl.DeviceIdType.MESH
F32 = jnp.float32
BF16 = jnp.bfloat16
LANES = 128
LAG = 3
GAP = 8
AHEAD = 3
VMEM_BYTES = 62 * 1024 * 1024


def joined(part, axis, combine):
    gathered = jax.tree.map(lambda a: lax.all_gather(a, axis), part)

    def take(source):
        return jax.tree.map(lambda a: lax.dynamic_index_in_dim(a, source, 0, False), gathered)

    return lax.fori_loop(
        1, lax.axis_size(axis), lambda source, state: combine(state, take(source)), take(0)
    )


def turn_forward(field, which):
    quarter = which % 4
    base = field if which < 4 else jnp.swapaxes(field, 0, 1)
    return jnp.rot90(base, quarter, axes=(0, 1))


def turn_inverse(field, which):
    quarter = which % 4
    base = jnp.rot90(field, -quarter, axes=(0, 1))
    return base if which < 4 else jnp.swapaxes(base, 0, 1)


def select_turn(field, rotations, turner):
    result = jnp.zeros_like(field)
    for which in range(8):
        result = jnp.where(rotations[None, None, :] == which, turner(field, which), result)
    return result


def combine_stats(first, second):
    top = jnp.maximum(first[0], second[0])
    total = first[1] * jnp.exp(first[0] - top) + second[1] * jnp.exp(second[0] - top)
    return (top, total)


def body(images, references, rotations, image_group, noise_var):
    gathered = lax.all_gather(references, "img", axis=0, tiled=True)
    rotated = select_turn(
        gathered.reshape(IMAGE_SIDE, IMAGE_SIDE, -1), rotations, turn_inverse
    ).reshape(PIXELS, -1)
    norms = jnp.sum(gathered * gathered, axis=0)
    group_hot = image_group[:, None] == jnp.arange(noise_var.shape[0])[None, :]
    sigma = jnp.sum(jnp.where(group_hot, noise_var[None, :], 0.0), axis=1)
    scores = (
        jnp.dot(
            images, rotated, precision=lax.Precision.HIGHEST, preferred_element_type=jnp.float32
        )
        - 0.5 * norms[None, :]
    ) / sigma[:, None]
    local_top = jnp.max(scores, axis=1)
    local_total = jnp.sum(jnp.exp(scores - local_top[:, None]), axis=1)
    top, total = joined((local_top, local_total), ("ref", "rep"), combine_stats)
    log_evidence = top + jnp.log(total)
    posterior = jnp.exp(scores - log_evidence[:, None])
    weight_sum = lax.psum(jnp.sum(posterior, axis=0), "img")
    numer_image = lax.dot_general(
        images,
        posterior,
        (((0,), (0,)), ((), ())),
        precision=lax.Precision.HIGHEST,
        preferred_element_type=jnp.float32,
    )
    numerator = select_turn(
        numer_image.reshape(IMAGE_SIDE, IMAGE_SIDE, -1), rotations, turn_forward
    ).reshape(PIXELS, -1)
    owned = lax.psum_scatter(numerator, "img", scatter_dimension=0, tiled=True)
    class_means = owned / (weight_sum + 1.0)[None, :]
    class_total = weight_sum.shape[0] * lax.axis_size("ref") * lax.axis_size("rep")
    image_total = images.shape[0] * lax.axis_size("img")
    class_weights = weight_sum * (class_total / image_total)
    return (class_means, class_weights, log_evidence)


def halves(x):
    high = x.astype(BF16)
    return high, (x - high.astype(F32)).astype(BF16)


def reverse_rows(x):
    place = lax.broadcasted_iota(jnp.int32, (8, x.shape[1]), 0)
    odd = place % 2 == 1
    second = (place // 2) % 2 == 1
    pieces = []
    for g in reversed(range(x.shape[0] // 8)):
        p = x[8 * g : 8 * g + 8]
        p = jnp.where(odd, pltpu.roll(p, 1, 0), pltpu.roll(p, 7, 0))
        p = jnp.where(second, pltpu.roll(p, 2, 0), pltpu.roll(p, 6, 0))
        pieces.append(pltpu.roll(p, 4, 0))
    return jnp.concatenate(pieces, axis=0)


def kernel(
    zs, weight_scale,
    images_ref, source_ref, rot_ref, group_ref, noise_ref,
    means_out, weights_ref, evidence_ref,
    means_ref, raw, full, wide, scores, parts, stats, posts, num, refs_ref, facs, sigmas, tall_high, tall_low, post_high, post_low,
    load_sem, refs_sem, z_recv, pair_recv, x_recv, cx_recv,
    in_send, out_send, far_send, pair_send, x_send, cx_send, g_send, g_recv,
    s_send, s_recv, t_send, t_recv, p_send, p_recv, f_send, f_recv, out_sem,
):
    z = lax.axis_index("img")
    x = lax.axis_index("ref")
    c = lax.axis_index("rep")
    rows = images_ref.shape[0]
    classes = refs_ref.shape[1]
    quarter = rows // 4
    side = IMAGE_SIDE
    band = side // zs
    apart = side + GAP
    section = PIXELS // 8
    others = [{"ref": 1 - x}, {"rep": 1 - c}, {"ref": 1 - x, "rep": 1 - c}]
    upper = jnp.where(z >= 2, 1, 0)
    middle = jnp.where((z == 1) | (z == 2), 1, 0)
    inward = 1 - 2 * upper

    def quarter_at(xi, ci):
        return pl.ds(pl.multiple_of((ci * 2 + xi) * quarter, 8), quarter)

    load_quarters = []
    for q, (xi, ci) in enumerate([(x, c), (1 - x, c), (x, 1 - c), (1 - x, 1 - c)]):
        at = quarter_at(xi, ci)
        load_quarters.append((pltpu.make_async_copy(images_ref.at[at, :], raw.at[at, :], load_sem.at[q]), at))
    for load, _ in load_quarters:
        load.start()
    load_refs = pltpu.make_async_copy(source_ref, refs_ref, refs_sem)
    load_refs.start()
    barrier = pltpu.get_barrier_semaphore()
    pl.semaphore_signal(barrier, inc=1, device_id={"img": z + inward}, device_id_type=MESH)

    @pl.when(middle == 1)
    def _():
        pl.semaphore_signal(barrier, inc=1, device_id={"img": z - inward}, device_id_type=MESH)

    for where in others:
        pl.semaphore_signal(barrier, inc=1, device_id=where, device_id_type=MESH)

    def repack(at):
        place = lax.broadcasted_iota(jnp.int32, (quarter, LANES), 1) // band
        low = place % 4
        for g in range(4):
            for v in range(4):
                start = 2 * g * section + v * LANES
                first = raw[at, start : start + LANES]
                start = (2 * g + 1) * section + v * LANES
                second = raw[at, start : start + LANES]
                first_a, first_b = pltpu.roll(first, band, 1), pltpu.roll(first, 5 * band, 1)
                second_a, second_b = pltpu.roll(second, 3 * band, 1), pltpu.roll(second, 7 * band, 1)
                outer = jnp.where(low < 2, jnp.where(low == 0, first_b, first_a), jnp.where(low == 2, second_b, second_a))
                inner = jnp.where(low < 2, second_b, first_a)
                which = (0 if g in (0, 3) else 4) + g // 2
                full[z, which, at, v * LANES : (v + 1) * LANES] = outer
                full[z, which + 2, at, v * LANES : (v + 1) * LANES] = inner

    load_quarters[0][0].wait()
    repack(load_quarters[0][1])
    pl.semaphore_wait(barrier, 4 + middle)

    def send(src, dst, ssem, rsem, where):
        return pltpu.make_async_remote_copy(
            src_ref=src, dst_ref=dst, send_sem=ssem, recv_sem=rsem,
            device_id=where, device_id_type=MESH,
        )

    def piece(src, sec):
        return full.at[src, sec, quarter_at(x, c), :]

    def go_in(src, sec):
        return send(piece(src, sec), piece(src, sec), in_send.at[src, sec], z_recv.at[src, sec], {"img": z + inward})

    def go_out(src, sec):
        return send(piece(src, sec), piece(src, sec), out_send.at[src, sec], z_recv.at[src, sec], {"img": z - inward})

    def go_far(sec):
        target = jnp.where(upper == 1, 0, zs - 1)
        return send(piece(z, sec), piece(z, sec), far_send.at[sec], z_recv.at[z, sec], {"img": target})

    def go_x(src, sec):
        return send(piece(src, sec), piece(src, sec), x_send.at[src, sec], x_recv.at[src, sec], {"ref": 1 - x})

    def go_cx(src, sec):
        pair = full.at[src, sec, pl.ds(pl.multiple_of(c * 2 * quarter, 8), 2 * quarter), :]
        return send(pair, pair, cx_send.at[src, sec], cx_recv.at[src, sec], {"rep": 1 - c})

    def go_pair(src, sec):
        rest = full.at[src, sec, quarter_at(1 - x, c), :]
        return send(rest, rest, pair_send.at[sec], pair_recv.at[sec], {"img": z + inward})

    def partial_in(src, number, slot):
        return send(scores.at[src], parts.at[slot], s_send.at[number], s_recv.at[slot], {"img": z + inward})

    def partial_out(src, number):
        return send(scores.at[src], parts.at[0], s_send.at[number], s_recv.at[0], {"img": z - inward})

    give_sigma = send(sigmas.at[0], sigmas.at[1], g_send, g_recv, {"img": zs - 1 - z})

    is_end = middle == 0
    is_middle = middle == 1
    near, across_z, far = z - inward, z + inward, z + 2 * inward

    def end_send(i):
        @pl.when(i < 6)
        def _():
            go_in(z, i + 2).start()

        @pl.when((i >= 6) & (i < 12))
        def _():
            go_pair(z, i - 4).start()

        @pl.when((i >= 12) & (i < 14))
        def _():
            go_far(i - 12).start()

    def middle_send(i):
        @pl.when(i < 6)
        def _():
            go_in(z, i + 2).start()
            go_out(z, lax.rem(i + 2, 6)).start()

        @pl.when((i >= 6) & (i < 10))
        def _():
            go_in(near, i - 4).start()
            go_out(across_z, i - 4).start()

        @pl.when((i >= 10) & (i < 12))
        def _():
            go_far(i - 10).start()

        @pl.when((i >= 12) & (i < 14))
        def _():
            go_in(near, i - 6).start()

    @pl.when(is_end)
    def _():
        for i in range(AHEAD):
            end_send(i)

    @pl.when(is_middle)
    def _():
        for i in range(AHEAD):
            middle_send(i)

    rot = rot_ref[...]
    is_row = (rot == 0) | (rot == 7)
    is_row_up = (rot == 5) | (rot == 2)
    is_col = (rot == 4) | (rot == 3)
    is_col_up = (rot == 1) | (rot == 6)
    flipped = (rot == 7) | (rot == 2) | (rot == 3) | (rot == 6)

    def lane(h):
        return slice(h * LANES, (h + 1) * LANES)

    def line(i):
        return pl.ds(pl.multiple_of(i * side, side), side)

    def row_at(b, i, which, stride):
        block = 8 * stride
        base = jnp.where(b >= 2, block, 0) + stride * lax.rem(i, 8)
        if which in (0, 3):
            place = base + 2 * block * middle + 2 * band * (i // 8) + (band if which == 0 else 0)
        else:
            place = base + 2 * block * (middle + 1) + 2 * band * (1 - i // 8) + (band if which == 2 else 0)
        return pl.ds(pl.multiple_of(place, 8), band)

    def column_at(b, i, g, half, stride):
        block = 8 * stride
        base = (0 if g in (0, 3) else 4 * block) + (block if g >= 2 else 0)
        swapped = half + middle * (1 - 2 * half)
        place = base + 2 * band * swapped + band * (1 - lax.rem(b, 2)) + i
        return pl.ds(place, 8, stride=stride)

    def turned(i):
        field = refs_ref[line(i), :]
        return jnp.where(flipped, reverse_rows(field), field)

    def put_rows(i, norm):
        raw_field = refs_ref[line(i), :]
        field = turned(i)
        up = jnp.where(is_row, field, 0.0)
        down = jnp.where(is_row_up, field, 0.0)
        for h in range(classes // LANES):
            for which in range(4):
                part = slice(which * band, (which + 1) * band)
                wide[h, row_at(z, i, which, apart), :] = up[part, lane(h)]
                wide[h, row_at(zs - 1 - z, band - 1 - i, which, apart), :] = down[part, lane(h)]
        return norm + jnp.sum(raw_field * raw_field, axis=0, keepdims=True)

    def put_columns(i, _):
        field = turned(i)
        across = jnp.where(is_col, field, 0.0)
        back = jnp.where(is_col_up, field, 0.0)

        def put(added):
            for h in range(classes // LANES):
                for g in range(4):
                    for half in range(2):
                        part = slice(g * band + half * 8, g * band + half * 8 + 8)
                        for at, value in (
                            (column_at(z, i, g, half, apart), across[part, lane(h)]),
                            (column_at(zs - 1 - z, band - 1 - i, g, half, apart), back[part, lane(h)]),
                        ):
                            if g in added:
                                wide[h, at, :] = wide[h, at, :] + value
                            else:
                                wide[h, at, :] = value

        @pl.when(is_end)
        def _():
            put((0, 3))

        @pl.when(is_middle)
        def _():
            put((1, 2))

        return 0

    def section_at(sec):
        return pl.ds(pl.multiple_of((sec - 2 * middle) * section, section), section)

    def multiply(src, sec):
        first = (sec - 2 * middle) * 8 * apart
        pieces = [pl.ds(pl.multiple_of(first + k * apart, 8), side) for k in range(section // side)]
        weight = jnp.concatenate(
            [jnp.concatenate([wide[h, at, :] for at in pieces], axis=0) for h in range(classes // LANES)], axis=1
        )
        return jnp.dot(full[src, sec], weight, precision=lax.Precision.HIGHEST, preferred_element_type=F32)

    def keep(src, sec):
        block = full[src, sec]
        if rows < LANES:
            block = jnp.concatenate([block, jnp.zeros((LANES - rows, section), F32)], axis=0)
        high, low = halves(block.T)
        slot = jnp.where(src == 0, 2, jnp.where(src == zs - 1, zs - 1, src - 1))
        at = pl.ds(pl.multiple_of(slot * LANES, LANES), LANES)
        tall_high[section_at(sec), at] = high
        tall_low[section_at(sec), at] = low

    for src in range(zs):
        post_high[src * LANES + rows : (src + 1) * LANES, :] = jnp.zeros((LANES - rows, classes), BF16)
        post_low[src * LANES + rows : (src + 1) * LANES, :] = jnp.zeros((LANES - rows, classes), BF16)

    groups = group_ref[...]
    sigma_row = jnp.ones(groups.shape, F32)
    for g in range(noise_ref.shape[1]):
        sigma_row = jnp.where(groups == g, noise_ref[0:1, g : g + 1], sigma_row)
    if rows < LANES:
        sigma_row = jnp.concatenate([sigma_row, jnp.ones((1, LANES - rows), F32)], axis=1)
    sigmas[0] = jnp.broadcast_to(sigma_row, (8, LANES))

    load_quarters[1][0].wait()
    repack(load_quarters[1][1])

    for load, at in load_quarters[2:]:
        load.wait()
        repack(at)
    load_refs.wait()
    norm = lax.fori_loop(0, band, put_rows, jnp.zeros((1, classes), F32))
    start = jnp.broadcast_to(-0.5 * norm, (rows, classes))
    for src in range(zs):
        scores[src] = start

    units = 6 * (zs - 1)

    def chunk(n):
        return z + inward * (n // 6 + 1), lax.rem(n + 2, 6)

    def end_unit(n):
        @pl.when(n < units)
        def _():
            src, sec = chunk(n)
            go_in(src, sec).wait_recv()
            go_x(src, sec).start()
            end_send(n + AHEAD)

        @pl.when((n >= LAG) & (n < units + LAG))
        def _():
            src, sec = chunk(n - LAG)
            go_x(src, sec).wait_recv()
            go_cx(src, sec).start()

    def pass_x(src, sec):
        go_in(src, sec).wait_recv()
        go_x(src, sec).start()

    def take_x(src, sec):
        go_x(src, sec).wait_recv()
        go_cx(src, sec).start()

    def middle_unit(n):
        @pl.when(n < 6)
        def _():
            pass_x(across_z, n + 2)
            go_in(near, n + 2).wait_recv()

        middle_send(n + AHEAD)

        @pl.when((n >= 6) & (n < 10))
        def _():
            pass_x(far, n - 4)
            go_out(far, n - 4).start()

        @pl.when((n >= 12) & (n < 14))
        def _():
            pass_x(far, n - 6)

        @pl.when((n >= 6) & (n < 12))
        def _():
            go_pair(near, n - 4).wait_recv()
            go_cx(near, n - 4).start()

        @pl.when((n >= LAG) & (n < LAG + 6))
        def _():
            take_x(across_z, n - LAG + 2)

        @pl.when((n >= LAG + 6) & (n < LAG + 10))
        def _():
            take_x(far, n - LAG - 4)

        @pl.when((n >= LAG + 12) & (n < LAG + 14))
        def _():
            take_x(far, n - LAG - 6)

    def take_item(item):
        other = jnp.maximum(item - 6, 0)
        end_src, end_sec = chunk(other)
        middle_src = jnp.where(other < 6, across_z, jnp.where(other < 12, near, far))
        own = item < 6
        src = jnp.where(own, z, jnp.where(is_end, end_src, middle_src))
        sec = jnp.where(own, 2 * middle + item, jnp.where(is_end, end_sec, 2 + lax.rem(other, 6)))

        @pl.when(item >= 6)
        def _():
            go_cx(src, sec).wait_recv()

        scores[src] = scores[src] + multiply(src, sec)
        keep(src, sec)

    def arrived(slot):
        partial_in(z, 0, slot).wait_recv()
        return parts[slot]

    def end_sums(n):
        for when, src, number in ((7, z, 0), (11, z + inward, 1), (15, z + 2 * inward, 2)):
            @pl.when(n == when)
            def _():
                partial_in(src, number, number).start()

    def middle_sums(n):
        @pl.when(n == 12)
        def _():
            scores[near] = scores[near] + arrived(0)
            partial_in(near, 0, 4).start()

        @pl.when(n == 15)
        def _():
            scores[z] = scores[z] + arrived(1)
            partial_in(z, 1, 3).start()

        @pl.when(n == 17)
        def _():
            scores[far] = scores[far] + arrived(4)
            partial_out(far, 2).start()

    def unit(n, _):
        @pl.when(is_end)
        def _():
            end_unit(n)

        @pl.when(is_middle)
        def _():
            middle_unit(n)

        @pl.when(n < 4)
        def _():
            lax.fori_loop(n * band // 4, (n + 1) * band // 4, put_columns, 0)

        @pl.when(n >= 4)
        def _():
            end_first = jnp.where(n < 10, 2 * (n - 4), n + 2)
            end_count = jnp.where(n < 10, 2, 1)
            middle_first = jnp.where(n < 15, 2 * (n - 4), 22)
            middle_count = jnp.where((n < 15) | (n == 17), 2, 0)
            first = jnp.where(is_end, end_first, middle_first)
            count = jnp.where(is_end, end_count, middle_count)

            def run(item, _):
                take_item(item)
                return 0

            lax.fori_loop(first, first + count, run, 0)

        @pl.when(n == 8)
        def _():
            give_sigma.start()

        @pl.when(is_end)
        def _():
            end_sums(n)

        @pl.when(is_middle)
        def _():
            middle_sums(n)

        return 0

    lax.fori_loop(0, units + LAG + 1, unit, 0)

    owned = zs - 1 - z

    @pl.when(is_end)
    def _():
        scores[owned] = scores[owned] + arrived(0)

    @pl.when(is_middle)
    def _():
        scores[owned] = scores[owned] + arrived(2) + arrived(3)

    def upright(row):
        return jnp.broadcast_to(row, (LANES, row.shape[1])).T[:rows, 0:1]

    give_sigma.wait_recv()
    total_score = scores[owned] / upright(sigmas[1, 0:1, :])
    top = jnp.max(total_score, axis=1, keepdims=True)
    shifted = jnp.exp(total_score - top)
    posts[owned] = shifted
    half_rows = rows // 2

    def give(src, half, where, ssem):
        part = posts.at[src, half * half_rows : (half + 1) * half_rows, :]
        return send(part, part, ssem, p_recv.at[src, half], {"img": where})

    def give_in(half):
        return give(owned, half, z + inward, p_send.at[0, half])

    def give_far(half):
        return give(owned, half, jnp.where(is_end, owned, z + 2 * inward), p_send.at[1, half])

    def give_out(half):
        return give(owned, half, z - inward, p_send.at[2, half])

    def pass_on(half):
        return give(far, half, z + inward, p_send.at[3, half])

    def give_factor(d):
        where = {"img": lax.rem(z + d, zs)}
        return send(facs.at[owned], facs.at[owned], f_send.at[d], f_recv.at[owned], where)

    def take_posts(src):
        @pl.when(is_end | (src != far))
        def _():
            for half in range(2):
                give(src, half, 0, p_send.at[0, half]).wait_recv()

        send(facs.at[src], facs.at[src], f_send.at[0], f_recv.at[src], {"img": owned}).wait_recv()

    for half in range(2):
        give_in(half).start()

    @pl.when(is_middle)
    def _():
        for half in range(2):
            give_out(half).start()

    total = jnp.sum(shifted, axis=1, keepdims=True)
    place = lax.broadcasted_iota(jnp.int32, (rows, LANES), 1)
    pair = jnp.where(place < LANES // 2, top, total)
    if rows < LANES:
        pair = jnp.concatenate([pair, jnp.ones((LANES - rows, LANES), F32)], axis=0)
    pair = pair.T
    tops, totals = pair[0:8], pair[LANES // 2 : LANES // 2 + 8]
    stats[3, 0:8, :] = tops
    stats[3, 8:16, :] = totals
    shares = [send(stats.at[3], stats.at[m], t_send.at[m], t_recv.at[m], where) for m, where in enumerate(others)]
    for share in shares:
        share.start()
    for half in range(2):
        give_far(half).start()
    for share in shares:
        share.wait()
    best = tops
    for m in range(3):
        best = jnp.maximum(best, stats[m, 0:8, :])
    summed = totals * jnp.exp(tops - best)
    for m in range(3):
        summed = summed + stats[m, 8:16, :] * jnp.exp(stats[m, 0:8, :] - best)
    evidence = best + jnp.log(summed)
    facs[owned, 0:8, :] = jnp.exp(tops - evidence)
    facs[owned, 8:16, :] = evidence
    for d in (3, 2, 1):
        give_factor(d).start()

    def settle_posts(src, slot, weight_sum):
        @pl.when(z != zs - 1 - src)
        def _():
            take_posts(src)

        factor = upright(facs[src, 0:1, :])
        post = posts[src] * factor
        high, low = halves(post)
        post_high[slot * LANES : slot * LANES + rows, :] = high
        post_low[slot * LANES : slot * LANES + rows, :] = low
        return weight_sum + jnp.sum(post, axis=0, keepdims=True)

    def weigh(half, add):
        part = slice(half * 2 * LANES, (half + 1) * 2 * LANES)

        def step(n, _):
            at = pl.ds(pl.multiple_of(2 * n * section, 2 * section), 2 * section)
            ah, al, bh, bl = tall_high[at, part], tall_low[at, part], post_high[part, :], post_low[part, :]
            one = lambda p, q: jnp.dot(p, q, preferred_element_type=F32)
            result = one(ah, bh) + (one(ah, bl) + one(al, bh))
            for k in range(2 * section // side):
                at = pl.ds(pl.multiple_of(2 * n * 8 * apart + k * apart, 8), side)
                for h in range(classes // LANES):
                    value = result[k * side : (k + 1) * side, lane(h)]
                    num[h, at, :] = num[h, at, :] + value if add else value
            return 0

        lax.fori_loop(0, 3, step, 0)


    @pl.when(is_middle)
    def _():
        for half in range(2):
            give(far, half, 0, p_send.at[0, half]).wait_recv()
            pass_on(half).start()

    weight_sum = settle_posts(1, 0, jnp.zeros((1, classes), F32))
    weight_sum = settle_posts(2, 1, weight_sum)
    weigh(0, False)
    weight_sum = settle_posts(0, 2, weight_sum)
    weight_sum = settle_posts(3, 3, weight_sum)
    weigh(1, True)
    weights_ref[...] = weight_sum * weight_scale
    evidence_ref[...] = facs[z, 8:9, :rows]
    scale = 1.0 / (weight_sum + 1.0)

    def finish(i, _):
        fields = []
        for h in range(classes // LANES):
            pull_row = lambda b, j: jnp.concatenate([num[h, row_at(b, j, which, apart), :] for which in range(4)], axis=0)
            pull_column = lambda b, j: jnp.concatenate(
                [num[h, column_at(b, j, g, half, apart), :] for g in range(4) for half in range(2)], axis=0
            )
            up = pull_row(z, i)
            down = pull_row(zs - 1 - z, band - 1 - i)
            across = pull_column(z, i)
            back = pull_column(zs - 1 - z, band - 1 - i)
            k = lane(h)
            fields.append(jnp.where(is_row[:, k], up, jnp.where(is_row_up[:, k], down, jnp.where(is_col[:, k], across, back))))
        field = jnp.concatenate(fields, axis=1)
        means_ref[line(i), :] = jnp.where(flipped, reverse_rows(field), field) * scale
        return 0

    step = band // 4

    def store(k):
        at = pl.ds(pl.multiple_of(k * step * side, step * side), step * side)
        return pltpu.make_async_copy(means_ref.at[at, :], means_out.at[at, :], out_sem.at[k])

    for k in range(4):
        lax.fori_loop(k * step, (k + 1) * step, finish, 0, unroll=4)
        store(k).start()

    @pl.when(is_end)
    def _():
        def settle(n, _):
            src, sec = chunk(n)
            go_x(src, sec).wait_send()
            go_cx(src, sec).wait_send()

            @pl.when(n < 6)
            def _():
                go_in(z, n + 2).wait_send()
                go_pair(z, n + 2).wait_send()

            return 0

        lax.fori_loop(0, units, settle, 0)

    @pl.when(is_middle)
    def _():
        def settle(n, _):
            go_in(z, n + 2).wait_send()
            go_out(z, n).wait_send()
            go_in(near, n + 2).wait_send()
            go_cx(near, n + 2).wait_send()
            for src in (across_z, far):
                @pl.when(n < 4)
                def _():
                    go_out(src, n + 2).wait_send()

                go_x(src, n + 2).wait_send()
                go_cx(src, n + 2).wait_send()

            return 0

        lax.fori_loop(0, 6, settle, 0)

    go_far(0).wait_send()
    go_far(1).wait_send()
    for k in range(4):
        store(k).wait()
    give_sigma.wait_send()
    for number in range(3):
        partial_in(z, number, 0).wait_send()
    for d in (1, 2, 3):
        give_factor(d).wait_send()
    for half in range(2):
        give_in(half).wait_send()
        give_far(half).wait_send()

        @pl.when(is_middle)
        def _():
            give_out(half).wait_send()
            pass_on(half).wait_send()


def deliver(means, weights, evidence, means_out, weights_out, evidence_out, held, held_weights, held_evidence, in_sem, out_sem):
    parts = in_sem.shape[0] - 2
    step = means.shape[0] // parts
    pieces = [(means.at[pl.ds(k * step, step)], held.at[pl.ds(k * step, step)], means_out.at[pl.ds(k * step, step)]) for k in range(parts)]
    pieces += [(weights, held_weights, weights_out), (evidence, held_evidence, evidence_out)]
    loads = [pltpu.make_async_copy(a, b, in_sem.at[k]) for k, (a, b, _) in enumerate(pieces)]
    stores = [pltpu.make_async_copy(b, d, out_sem.at[k]) for k, (_, b, d) in enumerate(pieces)]
    for load in loads:
        load.start()
    for load, store in zip(loads, stores):
        load.wait()
        store.start()
    for store in stores:
        store.wait()


def turned_images_body(zs, images, references, rotations, image_group, noise_var):
    rows = images.shape[0]
    pixels, classes = references.shape
    class_total = classes * lax.axis_size("ref") * lax.axis_size("rep")
    image_total = rows * zs
    dma = pltpu.SemaphoreType.DMA
    vmem = pl.BlockSpec(memory_space=pltpu.VMEM)
    many = dma((zs, 8))
    section = PIXELS // 8
    means, weight_sum, evidence = pl.pallas_call(
        functools.partial(kernel, zs, class_total / image_total),
        name="class_step",
        out_shape=(
            jax.ShapeDtypeStruct((pixels, classes), F32),
            jax.ShapeDtypeStruct((1, classes), F32),
            jax.ShapeDtypeStruct((1, rows), F32),
        ),
        in_specs=[pl.BlockSpec(memory_space=pl.ANY), pl.BlockSpec(memory_space=pl.ANY), vmem, vmem, vmem],
        out_specs=(pl.BlockSpec(memory_space=pl.ANY), vmem, vmem),
        scratch_shapes=[
            pltpu.VMEM((pixels, classes), F32),
            pltpu.VMEM((rows, PIXELS), F32),
            pltpu.VMEM((zs, 8, rows, section), F32),
            pltpu.VMEM((classes // LANES, 6 * 8 * (IMAGE_SIDE + GAP), LANES), F32),
            pltpu.VMEM((zs, rows, classes), F32),
            pltpu.VMEM((5, rows, classes), F32),
            pltpu.VMEM((4, 16, LANES), F32),
            pltpu.VMEM((zs, rows, classes), F32),
            pltpu.VMEM((classes // LANES, 6 * 8 * (IMAGE_SIDE + GAP), LANES), F32),
            pltpu.VMEM((pixels, classes), F32),
            pltpu.VMEM((zs, 16, LANES), F32),
            pltpu.VMEM((2, 8, LANES), F32),
            pltpu.VMEM((6 * section, zs * LANES), BF16),
            pltpu.VMEM((6 * section, zs * LANES), BF16),
            pltpu.VMEM((zs * LANES, classes), BF16),
            pltpu.VMEM((zs * LANES, classes), BF16),
            dma((4,)), dma, many, dma((8,)), many, many, many, many, dma((2,)), dma((8,)), many, many, dma, dma,
            dma((3,)), dma((5,)), dma((3,)), dma((3,)), dma((4, 2)), dma((zs, 2)), dma((zs,)), dma((zs,)), dma((4,)),
        ],
        compiler_params=pltpu.CompilerParams(
            collective_id=0, has_side_effects=True, vmem_limit_bytes=VMEM_BYTES
        ),
    )(images, references, rotations[None, :], image_group[None, :], noise_var[None, :])
    anywhere = pl.BlockSpec(memory_space=pl.ANY)
    results = (means, weight_sum, evidence)
    means, weight_sum, evidence = pl.pallas_call(
        deliver,
        name="deliver",
        out_shape=tuple(jax.ShapeDtypeStruct(a.shape, a.dtype) for a in results),
        in_specs=[anywhere] * 3,
        out_specs=(anywhere,) * 3,
        scratch_shapes=[pltpu.VMEM(a.shape, a.dtype) for a in results] + [dma((6,)), dma((6,))],
    )(*results)
    return (means, weight_sum[0], evidence[0])


def solution(mesh):
    sizes = dict(mesh.shape)
    placed = (
        P(("groups", "img"), None),
        P("img", ("groups", "ref", "rep")),
        P(("groups", "ref", "rep")),
        P(("groups", "img")),
        P(),
    )

    def choose(images, references, rotations, image_group, noise_var):
        zs = sizes["img"]
        rows = images.shape[0]
        fits = (
            sizes["ref"] == 2
            and sizes["rep"] == 2
            and rows % 32 == 0
            and rows <= LANES
            and zs == 4
            and IMAGE_SIDE == 64
            and references.shape[1] % LANES == 0
            and zs * rows * PIXELS * 4 <= 12 * 1024 * 1024
        )
        if fits:
            return turned_images_body(zs, images, references, rotations, image_group, noise_var)
        return body(images, references, rotations, image_group, noise_var)

    return jax.shard_map(
        choose,
        mesh=mesh,
        in_specs=placed,
        out_specs=(
            P("img", ("groups", "ref", "rep")),
            P(("groups", "ref", "rep")),
            P(("groups", "img")),
        ),
        check_vma=False,
    )
```
